32 devices in a mesh: leaf: 8 (over z, core), grp: 4 (over y, x).
Axes of the slice: x: 2, y: 2, z: 4, core: 2. Of those that a mesh axis runs over, the one named last changes fastest.
Arguments:
- leaf_rhs: bfloat16 [32768, 512], P(('leaf', 'grp')), may hold values from -6 to 6
- leaf_inv: bfloat16 [32768, 4096], P(('leaf', 'grp')), may hold values from -1 to 1, as said below
- ordering: int32 [8, 4096], P('leaf'), may hold values from 0 to 4095, each once within a row
- leaf_dinv: bfloat16 [32768], P(('leaf', 'grp')), may hold values from -2 to 2, as said below
- leaf_link: bfloat16 [32768, 32], P(('leaf', 'grp')), may hold values from -0.0625 to 0.0625
- sep_rhs: bfloat16 [3, 512, 128], P(None, 'grp', 'leaf'), may hold values from -6 to 6
- sep_factor: bfloat16 [128, 416], P(('leaf', 'grp')), may hold values from -1 to 1, as said below
- sep_dinv: bfloat16 [3, 128], P(None, 'leaf'), may hold values from -2 to 2, as said below
Outputs:
- leaf_solution: float32 [32768, 512], P(('leaf', 'grp'))
- sep_solution: float32 [3, 512, 128], P(None, 'grp', 'leaf')
The draws below stay inside these ranges and needn't reach their ends.
Inputs may be any that keep to these rules, and one draw needn't show every extreme that they name: Within each leaf's 4096 rows, leaf_inv is unit lower triangular. `sep_factor`: each W block is unit lower triangular within its separator. `leaf_dinv`: every entry has magnitude 0.5 or more. `sep_dinv`: every entry has magnitude 0.5 or more.
All inputs are finite; a program needn't handle non-finite values.
Results may differ from the reference program's by a relative error of at most 0.013.
Values may be sent and summed in bfloat16 or wider, within the bound.
No kernel may reach another device: no remote copies, remote signals or barrier semaphores. Data moves between devices by JAX's collectives and lax.ppermute only.
A program may use at most 128 MiB of HBM per device.

```python
import math
import jax
import jax.numpy as jnp
from jax import lax

RHS = 512
LEAF = 4096
LEVELS = 3
SEP_LEAF = 16
FIRST = 32
NSEP = 128
LEAF_ALL = 32768
N_LEAF = 8
N_GRP = 4


def noise_block(key, row_count, width):
    return jnp.clip(jax.random.normal(key, (row_count, width), jnp.float32), -4.0, 4.0)


def lower_unit(key, row_index, width, spread_scale):
    column_index = jnp.arange(width)
    noise = noise_block(key, row_index.shape[0], width)
    below = (column_index[None, :] < row_index[:, None]).astype(jnp.float32)
    diagonal = (column_index[None, :] == row_index[:, None]).astype(jnp.float32)
    return diagonal + below * noise * (spread_scale / math.sqrt(width))


def signed_scales(key, shape):
    magnitude_key, sign_key = jax.random.split(key)
    magnitude = jnp.exp(jax.random.uniform(magnitude_key, shape, jnp.float32, math.log(0.5), math.log(2.0)))
    signs = 2 * jax.random.randint(sign_key, shape, 0, 2) - 1
    return magnitude * signs.astype(jnp.float32)


def draw_leaf_inv(key, part):
    row_index = jnp.arange(N_LEAF * LEAF) % LEAF
    return lower_unit(key, row_index, LEAF, 1.0).astype(jnp.bfloat16)


def draw_leaf_dinv(key, part):
    return signed_scales(key, (N_LEAF * LEAF,)).astype(jnp.bfloat16)


def draw_sep_dinv(key, part):
    levels = N_LEAF.bit_length() - 1
    return signed_scales(key, (levels, NSEP)).astype(jnp.bfloat16)


def draw_sep_factor(key, part):
    levels = N_LEAF.bit_length() - 1
    row_index = jnp.arange(NSEP)
    blocks = []
    for tree_level in range(1, levels + 1):
        size_here = SEP_LEAF * 2 ** tree_level
        blocks.append(lower_unit(jax.random.fold_in(key, tree_level), row_index % size_here, size_here, 0.8))
        if tree_level >= 2:
            coupling = noise_block(jax.random.fold_in(key, 100 + tree_level), NSEP, size_here)
            blocks.append(coupling * (0.6 / math.sqrt(size_here)))
    return jnp.concatenate(blocks, axis=1).astype(jnp.bfloat16)


def block_levels(rng, dims, shards, least, largest):
    gain, own = 1.0, jax.random.fold_in(rng, 6)
    for position, blocks in shards:
        steps = jnp.exp(jax.random.uniform(jax.random.fold_in(own, position), (blocks,), jnp.float32, least / len(shards), largest / len(shards)))
        gain = gain * jnp.repeat(steps, dims[position] // blocks).reshape([-1 if axis == position else 1 for axis in range(len(dims))])
    return gain


def scatter_about(own_key, shape, scale, limit, cuts=(), kind=jnp.bfloat16):
    values = jax.random.normal(own_key, shape, jnp.float32) * scale
    if len(cuts) > 0:
        values = block_levels(own_key, shape, cuts, -0.22, 0.18) * values
    return jnp.clip(values, min=-limit, max=limit).astype(kind)


def setup_inputs(seed: int = 0) -> dict:
    streams_of = jax.random.split(jax.random.key(seed), 9)
    return {
        "leaf_rhs": scatter_about(streams_of[0], (LEAF_ALL, RHS), 1.0, 6.0, ((0, 32),)),
        "leaf_inv": draw_leaf_inv(jax.random.fold_in(streams_of[8], 71), 0),
        "ordering": jax.vmap(lambda own: jax.random.permutation(own, LEAF))(jax.random.split(streams_of[2], N_LEAF)).reshape((N_LEAF, LEAF)).astype(jnp.int32),
        "leaf_dinv": draw_leaf_dinv(jax.random.fold_in(streams_of[8], 71), 0),
        "leaf_link": scatter_about(streams_of[4], (LEAF_ALL, FIRST), (2 * LEAF) ** -0.5, 0.0625, ((0, 32),)),
        "sep_rhs": scatter_about(streams_of[5], (LEVELS, RHS, NSEP), 1.0, 6.0, ((1, 4), (2, 8))),
        "sep_factor": draw_sep_factor(jax.random.fold_in(streams_of[8], 71), 0),
        "sep_dinv": draw_sep_dinv(jax.random.fold_in(streams_of[8], 71), 0),
    }


def level_offset(sep_block, tree_level):
    if tree_level >= 2:
        return sep_block * (2 ** (tree_level + 1) - 6)
    return 0


def reference(leaf_rhs, leaf_inv, ordering, leaf_dinv, leaf_link, sep_rhs, sep_factor, sep_dinv):
    levels = N_LEAF.bit_length() - 1
    group_size = LEAF // N_GRP
    first_width = 2 * SEP_LEAF
    leaf_z = []
    inverses = []
    for leaf_index in range(N_LEAF):
        row_base = leaf_index * LEAF
        loads = leaf_rhs[row_base:row_base + LEAF]
        order_row = ordering[leaf_index]
        inverses.append(jnp.argsort(order_row).astype(jnp.int32))
        factor_rows = leaf_inv[row_base:row_base + LEAF]
        solved = jnp.dot(factor_rows, loads[order_row], preferred_element_type=jnp.float32)
        scales = leaf_dinv[row_base:row_base + LEAF].astype(jnp.float32)
        leaf_z.append((scales[:, None] * solved).astype(jnp.bfloat16))
    residual = {}
    for sep_index in range(N_LEAF // 2):
        crossing = jnp.zeros((first_width, RHS), jnp.float32)
        for leaf_index in (2 * sep_index, 2 * sep_index + 1):
            row_base = leaf_index * LEAF
            crossing = crossing + jnp.dot(leaf_link[row_base:row_base + LEAF].T, leaf_rhs[row_base:row_base + LEAF], preferred_element_type=jnp.float32)
        loads = sep_rhs[0, :, sep_index * first_width:(sep_index + 1) * first_width].T.astype(jnp.float32)
        residual[(1, sep_index)] = (loads - crossing).astype(jnp.bfloat16)
    z_sep = {}
    for tree_level in range(1, levels + 1):
        size_here = SEP_LEAF * 2 ** tree_level
        offset = level_offset(SEP_LEAF, tree_level)
        for sep_index in range(N_LEAF >> tree_level):
            row_base = sep_index * size_here
            block_rows = sep_factor[row_base:row_base + size_here]
            if tree_level >= 2:
                children = jnp.concatenate([residual[(tree_level - 1, 2 * sep_index)], residual[(tree_level - 1, 2 * sep_index + 1)]], axis=0)
                link_block = block_rows[:, offset + size_here:offset + 2 * size_here]
                loads = sep_rhs[tree_level - 1, :, row_base:row_base + size_here].T.astype(jnp.float32)
                residual[(tree_level, sep_index)] = (loads - jnp.dot(link_block, children, preferred_element_type=jnp.float32)).astype(jnp.bfloat16)
            solved = jnp.dot(block_rows[:, offset:offset + size_here], residual[(tree_level, sep_index)], preferred_element_type=jnp.float32)
            scales = sep_dinv[tree_level - 1, row_base:row_base + size_here].astype(jnp.float32)
            z_sep[(tree_level, sep_index)] = (scales[:, None] * solved).astype(jnp.bfloat16)
    answer = {}
    for tree_level in range(levels, 0, -1):
        size_here = SEP_LEAF * 2 ** tree_level
        offset = level_offset(SEP_LEAF, tree_level)
        for sep_index in range(N_LEAF >> tree_level):
            row_base = sep_index * size_here
            diagonal = sep_factor[row_base:row_base + size_here, offset:offset + size_here]
            sep_value = jnp.dot(diagonal.T, z_sep[(tree_level, sep_index)], preferred_element_type=jnp.float32)
            if tree_level < levels:
                parent_index = sep_index // 2
                parent_base = parent_index * 2 * size_here
                parent_offset = level_offset(SEP_LEAF, tree_level + 1)
                link_block = sep_factor[parent_base:parent_base + 2 * size_here, parent_offset + 2 * size_here:parent_offset + 4 * size_here]
                pushed = jnp.dot(link_block.T, answer[(tree_level + 1, parent_index)].astype(jnp.bfloat16), preferred_element_type=jnp.float32)
                part_base = (sep_index % 2) * size_here
                sep_value = sep_value - pushed[part_base:part_base + size_here]
            answer[(tree_level, sep_index)] = sep_value
    level_blocks = []
    for tree_level in range(1, levels + 1):
        pieces = []
        for sep_index in range(N_LEAF >> tree_level):
            pieces.append(answer[(tree_level, sep_index)])
        level_blocks.append(jnp.concatenate(pieces, axis=0).T)
    sep_solution = jnp.stack(level_blocks, axis=0)
    leaf_parts = []
    for leaf_index in range(N_LEAF):
        row_base = leaf_index * LEAF
        factor_rows = leaf_inv[row_base:row_base + LEAF]
        summed = jnp.zeros((LEAF, RHS), jnp.float32)
        for group_index in range(N_GRP):
            start_row = group_index * group_size
            group_term = jnp.dot(factor_rows[start_row:start_row + group_size].T, leaf_z[leaf_index][start_row:start_row + group_size], preferred_element_type=jnp.float32)
            rounded = lax.optimization_barrier(group_term.astype(jnp.bfloat16))
            summed = summed + rounded.astype(jnp.float32)
        reordered = summed[inverses[leaf_index]]
        first_solution = answer[(1, leaf_index // 2)].astype(jnp.bfloat16)
        leaf_parts.append(reordered - jnp.dot(leaf_link[row_base:row_base + LEAF], first_solution, preferred_element_type=jnp.float32))
    return jnp.concatenate(leaf_parts, axis=0), sep_solution
```

```python
import functools

import jax
import jax.numpy as jnp
from jax import lax
from jax.experimental import pallas as pl
from jax.experimental.pallas import tpu as pltpu
from jax.sharding import PartitionSpec as P

F32 = jnp.float32
BF16 = jnp.bfloat16


def exchange(block, axis, mask):
    count = lax.axis_size(axis)
    return lax.ppermute(block, axis, [(low, low ^ mask) for low in range(count)])


def level_offset(sep_block, tree_level):
    if tree_level >= 2:
        return sep_block * (2 ** (tree_level + 1) - 6)
    return 0


def dot_tn(lhs, rhs):
    return lax.dot_general(lhs, rhs, (((0,), (0,)), ((), ())), preferred_element_type=F32)


def dot_nn(lhs, rhs):
    return jnp.dot(lhs, rhs, preferred_element_type=F32)


def vmem():
    return pl.BlockSpec(memory_space=pltpu.VMEM)


def smem():
    return pl.BlockSpec(memory_space=pltpu.SMEM)


def from_partner(block, axis, distance):
    count = lax.axis_size(axis)
    route = []
    for low in range(count):
        high = low | 1 << distance
        if high != low and high < count:
            route += [(low, high), (high, low)]
    return lax.ppermute(block, axis, route)


def partner(values, level_bit):
    return from_partner(values.astype(jnp.bfloat16), "leaf", level_bit).astype(values.dtype)


def leaf_bit(level_bit):
    return jnp.right_shift(lax.axis_index("leaf"), level_bit) % 2


def spread(values, first_bit, last_bit):
    for level_bit in range(first_bit, last_bit):
        partner_rows = partner(values.astype(jnp.float32), level_bit).astype(jnp.bfloat16)
        low_first = jnp.concatenate([values, partner_rows], axis=-1)
        high_first = jnp.concatenate([partner_rows, values], axis=-1)
        values = jnp.where(leaf_bit(level_bit) == 0, low_first, high_first)
    return values


def halve_sum(values, bit_list):
    for level_bit in bit_list:
        half_width = values.shape[-1] // 2
        low_half = values[..., :half_width]
        high_half = values[..., half_width:]
        is_upper = leaf_bit(level_bit) == 1
        keep_half = jnp.where(is_upper, high_half, low_half)
        send_half = jnp.where(is_upper, low_half, high_half)
        values = keep_half + partner(send_half, level_bit)
    return values


def group_rows(values):
    return lax.all_gather(values, "grp", axis=0, tiled=True)


def level_width(sep_block, tree_level):
    if tree_level >= 2:
        return 2 * sep_block * 2**tree_level
    return sep_block * 2**tree_level


def local_general(leaf_rhs, leaf_inv, ordering, leaf_dinv, leaf_link, sep_rhs, sep_factor, sep_dinv):
    levels = sep_rhs.shape[0]
    sep_block = sep_rhs.shape[2]
    inverse = jnp.argsort(ordering[0])
    picked = jnp.take(leaf_inv, inverse, axis=1)
    leaf_y = jnp.dot(
        picked,
        lax.all_gather(leaf_rhs, "grp", axis=0, tiled=True),
        preferred_element_type=jnp.float32,
    )
    partial_sum = jnp.einsum("rk,rc->kc", leaf_rhs, leaf_link, preferred_element_type=jnp.float32)
    crossing = lax.psum_scatter(
        partial_sum.astype(jnp.bfloat16), "grp", scatter_dimension=0, tiled=True
    ).astype(jnp.float32)
    leaf_z = (leaf_dinv.astype(jnp.float32)[:, None] * leaf_y).astype(jnp.bfloat16)
    crossing = halve_sum(crossing, [0])
    sep_r = (sep_rhs[0].astype(jnp.float32) - crossing).astype(jnp.bfloat16)
    gathered = group_rows(sep_factor)

    def level_rows(tree_level):
        offset = level_offset(sep_block, tree_level)
        return lax.slice_in_dim(
            gathered, offset, offset + level_width(sep_block, tree_level), axis=1
        )

    z_blocks = []
    full_prev = sep_r
    for tree_level in range(1, levels + 1):
        rows_here = level_rows(tree_level)
        size_here = sep_block * 2**tree_level
        if tree_level >= 2:
            children = spread(full_prev, tree_level - 1, tree_level)
            link_rows = rows_here[:, size_here:]
            coupled = jnp.einsum(
                "kc,qc->kq", children, link_rows, preferred_element_type=jnp.float32
            )
            sep_r = (sep_rhs[tree_level - 1].astype(jnp.float32) - coupled).astype(jnp.bfloat16)
        full_prev = spread(sep_r, 0, tree_level)
        sep_y = jnp.einsum(
            "kc,qc->kq", full_prev, rows_here[:, :size_here], preferred_element_type=jnp.float32
        )
        z_blocks.append(
            (sep_dinv[tree_level - 1].astype(jnp.float32)[None, :] * sep_y).astype(jnp.bfloat16)
        )
    solution = [None] * levels
    upper_rows = level_rows(levels)
    size_top = sep_block * 2**levels
    partial_value = jnp.einsum(
        "kq,qc->kc",
        z_blocks[levels - 1],
        upper_rows[:, :size_top],
        preferred_element_type=jnp.float32,
    )
    current = halve_sum(partial_value, list(range(levels - 1, -1, -1)))
    solution[levels - 1] = current
    for tree_level in range(levels - 1, 0, -1):
        size_here = sep_block * 2**tree_level
        link_rows = upper_rows[:, 2 * size_here :]
        rows_here = level_rows(tree_level)
        pushed = -jnp.einsum(
            "kq,qc->kc", current.astype(jnp.bfloat16), link_rows, preferred_element_type=jnp.float32
        )
        pushed = halve_sum(pushed, [tree_level])
        pushed = pushed + jnp.einsum(
            "kq,qc->kc",
            z_blocks[tree_level - 1],
            rows_here[:, :size_here],
            preferred_element_type=jnp.float32,
        )
        current = halve_sum(pushed, list(range(tree_level - 1, -1, -1)))
        solution[tree_level - 1] = current
        upper_rows = rows_here
    first_full = spread(current.astype(jnp.bfloat16), 0, 1)
    first_all = group_rows(first_full)
    picked = jnp.take(leaf_inv, inverse, axis=1)
    leaf_x = lax.psum_scatter(
        jnp.einsum("rm,rk->mk", picked, leaf_z, preferred_element_type=jnp.float32).astype(
            jnp.bfloat16
        ),
        "grp",
        scatter_dimension=0,
        tiled=True,
    ).astype(jnp.float32)
    leaf_x = leaf_x - jnp.einsum(
        "rc,kc->rk", leaf_link, first_all, preferred_element_type=jnp.float32
    )
    return (leaf_x, jnp.stack(solution, axis=0))


def pack_body(rhs_ref, link_ref, sep_ref, fac_ref, out_ref):
    levels, width, sep_block = sep_ref.shape
    first = link_ref.shape[1]
    rows, cols = fac_ref.shape
    out_ref[0:first, :] = dot_tn(link_ref[...], rhs_ref[...]).astype(BF16)
    out_ref[first:, :] = jnp.zeros((out_ref.shape[0] - first, out_ref.shape[1]), BF16)
    for level in range(levels):
        out_ref[first : first + sep_block, level * width : (level + 1) * width] = (
            sep_ref[level].astype(F32).T.astype(BF16)
        )
    out_ref[first + sep_block : first + sep_block + rows, 0:cols] = fac_ref[...]


def leaf_body(place_ref, own_ref, x_ref, y_ref, d_ref, dinv_ref, out_ref, *, first, levels, rows, cols):
    sep_block = dinv_ref.shape[1]
    width = out_ref.shape[1]
    me = place_ref[1]
    parts = (own_ref, x_ref, y_ref, d_ref)
    total = parts[0][0:first, :].astype(F32)
    for part in parts[1:]:
        total = total + part[0:first, :].astype(F32)
    out_ref[0:first, :] = total.astype(BF16)
    part_width = width // len(parts)
    for index, part in enumerate(parts):
        lanes = pl.ds(pl.multiple_of((me ^ index) * part_width, part_width), part_width)
        for level in range(levels):
            out_ref[first + level * sep_block : first + (level + 1) * sep_block, lanes] = part[
                first : first + sep_block, level * part_width : (level + 1) * part_width
            ]
    row_owner = lax.broadcasted_iota(jnp.int32, (sep_block, width), 0) // rows
    lane = lax.broadcasted_iota(jnp.int32, (sep_block, width), 1)
    factor = jnp.zeros((sep_block, width), F32)
    for index, part in enumerate(parts):
        block = part[first + sep_block : first + 2 * sep_block, :].astype(F32)[0:rows, :]
        tiled = jnp.concatenate([block] * (sep_block // rows), axis=0)
        factor = factor + jnp.where(row_owner == (me ^ index), tiled, 0.0)
    pivots = dinv_ref[...].astype(F32).T
    for level in range(levels):
        column = jnp.broadcast_to(pivots[:, level : level + 1], (sep_block, width))
        factor = jnp.where(lane == cols + level, column, factor)
    out_ref[first + levels * sep_block :, :] = factor.astype(BF16)


def pair_body(place_ref, own_ref, other_ref, out_ref, *, first, levels, sep_block):
    is_odd = place_ref[0] % 2 == 1
    own = own_ref[...].astype(F32)
    other = other_ref[...].astype(F32)
    even = jnp.where(is_odd, other, own)
    odd = jnp.where(is_odd, own, other)
    crossing = even[0:first] + odd[0:first]
    for level in range(levels + 1):
        base = first + level * sep_block
        both = jnp.concatenate([even[base : base + sep_block], odd[base : base + sep_block]], axis=0)
        if level == 0:
            both = both - crossing
        out_ref[level * first : (level + 1) * first, :] = both.astype(BF16)


def tree_body(
    place_ref, *refs, count, first, levels, sep_block, cols, slice_width
):
    pairs = refs[:count]
    first_ref, sol_ref, stage_ref, val_ref = refs[count:]
    leaf, me = place_ref[0], place_ref[1]
    pair = leaf // 2
    nsep = count * first
    width = pairs[0].shape[1]
    for index, ref in enumerate(pairs):
        place = pl.ds(pl.multiple_of((pair ^ index) * first, first), first)
        for level in range(levels + 1):
            stage_ref[level, place, :] = ref[level * first : (level + 1) * first, :]
    factor = stage_ref[levels]
    column = lax.broadcasted_iota(jnp.int32, (width, nsep), 0)
    target = lax.broadcasted_iota(jnp.int32, (width, nsep), 1)
    row = lax.broadcasted_iota(jnp.int32, (nsep, nsep), 0)
    lane = lax.broadcasted_iota(jnp.int32, (nsep, nsep), 1)

    def block_diagonal(offset, size):
        choose = jnp.where(column == offset + target % size, 1.0, 0.0).astype(BF16)
        spread = dot_nn(factor, choose)
        return jnp.where(row // size == lane // size, spread, 0.0).astype(BF16)

    weights, couplings, z_blocks = [], [], []
    residual = stage_ref[0]
    for level in range(1, levels + 1):
        size = sep_block * 2**level
        offset = level_offset(sep_block, level)
        weight = block_diagonal(offset, size)
        coupling = None
        if level >= 2:
            coupling = block_diagonal(offset + size, size)
            residual = (stage_ref[level - 1].astype(F32) - dot_nn(coupling, residual)).astype(BF16)
        choose = jnp.where(column == cols + level - 1, 1.0, 0.0).astype(BF16)
        scale = dot_nn(factor, choose)
        scale = jnp.concatenate([scale] * (width // nsep), axis=1)
        z_blocks.append((scale * dot_nn(weight, residual)).astype(BF16))
        weights.append(weight)
        couplings.append(coupling)
    current = None
    for level in range(levels, 0, -1):
        value = dot_tn(weights[level - 1], z_blocks[level - 1])
        if level < levels:
            value = value - dot_tn(couplings[level], current.astype(BF16))
        current = value
        val_ref[...] = value
        lanes = pl.ds(pl.multiple_of(me * slice_width, slice_width), slice_width)
        mine = val_ref[pl.ds(pl.multiple_of(leaf * sep_block, sep_block), sep_block), lanes]
        sol_ref[level - 1] = mine.T
    first_ref[...] = val_ref[pl.ds(pl.multiple_of(pair * first, first), first), :].astype(BF16)


def tree(place, rhs, link, sep_rhs, sep_factor, sep_dinv):
    levels, slice_width, sep_block = sep_rhs.shape
    first = link.shape[1]
    width = rhs.shape[1]
    rows, cols = sep_factor.shape
    aux = pl.pallas_call(
        pack_body,
        out_shape=jax.ShapeDtypeStruct((first + 2 * sep_block, width), BF16),
        in_specs=[vmem()] * 4,
        out_specs=vmem(),
        name="pack",
    )(rhs, link, sep_rhs, sep_factor)
    aux_x, aux_y, aux_d = (exchange(aux, "grp", mask) for mask in (1, 2, 3))
    leaf_block = pl.pallas_call(
        functools.partial(leaf_body, first=first, levels=levels, rows=rows, cols=cols),
        out_shape=jax.ShapeDtypeStruct((first + (levels + 1) * sep_block, width), BF16),
        in_specs=[smem()] + [vmem()] * 5,
        out_specs=vmem(),
        name="leafblock",
    )(place, aux, aux_x, aux_y, aux_d, sep_dinv)
    partner = exchange(leaf_block, "leaf", 1)
    pair_block = pl.pallas_call(
        functools.partial(pair_body, first=first, levels=levels, sep_block=sep_block),
        out_shape=jax.ShapeDtypeStruct(((levels + 1) * first, width), BF16),
        in_specs=[smem(), vmem(), vmem()],
        out_specs=vmem(),
        name="pairblock",
    )(place, leaf_block, partner)
    count = lax.axis_size("leaf") // 2
    pairs = [pair_block] + [exchange(pair_block, "leaf", 2 * mask) for mask in range(1, count)]
    nsep = count * first
    return pl.pallas_call(
        functools.partial(
            tree_body,
            count=count,
            first=first,
            levels=levels,
            sep_block=sep_block,
            cols=cols,
            slice_width=slice_width,
        ),
        out_shape=(
            jax.ShapeDtypeStruct((first, width), BF16),
            jax.ShapeDtypeStruct((levels, slice_width, sep_block), F32),
        ),
        in_specs=[smem()] + [vmem()] * count,
        out_specs=(vmem(), vmem()),
        scratch_shapes=[pltpu.VMEM((levels + 1, nsep, width), BF16), pltpu.VMEM((nsep, width), F32)],
        name="tree",
    )(place, *pairs)


def local_pairs(leaf_rhs, leaf_inv, ordering, leaf_dinv, leaf_link, sep_rhs, sep_factor, sep_dinv):
    rows = leaf_rhs.shape[0]
    half = rows // 2
    leaf = lax.axis_index("leaf").astype(jnp.int32)
    me = lax.axis_index("grp").astype(jnp.int32)
    place = jnp.stack([leaf, me])

    rhs_x = exchange(leaf_rhs, "grp", 1)
    rhs_y = exchange(leaf_rhs, "grp", 2)
    first_all, solution_here = tree(place, leaf_rhs, leaf_link, sep_rhs, sep_factor, sep_dinv)
    far_low = exchange(rhs_x[:half], "grp", 2)
    far_high = exchange(rhs_y[half:], "grp", 1)

    inverse = jnp.argsort(ordering[0])
    inverse = inverse.reshape(-1, rows)
    inverse = jnp.concatenate([inverse[me ^ index] for index in range(inverse.shape[0])])
    picked = jnp.take(leaf_inv, inverse, axis=1).T
    blocks = [picked[index * rows : (index + 1) * rows] for index in range(lax.axis_size("grp"))]

    leaf_y = dot_tn(blocks[0], leaf_rhs)
    leaf_y = leaf_y + dot_tn(blocks[1], rhs_x)
    leaf_y = leaf_y + dot_tn(blocks[2], rhs_y)
    leaf_y = leaf_y + dot_tn(blocks[3][:half], far_low)
    leaf_y = leaf_y + dot_tn(blocks[3][half:], far_high)
    leaf_z = (leaf_dinv.astype(F32)[:, None] * leaf_y).astype(BF16)

    far = dot_nn(blocks[3], leaf_z).astype(BF16)
    relay_low = exchange(far[:half], "grp", 1)
    relay_high = exchange(far[half:], "grp", 2)
    near_x = dot_nn(blocks[1], leaf_z)
    x_low = exchange(near_x[:half].astype(BF16), "grp", 1)
    near_y = dot_nn(blocks[2], leaf_z)
    y_high = exchange(near_y[half:].astype(BF16), "grp", 2)
    x_high = exchange((near_x[half:] + relay_high.astype(F32)).astype(BF16), "grp", 1)
    y_low = exchange((near_y[:half] + relay_low.astype(F32)).astype(BF16), "grp", 2)
    own = dot_nn(blocks[0], leaf_z) - dot_nn(leaf_link, first_all)
    low = own[:half] + x_low.astype(F32) + y_low.astype(F32)
    high = own[half:] + x_high.astype(F32) + y_high.astype(F32)
    return jnp.concatenate([low, high], axis=0), solution_here


def fits(leaf_rhs, leaf_inv, sep_rhs, sep_factor, leaf_link):
    levels, slice_width, sep_block = sep_rhs.shape
    width = leaf_rhs.shape[1]
    count = lax.axis_size("grp")
    leaves = lax.axis_size("leaf")
    return (
        count == 2**2
        and leaf_inv.shape[1] == count * leaf_rhs.shape[0]
        and leaf_rhs.shape[0] % 256 == 0
        and leaf_link.shape[1] == 2 * sep_block
        and sep_block % 16 == 0
        and slice_width % 128 == 0
        and levels <= count
        and sep_block % sep_factor.shape[0] == 0
        and sep_factor.shape[1] + levels <= width
        and width % (leaves * sep_block) == 0
    )


def local(*args):
    leaf_rhs, leaf_inv, _, _, leaf_link, sep_rhs, sep_factor, _ = args
    if fits(leaf_rhs, leaf_inv, sep_rhs, sep_factor, leaf_link):
        return local_pairs(*args)
    return local_general(*args)


def solution(mesh):
    placed = (
        P(("leaf", "grp"), None),
        P(("leaf", "grp"), None),
        P("leaf", None),
        P(("leaf", "grp")),
        P(("leaf", "grp"), None),
        P(None, "grp", "leaf"),
        P(("leaf", "grp"), None),
        P(None, "leaf"),
    )
    return jax.shard_map(
        local,
        mesh=mesh,
        in_specs=placed,
        out_specs=(P(("leaf", "grp"), None), P(None, "grp", "leaf")),
        check_vma=False,
    )
```

```python
import functools
import math

import jax
import jax.numpy as jnp
from jax import lax
from jax.experimental import pallas as pl
from jax.experimental.pallas import tpu as pltpu
from jax.sharding import PartitionSpec as P


F32 = jnp.float32
BF16 = jnp.bfloat16
LANES = 128
UNROLL = 32


def exchange(block, axis, mask):
    count = lax.axis_size(axis)
    return lax.ppermute(block, axis, [(low, low ^ mask) for low in range(count)])


def level_offset(sep_block, tree_level):
    if tree_level >= 2:
        return sep_block * (2 ** (tree_level + 1) - 6)
    return 0


def dot_tn(lhs, rhs):
    return lax.dot_general(lhs, rhs, (((0,), (0,)), ((), ())), preferred_element_type=F32)


def dot_nn(lhs, rhs):
    return jnp.dot(lhs, rhs, preferred_element_type=F32)


def vmem():
    return pl.BlockSpec(memory_space=pltpu.VMEM)


def smem():
    return pl.BlockSpec(memory_space=pltpu.SMEM)


def call(body, ops, specs, out_shape, after=(), **rest):
    skip = len(after)

    def skipping(*refs):
        body(*refs[skip:])

    out_specs = jax.tree.map(lambda _: vmem(), out_shape)
    return pl.pallas_call(
        skipping,
        out_shape=out_shape,
        in_specs=[pl.BlockSpec(memory_space=pl.ANY)] * skip + specs,
        out_specs=out_specs,
        **rest,
    )(*after, *ops)


def from_partner(block, axis, distance):
    count = lax.axis_size(axis)
    route = []
    for low in range(count):
        high = low | 1 << distance
        if high != low and high < count:
            route += [(low, high), (high, low)]
    return lax.ppermute(block, axis, route)


def partner(values, level_bit):
    return from_partner(values.astype(jnp.bfloat16), "leaf", level_bit).astype(values.dtype)


def leaf_bit(level_bit):
    return jnp.right_shift(lax.axis_index("leaf"), level_bit) % 2


def spread(values, first_bit, last_bit):
    for level_bit in range(first_bit, last_bit):
        partner_rows = partner(values.astype(jnp.float32), level_bit).astype(jnp.bfloat16)
        low_first = jnp.concatenate([values, partner_rows], axis=-1)
        high_first = jnp.concatenate([partner_rows, values], axis=-1)
        values = jnp.where(leaf_bit(level_bit) == 0, low_first, high_first)
    return values


def halve_sum(values, bit_list):
    for level_bit in bit_list:
        half_width = values.shape[-1] // 2
        low_half = values[..., :half_width]
        high_half = values[..., half_width:]
        is_upper = leaf_bit(level_bit) == 1
        keep_half = jnp.where(is_upper, high_half, low_half)
        send_half = jnp.where(is_upper, low_half, high_half)
        values = keep_half + partner(send_half, level_bit)
    return values


def group_rows(values):
    return lax.all_gather(values, "grp", axis=0, tiled=True)


def level_width(sep_block, tree_level):
    if tree_level >= 2:
        return 2 * sep_block * 2**tree_level
    return sep_block * 2**tree_level


def local_general(leaf_rhs, leaf_inv, ordering, leaf_dinv, leaf_link, sep_rhs, sep_factor, sep_dinv):
    levels = sep_rhs.shape[0]
    sep_block = sep_rhs.shape[2]
    inverse = jnp.argsort(ordering[0])
    picked = jnp.take(leaf_inv, inverse, axis=1)
    leaf_y = jnp.dot(
        picked,
        lax.all_gather(leaf_rhs, "grp", axis=0, tiled=True),
        preferred_element_type=jnp.float32,
    )
    partial_sum = jnp.einsum("rk,rc->kc", leaf_rhs, leaf_link, preferred_element_type=jnp.float32)
    crossing = lax.psum_scatter(
        partial_sum.astype(jnp.bfloat16), "grp", scatter_dimension=0, tiled=True
    ).astype(jnp.float32)
    leaf_z = (leaf_dinv.astype(jnp.float32)[:, None] * leaf_y).astype(jnp.bfloat16)
    crossing = halve_sum(crossing, [0])
    sep_r = (sep_rhs[0].astype(jnp.float32) - crossing).astype(jnp.bfloat16)
    gathered = group_rows(sep_factor)

    def level_rows(tree_level):
        offset = level_offset(sep_block, tree_level)
        return lax.slice_in_dim(
            gathered, offset, offset + level_width(sep_block, tree_level), axis=1
        )

    z_blocks = []
    full_prev = sep_r
    for tree_level in range(1, levels + 1):
        rows_here = level_rows(tree_level)
        size_here = sep_block * 2**tree_level
        if tree_level >= 2:
            children = spread(full_prev, tree_level - 1, tree_level)
            link_rows = rows_here[:, size_here:]
            coupled = jnp.einsum(
                "kc,qc->kq", children, link_rows, preferred_element_type=jnp.float32
            )
            sep_r = (sep_rhs[tree_level - 1].astype(jnp.float32) - coupled).astype(jnp.bfloat16)
        full_prev = spread(sep_r, 0, tree_level)
        sep_y = jnp.einsum(
            "kc,qc->kq", full_prev, rows_here[:, :size_here], preferred_element_type=jnp.float32
        )
        z_blocks.append(
            (sep_dinv[tree_level - 1].astype(jnp.float32)[None, :] * sep_y).astype(jnp.bfloat16)
        )
    solution = [None] * levels
    upper_rows = level_rows(levels)
    size_top = sep_block * 2**levels
    partial_value = jnp.einsum(
        "kq,qc->kc",
        z_blocks[levels - 1],
        upper_rows[:, :size_top],
        preferred_element_type=jnp.float32,
    )
    current = halve_sum(partial_value, list(range(levels - 1, -1, -1)))
    solution[levels - 1] = current
    for tree_level in range(levels - 1, 0, -1):
        size_here = sep_block * 2**tree_level
        link_rows = upper_rows[:, 2 * size_here :]
        rows_here = level_rows(tree_level)
        pushed = -jnp.einsum(
            "kq,qc->kc", current.astype(jnp.bfloat16), link_rows, preferred_element_type=jnp.float32
        )
        pushed = halve_sum(pushed, [tree_level])
        pushed = pushed + jnp.einsum(
            "kq,qc->kc",
            z_blocks[tree_level - 1],
            rows_here[:, :size_here],
            preferred_element_type=jnp.float32,
        )
        current = halve_sum(pushed, list(range(tree_level - 1, -1, -1)))
        solution[tree_level - 1] = current
        upper_rows = rows_here
    first_full = spread(current.astype(jnp.bfloat16), 0, 1)
    first_all = group_rows(first_full)
    picked = jnp.take(leaf_inv, inverse, axis=1)
    leaf_x = lax.psum_scatter(
        jnp.einsum("rm,rk->mk", picked, leaf_z, preferred_element_type=jnp.float32).astype(
            jnp.bfloat16
        ),
        "grp",
        scatter_dimension=0,
        tiled=True,
    ).astype(jnp.float32)
    leaf_x = leaf_x - jnp.einsum(
        "rc,kc->rk", leaf_link, first_all, preferred_element_type=jnp.float32
    )
    return (leaf_x, jnp.stack(solution, axis=0))


def pack_body(rhs_ref, link_ref, sep_ref, fac_ref, out_ref):
    levels, sep_block, width = sep_ref.shape
    first = link_ref.shape[0]
    rows, cols = fac_ref.shape
    out_ref[0:first, :] = dot_nn(link_ref[...], rhs_ref[...]).astype(BF16)
    out_ref[first:, :] = jnp.zeros((out_ref.shape[0] - first, out_ref.shape[1]), BF16)
    for level in range(levels):
        out_ref[first : first + sep_block, level * width : (level + 1) * width] = sep_ref[
            level
        ]
    out_ref[first + sep_block : first + sep_block + rows, 0:cols] = fac_ref[...]


def leaf_body(place_ref, own_ref, x_ref, y_ref, d_ref, dinv_ref, out_ref, *, first, levels, rows, cols):
    sep_block = dinv_ref.shape[1]
    width = out_ref.shape[1]
    me = place_ref[1]
    parts = (own_ref, x_ref, y_ref, d_ref)
    total = parts[0][0:first, :].astype(F32)
    for part in parts[1:]:
        total = total + part[0:first, :].astype(F32)
    out_ref[0:first, :] = total.astype(BF16)
    part_width = width // len(parts)
    for index, part in enumerate(parts):
        lanes = pl.ds(pl.multiple_of((me ^ index) * part_width, part_width), part_width)
        for level in range(levels):
            out_ref[first + level * sep_block : first + (level + 1) * sep_block, lanes] = part[
                first : first + sep_block, level * part_width : (level + 1) * part_width
            ]
    row_owner = lax.broadcasted_iota(jnp.int32, (sep_block, width), 0) // rows
    lane = lax.broadcasted_iota(jnp.int32, (sep_block, width), 1)
    factor = jnp.zeros((sep_block, width), F32)
    for index, part in enumerate(parts):
        block = part[first + sep_block : first + 2 * sep_block, :].astype(F32)[0:rows, :]
        tiled = jnp.concatenate([block] * (sep_block // rows), axis=0)
        factor = factor + jnp.where(row_owner == (me ^ index), tiled, 0.0)
    pivots = dinv_ref[...].astype(F32).T
    for level in range(levels):
        column = jnp.broadcast_to(pivots[:, level : level + 1], (sep_block, width))
        factor = jnp.where(lane == cols + level, column, factor)
    out_ref[first + levels * sep_block :, :] = factor.astype(BF16)


def pair_body(place_ref, own_ref, other_ref, out_ref, *, first, levels, sep_block):
    is_odd = place_ref[0] % 2 == 1
    own = own_ref[...].astype(F32)
    other = other_ref[...].astype(F32)
    even = jnp.where(is_odd, other, own)
    odd = jnp.where(is_odd, own, other)
    crossing = even[0:first] + odd[0:first]
    for level in range(levels + 1):
        base = first + level * sep_block
        both = jnp.concatenate([even[base : base + sep_block], odd[base : base + sep_block]], axis=0)
        if level == 0:
            both = both - crossing
        out_ref[level * first : (level + 1) * first, :] = both.astype(BF16)


def tree_body(
    place_ref, *refs, count, first, levels, sep_block, cols, slice_width
):
    pairs = refs[:count]
    first_ref, sol_ref, stage_ref, val_ref = refs[count:]
    leaf, me = place_ref[0], place_ref[1]
    pair = leaf // 2
    nsep = count * first
    width = pairs[0].shape[1]
    for index, ref in enumerate(pairs):
        place = pl.ds(pl.multiple_of((pair ^ index) * first, first), first)
        for level in range(levels + 1):
            stage_ref[level, place, :] = ref[level * first : (level + 1) * first, :]
    factor = stage_ref[levels]
    column = lax.broadcasted_iota(jnp.int32, (width, nsep), 0)
    target = lax.broadcasted_iota(jnp.int32, (width, nsep), 1)
    row = lax.broadcasted_iota(jnp.int32, (nsep, nsep), 0)
    lane = lax.broadcasted_iota(jnp.int32, (nsep, nsep), 1)

    def block_diagonal(offset, size):
        choose = jnp.where(column == offset + target % size, 1.0, 0.0).astype(BF16)
        spread = dot_nn(factor, choose)
        return jnp.where(row // size == lane // size, spread, 0.0).astype(BF16)

    weights, couplings, z_blocks = [], [], []
    residual = stage_ref[0]
    for level in range(1, levels + 1):
        size = sep_block * 2**level
        offset = level_offset(sep_block, level)
        weight = block_diagonal(offset, size)
        coupling = None
        if level >= 2:
            coupling = block_diagonal(offset + size, size)
            residual = (stage_ref[level - 1].astype(F32) - dot_nn(coupling, residual)).astype(BF16)
        choose = jnp.where(column == cols + level - 1, 1.0, 0.0).astype(BF16)
        scale = dot_nn(factor, choose)
        scale = jnp.concatenate([scale] * (width // nsep), axis=1)
        z_blocks.append((scale * dot_nn(weight, residual)).astype(BF16))
        weights.append(weight)
        couplings.append(coupling)
    current = None
    for level in range(levels, 0, -1):
        value = dot_tn(weights[level - 1], z_blocks[level - 1])
        if level < levels:
            value = value - dot_tn(couplings[level], current.astype(BF16))
        current = value
        val_ref[...] = value
        lanes = pl.ds(pl.multiple_of(me * slice_width, slice_width), slice_width)
        mine = val_ref[pl.ds(pl.multiple_of(leaf * sep_block, sep_block), sep_block), lanes]
        sol_ref[level - 1] = mine
    first_ref[...] = val_ref[pl.ds(pl.multiple_of(pair * first, first), first), :].astype(BF16)


def arrange_body(dest_ref, factor_ref, *refs):
    outs, (turned_ref, sorted_ref) = refs[:-2], refs[-2:]
    step = pl.program_id(0)
    rows, width = factor_ref.shape
    tiles = rows // LANES
    turned = factor_ref[...].astype(F32).T
    for tile in range(tiles):
        turned_ref[pl.ds(tile, width, stride=tiles), :] = turned[:, tile * LANES : (tile + 1) * LANES]

    def move(group, carry):
        for lane in range(UNROLL):
            source = group * UNROLL + lane
            target = dest_ref[step * width + source]
            sorted_ref[pl.ds(pl.multiple_of(target * tiles, tiles), tiles), :] = turned_ref[
                pl.ds(pl.multiple_of(source * tiles, tiles), tiles), :
            ]
        return carry

    lax.fori_loop(0, width // UNROLL, move, 0)

    @pl.when(step == pl.num_programs(0) - 1)
    def _():
        for index, out_ref in enumerate(outs):
            count = out_ref.shape[0]
            chunk = min(count, 256)

            def write(part, carry, index=index, out_ref=out_ref, count=count, chunk=chunk):
                base = index * count * tiles + part * chunk * tiles
                for tile in range(tiles):
                    out_ref[
                        pl.ds(pl.multiple_of(part * chunk, chunk), chunk),
                        tile * LANES : (tile + 1) * LANES,
                    ] = sorted_ref[pl.ds(base + tile, chunk, stride=tiles), :].astype(BF16)
                return carry

            lax.fori_loop(0, count // chunk, write, 0)


def arrange(factor, dest, count):
    rows, cols = factor.shape
    width = math.gcd(cols, 4 * LANES)
    part = cols // count
    return pl.pallas_call(
        arrange_body,
        grid=(cols // width,),
        out_shape=[jax.ShapeDtypeStruct((part, rows), BF16)] * count,
        in_specs=[smem(), pl.BlockSpec((rows, width), lambda step: (0, step))],
        out_specs=[vmem()] * count,
        scratch_shapes=[
            pltpu.VMEM((width * rows // LANES, LANES), F32),
            pltpu.VMEM((cols * rows // LANES, LANES), F32),
        ],
        compiler_params=pltpu.CompilerParams(vmem_limit_bytes=48 * 2**20),
        name="arrange",
    )(dest, factor)


def local_pairs(leaf_rhs, leaf_inv, ordering, leaf_dinv, leaf_link, sep_rhs, sep_factor, sep_dinv):
    rows, width = leaf_rhs.shape
    half = rows // 2
    group = lax.axis_size("grp")
    levels, slice_width, sep_block = sep_rhs.shape
    first = leaf_link.shape[1]
    fac_rows, cols = sep_factor.shape
    leaf = lax.axis_index("leaf").astype(jnp.int32)
    me = lax.axis_index("grp").astype(jnp.int32)
    place = jnp.stack([leaf, me])
    link_turned = leaf_link.T

    low, high = leaf_rhs[:half], leaf_rhs[half:]
    x_low = exchange(low, "grp", 1)
    y_high = exchange(high, "grp", 2)
    x_high = exchange(high, "grp", 1)
    y_low = exchange(low, "grp", 2)
    dest = (ordering[0] // rows ^ me) * rows + ordering[0] % rows
    blocks = arrange(leaf_inv, dest, group)
    d_low = exchange(x_low, "grp", 2)
    d_high = exchange(y_high, "grp", 1)

    aux = call(
        pack_body,
        (leaf_rhs, link_turned, jnp.swapaxes(sep_rhs, 1, 2), sep_factor),
        [vmem()] * 4,
        jax.ShapeDtypeStruct((first + 2 * sep_block, width), BF16),
        after=(x_low, y_high),
    )
    aux_parts = [aux] + [exchange(aux, "grp", mask) for mask in range(1, group)]

    leaf_y = dot_tn(blocks[0], leaf_rhs)
    leaf_y = leaf_y + dot_tn(blocks[1][:half], x_low)
    leaf_y = leaf_y + dot_tn(blocks[2][half:], y_high)
    leaf_y = leaf_y + dot_tn(blocks[1][half:], x_high)
    leaf_y = leaf_y + dot_tn(blocks[2][:half], y_low)
    leaf_y = leaf_y + dot_tn(blocks[3][:half], d_low)
    leaf_y = leaf_y + dot_tn(blocks[3][half:], d_high)
    leaf_z = (leaf_dinv.astype(F32)[:, None] * leaf_y).astype(BF16)

    relay_low = exchange(dot_nn(blocks[3][:half], leaf_z).astype(BF16), "grp", 1)
    relay_high = exchange(dot_nn(blocks[3][half:], leaf_z).astype(BF16), "grp", 2)
    sum_x_low = exchange(dot_nn(blocks[1][:half], leaf_z).astype(BF16), "grp", 1)
    sum_y_high = exchange(dot_nn(blocks[2][half:], leaf_z).astype(BF16), "grp", 2)
    near_x_high = dot_nn(blocks[1][half:], leaf_z)
    near_y_low = dot_nn(blocks[2][:half], leaf_z)

    own = dot_nn(blocks[0], leaf_z)
    leaf_block = call(
        functools.partial(leaf_body, first=first, levels=levels, rows=fac_rows, cols=cols),
        (place, *aux_parts, sep_dinv),
        [smem()] + [vmem()] * 5,
        jax.ShapeDtypeStruct((first + (levels + 1) * sep_block, width), BF16),
        after=(near_x_high, near_y_low, own),
    )
    partner = exchange(leaf_block, "leaf", 1)
    pair_block = call(
        functools.partial(pair_body, first=first, levels=levels, sep_block=sep_block),
        (place, leaf_block, partner),
        [smem(), vmem(), vmem()],
        jax.ShapeDtypeStruct(((levels + 1) * first, width), BF16),
    )
    count = lax.axis_size("leaf") // 2
    pairs = [pair_block] + [exchange(pair_block, "leaf", 2 * mask) for mask in range(1, count)]
    nsep = count * first
    first_all, sep_turned = pl.pallas_call(
        functools.partial(
            tree_body,
            count=count,
            first=first,
            levels=levels,
            sep_block=sep_block,
            cols=cols,
            slice_width=slice_width,
        ),
        out_shape=(
            jax.ShapeDtypeStruct((first, width), BF16),
            jax.ShapeDtypeStruct((levels, sep_block, slice_width), F32),
        ),
        in_specs=[smem()] + [vmem()] * count,
        out_specs=(vmem(), vmem()),
        scratch_shapes=[pltpu.VMEM((levels + 1, nsep, width), BF16), pltpu.VMEM((nsep, width), F32)],
        name="tree",
    )(place, *pairs)

    sum_x_high = exchange((near_x_high + relay_high.astype(F32)).astype(BF16), "grp", 1)
    sum_y_low = exchange((near_y_low + relay_low.astype(F32)).astype(BF16), "grp", 2)
    own = own - dot_tn(link_turned, first_all)
    own_low = own[:half] + sum_x_low.astype(F32) + sum_y_low.astype(F32)
    own_high = own[half:] + sum_x_high.astype(F32) + sum_y_high.astype(F32)
    return jnp.concatenate([own_low, own_high], axis=0), jnp.swapaxes(sep_turned, 1, 2)


def fits(leaf_rhs, leaf_inv, sep_rhs, sep_factor, leaf_link):
    levels, slice_width, sep_block = sep_rhs.shape
    width = leaf_rhs.shape[1]
    count = lax.axis_size("grp")
    leaves = lax.axis_size("leaf")
    return (
        count == 2**2
        and leaf_inv.shape[1] == count * leaf_rhs.shape[0]
        and leaf_rhs.shape[0] % 256 == 0
        and leaf_rhs.shape[0] // LANES == 8
        and leaf_link.shape[1] == 2 * sep_block
        and sep_block % 16 == 0
        and slice_width % 128 == 0
        and levels <= count
        and sep_block % sep_factor.shape[0] == 0
        and sep_factor.shape[1] + levels <= width
        and width % (leaves * sep_block) == 0
    )


def local(*args):
    leaf_rhs, leaf_inv, _, _, leaf_link, sep_rhs, sep_factor, _ = args
    if fits(leaf_rhs, leaf_inv, sep_rhs, sep_factor, leaf_link):
        return local_pairs(*args)
    return local_general(*args)


def solution(mesh):
    placed = (
        P(("leaf", "grp"), None),
        P(("leaf", "grp"), None),
        P("leaf", None),
        P(("leaf", "grp")),
        P(("leaf", "grp"), None),
        P(None, "grp", "leaf"),
        P(("leaf", "grp"), None),
        P(None, "leaf"),
    )
    return jax.shard_map(
        local,
        mesh=mesh,
        in_specs=placed,
        out_specs=(P(("leaf", "grp"), None), P(None, "grp", "leaf")),
        check_vma=False,
    )
```

```python
import functools
import math

import jax
import jax.numpy as jnp
from jax import lax
from jax.experimental import pallas as pl
from jax.experimental.pallas import tpu as pltpu
from jax.sharding import PartitionSpec as P


F32 = jnp.float32
BF16 = jnp.bfloat16
LANES = 128
UNROLL = 32


def exchange(block, axis, mask):
    count = lax.axis_size(axis)
    return lax.ppermute(block, axis, [(low, low ^ mask) for low in range(count)])


def level_offset(sep_block, tree_level):
    if tree_level >= 2:
        return sep_block * (2 ** (tree_level + 1) - 6)
    return 0


def dot_tn(lhs, rhs):
    return lax.dot_general(lhs, rhs, (((0,), (0,)), ((), ())), preferred_element_type=F32)


def dot_nn(lhs, rhs):
    return jnp.dot(lhs, rhs, preferred_element_type=F32)


def vmem():
    return pl.BlockSpec(memory_space=pltpu.VMEM)


def smem():
    return pl.BlockSpec(memory_space=pltpu.SMEM)


def call(body, ops, specs, out_shape, after=(), grant=16, **rest):
    skip = len(after)
    rest.setdefault("out_specs", jax.tree.map(lambda _: vmem(), out_shape))

    def skipping(*refs):
        body(*refs[skip:])

    return pl.pallas_call(
        skipping,
        out_shape=out_shape,
        in_specs=[pl.BlockSpec(memory_space=pl.ANY)] * skip + specs,
        compiler_params=pltpu.CompilerParams(vmem_limit_bytes=grant * 2**20),
        **rest,
    )(*after, *ops)


def from_partner(block, axis, distance):
    count = lax.axis_size(axis)
    route = []
    for low in range(count):
        high = low | 1 << distance
        if high != low and high < count:
            route += [(low, high), (high, low)]
    return lax.ppermute(block, axis, route)


def partner(values, level_bit):
    return from_partner(values.astype(jnp.bfloat16), "leaf", level_bit).astype(values.dtype)


def leaf_bit(level_bit):
    return jnp.right_shift(lax.axis_index("leaf"), level_bit) % 2


def spread(values, first_bit, last_bit):
    for level_bit in range(first_bit, last_bit):
        partner_rows = partner(values.astype(jnp.float32), level_bit).astype(jnp.bfloat16)
        low_first = jnp.concatenate([values, partner_rows], axis=-1)
        high_first = jnp.concatenate([partner_rows, values], axis=-1)
        values = jnp.where(leaf_bit(level_bit) == 0, low_first, high_first)
    return values


def halve_sum(values, bit_list):
    for level_bit in bit_list:
        half_width = values.shape[-1] // 2
        low_half = values[..., :half_width]
        high_half = values[..., half_width:]
        is_upper = leaf_bit(level_bit) == 1
        keep_half = jnp.where(is_upper, high_half, low_half)
        send_half = jnp.where(is_upper, low_half, high_half)
        values = keep_half + partner(send_half, level_bit)
    return values


def group_rows(values):
    return lax.all_gather(values, "grp", axis=0, tiled=True)


def level_width(sep_block, tree_level):
    if tree_level >= 2:
        return 2 * sep_block * 2**tree_level
    return sep_block * 2**tree_level


def local_general(leaf_rhs, leaf_inv, ordering, leaf_dinv, leaf_link, sep_rhs, sep_factor, sep_dinv):
    levels = sep_rhs.shape[0]
    sep_block = sep_rhs.shape[2]
    inverse = jnp.argsort(ordering[0])
    picked = jnp.take(leaf_inv, inverse, axis=1)
    leaf_y = jnp.dot(
        picked,
        lax.all_gather(leaf_rhs, "grp", axis=0, tiled=True),
        preferred_element_type=jnp.float32,
    )
    partial_sum = jnp.einsum("rk,rc->kc", leaf_rhs, leaf_link, preferred_element_type=jnp.float32)
    crossing = lax.psum_scatter(
        partial_sum.astype(jnp.bfloat16), "grp", scatter_dimension=0, tiled=True
    ).astype(jnp.float32)
    leaf_z = (leaf_dinv.astype(jnp.float32)[:, None] * leaf_y).astype(jnp.bfloat16)
    crossing = halve_sum(crossing, [0])
    sep_r = (sep_rhs[0].astype(jnp.float32) - crossing).astype(jnp.bfloat16)
    gathered = group_rows(sep_factor)

    def level_rows(tree_level):
        offset = level_offset(sep_block, tree_level)
        return lax.slice_in_dim(
            gathered, offset, offset + level_width(sep_block, tree_level), axis=1
        )

    z_blocks = []
    full_prev = sep_r
    for tree_level in range(1, levels + 1):
        rows_here = level_rows(tree_level)
        size_here = sep_block * 2**tree_level
        if tree_level >= 2:
            children = spread(full_prev, tree_level - 1, tree_level)
            link_rows = rows_here[:, size_here:]
            coupled = jnp.einsum(
                "kc,qc->kq", children, link_rows, preferred_element_type=jnp.float32
            )
            sep_r = (sep_rhs[tree_level - 1].astype(jnp.float32) - coupled).astype(jnp.bfloat16)
        full_prev = spread(sep_r, 0, tree_level)
        sep_y = jnp.einsum(
            "kc,qc->kq", full_prev, rows_here[:, :size_here], preferred_element_type=jnp.float32
        )
        z_blocks.append(
            (sep_dinv[tree_level - 1].astype(jnp.float32)[None, :] * sep_y).astype(jnp.bfloat16)
        )
    solution = [None] * levels
    upper_rows = level_rows(levels)
    size_top = sep_block * 2**levels
    partial_value = jnp.einsum(
        "kq,qc->kc",
        z_blocks[levels - 1],
        upper_rows[:, :size_top],
        preferred_element_type=jnp.float32,
    )
    current = halve_sum(partial_value, list(range(levels - 1, -1, -1)))
    solution[levels - 1] = current
    for tree_level in range(levels - 1, 0, -1):
        size_here = sep_block * 2**tree_level
        link_rows = upper_rows[:, 2 * size_here :]
        rows_here = level_rows(tree_level)
        pushed = -jnp.einsum(
            "kq,qc->kc", current.astype(jnp.bfloat16), link_rows, preferred_element_type=jnp.float32
        )
        pushed = halve_sum(pushed, [tree_level])
        pushed = pushed + jnp.einsum(
            "kq,qc->kc",
            z_blocks[tree_level - 1],
            rows_here[:, :size_here],
            preferred_element_type=jnp.float32,
        )
        current = halve_sum(pushed, list(range(tree_level - 1, -1, -1)))
        solution[tree_level - 1] = current
        upper_rows = rows_here
    first_full = spread(current.astype(jnp.bfloat16), 0, 1)
    first_all = group_rows(first_full)
    picked = jnp.take(leaf_inv, inverse, axis=1)
    leaf_x = lax.psum_scatter(
        jnp.einsum("rm,rk->mk", picked, leaf_z, preferred_element_type=jnp.float32).astype(
            jnp.bfloat16
        ),
        "grp",
        scatter_dimension=0,
        tiled=True,
    ).astype(jnp.float32)
    leaf_x = leaf_x - jnp.einsum(
        "rc,kc->rk", leaf_link, first_all, preferred_element_type=jnp.float32
    )
    return (leaf_x, jnp.stack(solution, axis=0))


def pack_body(low_ref, high_ref, link_ref, sep_ref, fac_ref, out_ref):
    levels, sep_block, width = sep_ref.shape
    first = link_ref.shape[0]
    rows, cols = fac_ref.shape
    half = low_ref.shape[0]
    crossing = dot_nn(link_ref[:, :half], low_ref[...]) + dot_nn(link_ref[:, half:], high_ref[...])
    out_ref[0:first, :] = crossing.astype(BF16)
    out_ref[first:, :] = jnp.zeros((out_ref.shape[0] - first, out_ref.shape[1]), BF16)
    for level in range(levels):
        out_ref[first : first + sep_block, level * width : (level + 1) * width] = sep_ref[
            level
        ]
    out_ref[first + sep_block : first + sep_block + rows, 0:cols] = fac_ref[...]


def leaf_body(own_ref, x_ref, y_ref, d_ref, dinv_ref, out_ref, *, first, levels, rows, cols):
    sep_block = dinv_ref.shape[1]
    width = out_ref.shape[1]
    me = lax.axis_index("grp")
    parts = (own_ref, x_ref, y_ref, d_ref)
    total = parts[0][0:first, :].astype(F32)
    for part in parts[1:]:
        total = total + part[0:first, :].astype(F32)
    out_ref[0:first, :] = total.astype(BF16)
    part_width = width // len(parts)
    for index, part in enumerate(parts):
        lanes = pl.ds(pl.multiple_of((me ^ index) * part_width, part_width), part_width)
        for level in range(levels):
            out_ref[first + level * sep_block : first + (level + 1) * sep_block, lanes] = part[
                first : first + sep_block, level * part_width : (level + 1) * part_width
            ]
    row_owner = lax.broadcasted_iota(jnp.int32, (sep_block, width), 0) // rows
    lane = lax.broadcasted_iota(jnp.int32, (sep_block, width), 1)
    factor = jnp.zeros((sep_block, width), F32)
    for index, part in enumerate(parts):
        block = part[first + sep_block : first + 2 * sep_block, :].astype(F32)[0:rows, :]
        tiled = jnp.concatenate([block] * (sep_block // rows), axis=0)
        factor = factor + jnp.where(row_owner == (me ^ index), tiled, 0.0)
    pivots = dinv_ref[...].astype(F32).T
    for level in range(levels):
        column = jnp.broadcast_to(pivots[:, level : level + 1], (sep_block, width))
        factor = jnp.where(lane == cols + level, column, factor)
    out_ref[first + levels * sep_block :, :] = factor.astype(BF16)


def pair_body(own_ref, other_ref, out_ref, *, first, levels, sep_block):
    is_odd = lax.axis_index("leaf") % 2 == 1
    own = own_ref[...].astype(F32)
    other = other_ref[...].astype(F32)
    even = jnp.where(is_odd, other, own)
    odd = jnp.where(is_odd, own, other)
    crossing = even[0:first] + odd[0:first]
    for level in range(levels + 1):
        base = first + level * sep_block
        both = jnp.concatenate([even[base : base + sep_block], odd[base : base + sep_block]], axis=0)
        if level == 0:
            both = both - crossing
        out_ref[level * first : (level + 1) * first, :] = both.astype(BF16)


def tree_body(
    *refs, count, first, levels, sep_block, cols, slice_width
):
    pairs = refs[:count]
    first_ref, sol_ref, stage_ref, val_ref = refs[count:]
    leaf, me = lax.axis_index("leaf"), lax.axis_index("grp")
    pair = leaf // 2
    nsep = count * first
    width = pairs[0].shape[1]
    for index, ref in enumerate(pairs):
        place = pl.ds(pl.multiple_of((pair ^ index) * first, first), first)
        for level in range(levels + 1):
            stage_ref[level, place, :] = ref[level * first : (level + 1) * first, :]
    factor = stage_ref[levels]
    column = lax.broadcasted_iota(jnp.int32, (width, nsep), 0)
    target = lax.broadcasted_iota(jnp.int32, (width, nsep), 1)
    row = lax.broadcasted_iota(jnp.int32, (nsep, nsep), 0)
    lane = lax.broadcasted_iota(jnp.int32, (nsep, nsep), 1)

    def block_diagonal(offset, size):
        choose = jnp.where(column == offset + target % size, 1.0, 0.0).astype(BF16)
        spread = dot_nn(factor, choose)
        return jnp.where(row // size == lane // size, spread, 0.0).astype(BF16)

    weights, couplings, z_blocks = [], [], []
    residual = stage_ref[0]
    for level in range(1, levels + 1):
        size = sep_block * 2**level
        offset = level_offset(sep_block, level)
        weight = block_diagonal(offset, size)
        coupling = None
        if level >= 2:
            coupling = block_diagonal(offset + size, size)
            residual = (stage_ref[level - 1].astype(F32) - dot_nn(coupling, residual)).astype(BF16)
        choose = jnp.where(column == cols + level - 1, 1.0, 0.0).astype(BF16)
        scale = dot_nn(factor, choose)
        scale = jnp.concatenate([scale] * (width // nsep), axis=1)
        z_blocks.append((scale * dot_nn(weight, residual)).astype(BF16))
        weights.append(weight)
        couplings.append(coupling)
    current = None
    for level in range(levels, 0, -1):
        value = dot_tn(weights[level - 1], z_blocks[level - 1])
        if level < levels:
            value = value - dot_tn(couplings[level], current.astype(BF16))
        current = value
        val_ref[...] = value
        lanes = pl.ds(pl.multiple_of(me * slice_width, slice_width), slice_width)
        mine = val_ref[pl.ds(pl.multiple_of(leaf * sep_block, sep_block), sep_block), lanes]
        sol_ref[level - 1] = mine
    first_ref[...] = val_ref[pl.ds(pl.multiple_of(pair * first, first), first), :].astype(BF16)


def arrange_body(dest_ref, factor_ref, *refs):
    outs, (turned_ref, sorted_ref) = refs[:-2], refs[-2:]
    step = pl.program_id(0)
    rows, width = factor_ref.shape
    tiles = rows // LANES
    turned = factor_ref[...].astype(F32).T
    for tile in range(tiles):
        turned_ref[pl.ds(tile, width, stride=tiles), :] = turned[:, tile * LANES : (tile + 1) * LANES]

    def move(group, carry):
        for lane in range(UNROLL):
            source = group * UNROLL + lane
            target = dest_ref[step * width + source]
            sorted_ref[pl.ds(pl.multiple_of(target * tiles, tiles), tiles), :] = turned_ref[
                pl.ds(pl.multiple_of(source * tiles, tiles), tiles), :
            ]
        return carry

    lax.fori_loop(0, width // UNROLL, move, 0)

    @pl.when(step == pl.num_programs(0) - 1)
    def _():
        for index, out_ref in enumerate(outs):
            count = out_ref.shape[0]
            chunk = min(count, 256)

            def write(part, carry, index=index, out_ref=out_ref, count=count, chunk=chunk):
                base = index * count * tiles + part * chunk * tiles
                for tile in range(tiles):
                    out_ref[
                        pl.ds(pl.multiple_of(part * chunk, chunk), chunk),
                        tile * LANES : (tile + 1) * LANES,
                    ] = sorted_ref[pl.ds(base + tile, chunk, stride=tiles), :].astype(BF16)
                return carry

            lax.fori_loop(0, count // chunk, write, 0)


def arrange(factor, dest, count):
    rows, cols = factor.shape
    width = math.gcd(cols, 4 * LANES)
    part = cols // count
    return call(
        arrange_body,
        (dest, pltpu.with_memory_space_constraint(factor, pltpu.HBM)),
        [smem(), pl.BlockSpec((rows, width), lambda step: (0, step))],
        [jax.ShapeDtypeStruct((part, rows), BF16)] * count,
        grant=26,
        grid=(cols // width,),
        scratch_shapes=[
            pltpu.VMEM((width * rows // LANES, LANES), F32),
            pltpu.VMEM((cols * rows // LANES, LANES), F32),
        ],
    )


def split_body(rhs_ref, low_ref, high_ref, sems):
    half = low_ref.shape[0]
    copies = [
        pltpu.make_async_copy(rhs_ref.at[pl.ds(index * half, half), :], ref, sems.at[index])
        for index, ref in enumerate((low_ref, high_ref))
    ]
    for copy in copies:
        copy.start()
    for copy in copies:
        copy.wait()


def forward_body(own_ref, x_ref, y_ref, *refs):
    pieces, (out_ref, factor_ref, loads_ref) = refs[:-3], refs[-3:]
    rows = own_ref.shape[0]
    half = rows // 2
    for index, ref in enumerate((own_ref, x_ref, y_ref)):
        factor_ref[index * rows : (index + 1) * rows, :] = ref[...]
    for index, ref in enumerate(pieces):
        loads_ref[index * half : (index + 1) * half, :] = ref[...]
    out_ref[...] = dot_tn(factor_ref[...], loads_ref[...])


def far_body(
    far_ref, low_ref, high_ref, near_ref, dinv_ref, z_ref, relay_low_ref, relay_high_ref, loads_ref, part_ref
):
    half = low_ref.shape[0]
    loads_ref[:half, :] = low_ref[...]
    loads_ref[half:, :] = high_ref[...]
    part_ref[...] = near_ref[...] + dot_tn(far_ref[...], loads_ref[...])
    pivots = dinv_ref[...].astype(F32)
    width = part_ref.shape[1]
    for tile in range(pivots.shape[0]):
        rows = slice(tile * LANES, (tile + 1) * LANES)
        scale = jnp.broadcast_to(pivots[tile : tile + 1, :], (LANES, LANES)).T
        scale = jnp.concatenate([scale] * (width // LANES), axis=1)
        z_ref[rows, :] = (scale * part_ref[rows, :]).astype(BF16)
    relay_low_ref[...] = dot_nn(far_ref[:half, :], z_ref[...]).astype(BF16)
    relay_high_ref[...] = dot_nn(far_ref[half:, :], z_ref[...]).astype(BF16)


def near_body(own_ref, x_ref, y_ref, z_ref, x_low_ref, y_high_ref, x_high_ref, y_low_ref, out_ref):
    half = x_low_ref.shape[0]
    x_low_ref[...] = dot_nn(x_ref[:half, :], z_ref[...]).astype(BF16)
    y_high_ref[...] = dot_nn(y_ref[half:, :], z_ref[...]).astype(BF16)
    x_high_ref[...] = dot_nn(x_ref[half:, :], z_ref[...])
    y_low_ref[...] = dot_nn(y_ref[:half, :], z_ref[...])
    out_ref[...] = dot_nn(own_ref[...], z_ref[...])


def last_body(own_ref, link_ref, first_ref, x_low_ref, x_high_ref, y_low_ref, y_high_ref, out_ref):
    block = out_ref.shape[0]
    step = pl.program_id(0)
    per_half = x_low_ref.shape[0] // block
    rows = pl.ds(pl.multiple_of(step * block, block), block)
    base = own_ref[rows, :] - dot_tn(link_ref[:, rows], first_ref[...])
    part = pl.ds(pl.multiple_of(step % per_half * block, block), block)

    @pl.when(step < per_half)
    def _():
        out_ref[...] = base + x_low_ref[part, :].astype(F32) + y_low_ref[part, :].astype(F32)

    @pl.when(step >= per_half)
    def _():
        out_ref[...] = base + x_high_ref[part, :].astype(F32) + y_high_ref[part, :].astype(F32)


def local_pairs(leaf_rhs, leaf_inv, ordering, leaf_dinv, leaf_link, sep_rhs, sep_factor, sep_dinv):
    rows, width = leaf_rhs.shape
    half = rows // 2
    group = lax.axis_size("grp")
    levels, slice_width, sep_block = sep_rhs.shape
    first = leaf_link.shape[1]
    fac_rows, cols = sep_factor.shape
    me = lax.axis_index("grp").astype(jnp.int32)
    link_turned = leaf_link.T
    half_bf16 = jax.ShapeDtypeStruct((half, width), BF16)
    half_f32 = jax.ShapeDtypeStruct((half, width), F32)
    full_f32 = jax.ShapeDtypeStruct((rows, width), F32)

    low, high = call(
        split_body,
        (pltpu.with_memory_space_constraint(leaf_rhs, pltpu.HBM),),
        [pl.BlockSpec(memory_space=pltpu.HBM)],
        (half_bf16, half_bf16),
        scratch_shapes=[pltpu.SemaphoreType.DMA((2,))],
    )
    x_low = exchange(low, "grp", 1)
    y_high = exchange(high, "grp", 2)
    x_high = exchange(high, "grp", 1)
    y_low = exchange(low, "grp", 2)
    dest = (ordering[0] // rows ^ me) * rows + ordering[0] % rows
    blocks = arrange(leaf_inv, dest, group)
    d_low = exchange(x_low, "grp", 2)
    d_high = exchange(y_high, "grp", 1)

    aux = call(
        pack_body,
        (low, high, link_turned, jnp.swapaxes(sep_rhs, 1, 2), sep_factor),
        [vmem()] * 5,
        jax.ShapeDtypeStruct((first + 2 * sep_block, width), BF16),
        after=(x_low, y_high),
    )
    aux_parts = [aux] + [exchange(aux, "grp", mask) for mask in range(1, group)]

    part_y = call(
        forward_body,
        (*blocks[:3], low, high, x_low, x_high, y_low, y_high),
        [vmem()] * 9,
        full_f32,
        after=(aux,),
        scratch_shapes=[pltpu.VMEM((3 * rows, rows), BF16), pltpu.VMEM((3 * rows, width), BF16)],
    )
    leaf_z, far_low, far_high = call(
        far_body,
        (blocks[3], d_low, d_high, part_y, leaf_dinv.reshape(-1, LANES)),
        [vmem()] * 5,
        (jax.ShapeDtypeStruct((rows, width), BF16), half_bf16, half_bf16),
        scratch_shapes=[pltpu.VMEM((rows, width), BF16), pltpu.VMEM((rows, width), F32)],
    )
    relay_low = exchange(far_low, "grp", 1)
    relay_high = exchange(far_high, "grp", 2)

    leaf_block = call(
        functools.partial(leaf_body, first=first, levels=levels, rows=fac_rows, cols=cols),
        (*aux_parts, sep_dinv),
        [vmem()] * 5,
        jax.ShapeDtypeStruct((first + (levels + 1) * sep_block, width), BF16),
        after=(far_low,),
    )
    partner = exchange(leaf_block, "leaf", 1)
    near_x_low, near_y_high, near_x_high, near_y_low, own = call(
        near_body,
        (*blocks[:3], leaf_z),
        [vmem()] * 4,
        (half_bf16, half_bf16, half_f32, half_f32, full_f32),
        after=(leaf_block,),
    )
    sum_x_low = exchange(near_x_low, "grp", 1)
    sum_y_high = exchange(near_y_high, "grp", 2)
    pair_block = call(
        functools.partial(pair_body, first=first, levels=levels, sep_block=sep_block),
        (leaf_block, partner),
        [vmem(), vmem()],
        jax.ShapeDtypeStruct(((levels + 1) * first, width), BF16),
        after=(own,),
    )
    count = lax.axis_size("leaf") // 2
    pairs = [pair_block] + [exchange(pair_block, "leaf", 2 * mask) for mask in range(1, count)]
    nsep = count * first
    first_all, sep_turned = call(
        functools.partial(
            tree_body,
            count=count,
            first=first,
            levels=levels,
            sep_block=sep_block,
            cols=cols,
            slice_width=slice_width,
        ),
        pairs,
        [vmem()] * count,
        (
            jax.ShapeDtypeStruct((first, width), BF16),
            jax.ShapeDtypeStruct((levels, sep_block, slice_width), F32),
        ),
        scratch_shapes=[pltpu.VMEM((levels + 1, nsep, width), BF16), pltpu.VMEM((nsep, width), F32)],
    )
    sum_x_high = exchange((near_x_high + relay_high.astype(F32)).astype(BF16), "grp", 1)
    sum_y_low = exchange((near_y_low + relay_low.astype(F32)).astype(BF16), "grp", 2)
    block = rows // 4
    leaf_x = call(
        last_body,
        (own, link_turned, first_all, sum_x_low, sum_x_high, sum_y_low, sum_y_high),
        [vmem()] * 7,
        full_f32,
        grid=(rows // block,),
        out_specs=pl.BlockSpec((block, width), lambda step: (step, 0)),
    )
    return leaf_x, jnp.swapaxes(sep_turned, 1, 2)


def fits(leaf_rhs, leaf_inv, sep_rhs, sep_factor, leaf_link):
    levels, slice_width, sep_block = sep_rhs.shape
    width = leaf_rhs.shape[1]
    count = lax.axis_size("grp")
    leaves = lax.axis_size("leaf")
    return (
        count == 2**2
        and leaf_inv.shape[1] == count * leaf_rhs.shape[0]
        and leaf_rhs.shape[0] % 256 == 0
        and leaf_rhs.shape[0] // LANES == 8
        and leaf_link.shape[1] == 2 * sep_block
        and sep_block % 16 == 0
        and slice_width % 128 == 0
        and levels <= count
        and sep_block % sep_factor.shape[0] == 0
        and sep_factor.shape[1] + levels <= width
        and width % (leaves * sep_block) == 0
    )


def local(*args):
    leaf_rhs, leaf_inv, _, _, leaf_link, sep_rhs, sep_factor, _ = args
    if fits(leaf_rhs, leaf_inv, sep_rhs, sep_factor, leaf_link):
        return local_pairs(*args)
    return local_general(*args)


def solution(mesh):
    placed = (
        P(("leaf", "grp"), None),
        P(("leaf", "grp"), None),
        P("leaf", None),
        P(("leaf", "grp")),
        P(("leaf", "grp"), None),
        P(None, "grp", "leaf"),
        P(("leaf", "grp"), None),
        P(None, "leaf"),
    )
    return jax.shard_map(
        local,
        mesh=mesh,
        in_specs=placed,
        out_specs=(P(("leaf", "grp"), None), P(None, "grp", "leaf")),
        check_vma=False,
    )
```

```python
import functools
import math

import jax
import jax.numpy as jnp
from jax import lax
from jax.experimental import pallas as pl
from jax.experimental.pallas import tpu as pltpu
from jax.sharding import PartitionSpec as P


F32 = jnp.float32
BF16 = jnp.bfloat16
LANES = 128
UNROLL = 32


def exchange(block, axis, mask):
    count = lax.axis_size(axis)
    return lax.ppermute(block, axis, [(low, low ^ mask) for low in range(count)])


def level_offset(sep_block, tree_level):
    if tree_level >= 2:
        return sep_block * (2 ** (tree_level + 1) - 6)
    return 0


def dot_tn(lhs, rhs):
    return lax.dot_general(lhs, rhs, (((0,), (0,)), ((), ())), preferred_element_type=F32)


def dot_nn(lhs, rhs):
    return jnp.dot(lhs, rhs, preferred_element_type=F32)


def vmem():
    return pl.BlockSpec(memory_space=pltpu.VMEM)


def smem():
    return pl.BlockSpec(memory_space=pltpu.SMEM)


def call(body, ops, specs, out_shape, after=(), grant=16, **rest):
    skip = len(after)
    rest.setdefault("out_specs", jax.tree.map(lambda _: vmem(), out_shape))

    def skipping(*refs):
        body(*refs[skip:])

    return pl.pallas_call(
        skipping,
        out_shape=out_shape,
        in_specs=[pl.BlockSpec(memory_space=pl.ANY)] * skip + specs,
        compiler_params=pltpu.CompilerParams(vmem_limit_bytes=grant * 2**20),
        **rest,
    )(*after, *ops)


def from_partner(block, axis, distance):
    count = lax.axis_size(axis)
    route = []
    for low in range(count):
        high = low | 1 << distance
        if high != low and high < count:
            route += [(low, high), (high, low)]
    return lax.ppermute(block, axis, route)


def partner(values, level_bit):
    return from_partner(values.astype(jnp.bfloat16), "leaf", level_bit).astype(values.dtype)


def leaf_bit(level_bit):
    return jnp.right_shift(lax.axis_index("leaf"), level_bit) % 2


def spread(values, first_bit, last_bit):
    for level_bit in range(first_bit, last_bit):
        partner_rows = partner(values.astype(jnp.float32), level_bit).astype(jnp.bfloat16)
        low_first = jnp.concatenate([values, partner_rows], axis=-1)
        high_first = jnp.concatenate([partner_rows, values], axis=-1)
        values = jnp.where(leaf_bit(level_bit) == 0, low_first, high_first)
    return values


def halve_sum(values, bit_list):
    for level_bit in bit_list:
        half_width = values.shape[-1] // 2
        low_half = values[..., :half_width]
        high_half = values[..., half_width:]
        is_upper = leaf_bit(level_bit) == 1
        keep_half = jnp.where(is_upper, high_half, low_half)
        send_half = jnp.where(is_upper, low_half, high_half)
        values = keep_half + partner(send_half, level_bit)
    return values


def group_rows(values):
    return lax.all_gather(values, "grp", axis=0, tiled=True)


def level_width(sep_block, tree_level):
    if tree_level >= 2:
        return 2 * sep_block * 2**tree_level
    return sep_block * 2**tree_level


def local_general(leaf_rhs, leaf_inv, ordering, leaf_dinv, leaf_link, sep_rhs, sep_factor, sep_dinv):
    levels = sep_rhs.shape[0]
    sep_block = sep_rhs.shape[2]
    inverse = jnp.argsort(ordering[0])
    picked = jnp.take(leaf_inv, inverse, axis=1)
    leaf_y = jnp.dot(
        picked,
        lax.all_gather(leaf_rhs, "grp", axis=0, tiled=True),
        preferred_element_type=jnp.float32,
    )
    partial_sum = jnp.einsum("rk,rc->kc", leaf_rhs, leaf_link, preferred_element_type=jnp.float32)
    crossing = lax.psum_scatter(
        partial_sum.astype(jnp.bfloat16), "grp", scatter_dimension=0, tiled=True
    ).astype(jnp.float32)
    leaf_z = (leaf_dinv.astype(jnp.float32)[:, None] * leaf_y).astype(jnp.bfloat16)
    crossing = halve_sum(crossing, [0])
    sep_r = (sep_rhs[0].astype(jnp.float32) - crossing).astype(jnp.bfloat16)
    gathered = group_rows(sep_factor)

    def level_rows(tree_level):
        offset = level_offset(sep_block, tree_level)
        return lax.slice_in_dim(
            gathered, offset, offset + level_width(sep_block, tree_level), axis=1
        )

    z_blocks = []
    full_prev = sep_r
    for tree_level in range(1, levels + 1):
        rows_here = level_rows(tree_level)
        size_here = sep_block * 2**tree_level
        if tree_level >= 2:
            children = spread(full_prev, tree_level - 1, tree_level)
            link_rows = rows_here[:, size_here:]
            coupled = jnp.einsum(
                "kc,qc->kq", children, link_rows, preferred_element_type=jnp.float32
            )
            sep_r = (sep_rhs[tree_level - 1].astype(jnp.float32) - coupled).astype(jnp.bfloat16)
        full_prev = spread(sep_r, 0, tree_level)
        sep_y = jnp.einsum(
            "kc,qc->kq", full_prev, rows_here[:, :size_here], preferred_element_type=jnp.float32
        )
        z_blocks.append(
            (sep_dinv[tree_level - 1].astype(jnp.float32)[None, :] * sep_y).astype(jnp.bfloat16)
        )
    solution = [None] * levels
    upper_rows = level_rows(levels)
    size_top = sep_block * 2**levels
    partial_value = jnp.einsum(
        "kq,qc->kc",
        z_blocks[levels - 1],
        upper_rows[:, :size_top],
        preferred_element_type=jnp.float32,
    )
    current = halve_sum(partial_value, list(range(levels - 1, -1, -1)))
    solution[levels - 1] = current
    for tree_level in range(levels - 1, 0, -1):
        size_here = sep_block * 2**tree_level
        link_rows = upper_rows[:, 2 * size_here :]
        rows_here = level_rows(tree_level)
        pushed = -jnp.einsum(
            "kq,qc->kc", current.astype(jnp.bfloat16), link_rows, preferred_element_type=jnp.float32
        )
        pushed = halve_sum(pushed, [tree_level])
        pushed = pushed + jnp.einsum(
            "kq,qc->kc",
            z_blocks[tree_level - 1],
            rows_here[:, :size_here],
            preferred_element_type=jnp.float32,
        )
        current = halve_sum(pushed, list(range(tree_level - 1, -1, -1)))
        solution[tree_level - 1] = current
        upper_rows = rows_here
    first_full = spread(current.astype(jnp.bfloat16), 0, 1)
    first_all = group_rows(first_full)
    picked = jnp.take(leaf_inv, inverse, axis=1)
    leaf_x = lax.psum_scatter(
        jnp.einsum("rm,rk->mk", picked, leaf_z, preferred_element_type=jnp.float32).astype(
            jnp.bfloat16
        ),
        "grp",
        scatter_dimension=0,
        tiled=True,
    ).astype(jnp.float32)
    leaf_x = leaf_x - jnp.einsum(
        "rc,kc->rk", leaf_link, first_all, preferred_element_type=jnp.float32
    )
    return (leaf_x, jnp.stack(solution, axis=0))


def pack_body(low_ref, high_ref, link_ref, sep_ref, fac_ref, out_ref):
    levels, sep_block, width = sep_ref.shape
    first = link_ref.shape[0]
    rows, cols = fac_ref.shape
    half = low_ref.shape[0]
    crossing = dot_nn(link_ref[:, :half], low_ref[...]) + dot_nn(link_ref[:, half:], high_ref[...])
    out_ref[0:first, :] = crossing.astype(BF16)
    for level in range(levels):
        out_ref[first : first + sep_block, level * width : (level + 1) * width] = sep_ref[
            level
        ]
    tiles = sep_block // rows
    factor = fac_ref[...].astype(F32)
    factor = jnp.concatenate([factor, jnp.zeros((rows, tiles * LANES - cols), F32)], axis=1)
    folded = [factor[:, tile * LANES : (tile + 1) * LANES] for tile in range(tiles)]
    out_ref[first:, levels * width :] = jnp.concatenate(folded, axis=0).astype(BF16)


def leaf_body(own_ref, x_ref, y_ref, d_ref, dinv_ref, out_ref, *, first, levels, rows, cols):
    sep_block = dinv_ref.shape[1]
    width = out_ref.shape[1]
    me = lax.axis_index("grp")
    parts = (own_ref, x_ref, y_ref, d_ref)
    total = parts[0][0:first, :].astype(F32)
    for part in parts[1:]:
        total = total + part[0:first, :].astype(F32)
    out_ref[0:first, :] = total.astype(BF16)
    part_width = width // len(parts)
    for index, part in enumerate(parts):
        lanes = pl.ds(pl.multiple_of((me ^ index) * part_width, part_width), part_width)
        for level in range(levels):
            out_ref[first + level * sep_block : first + (level + 1) * sep_block, lanes] = part[
                first : first + sep_block, level * part_width : (level + 1) * part_width
            ]
    row_owner = lax.broadcasted_iota(jnp.int32, (sep_block, width), 0) // rows
    lane = lax.broadcasted_iota(jnp.int32, (sep_block, width), 1)
    factor = jnp.zeros((sep_block, width), F32)
    for index, part in enumerate(parts):
        folded = part[first:, levels * part_width :].astype(F32)
        block = [folded[tile * rows : (tile + 1) * rows, :] for tile in range(sep_block // rows)]
        block = jnp.concatenate(block, axis=1)
        tiled = jnp.concatenate([block] * (sep_block // rows), axis=0)
        factor = factor + jnp.where(row_owner == (me ^ index), tiled, 0.0)
    pivots = dinv_ref[...].astype(F32).T
    for level in range(levels):
        column = jnp.broadcast_to(pivots[:, level : level + 1], (sep_block, width))
        factor = jnp.where(lane == cols + level, column, factor)
    out_ref[first + levels * sep_block :, :] = factor.astype(BF16)


def pair_body(own_ref, other_ref, out_ref, *, first, levels, sep_block):
    is_odd = lax.axis_index("leaf") % 2 == 1
    own = own_ref[...].astype(F32)
    other = other_ref[...].astype(F32)
    even = jnp.where(is_odd, other, own)
    odd = jnp.where(is_odd, own, other)
    crossing = even[0:first] + odd[0:first]
    for level in range(levels + 1):
        base = first + level * sep_block
        both = jnp.concatenate([even[base : base + sep_block], odd[base : base + sep_block]], axis=0)
        if level == 0:
            both = both - crossing
        out_ref[level * first : (level + 1) * first, :] = both.astype(BF16)


def tree_body(
    *refs, count, first, levels, sep_block, cols, slice_width
):
    pairs = refs[:count]
    first_ref, sol_ref, stage_ref, val_ref = refs[count:]
    leaf, me = lax.axis_index("leaf"), lax.axis_index("grp")
    pair = leaf // 2
    nsep = count * first
    width = pairs[0].shape[1]
    for index, ref in enumerate(pairs):
        place = pl.ds(pl.multiple_of((pair ^ index) * first, first), first)
        for level in range(levels + 1):
            stage_ref[level, place, :] = ref[level * first : (level + 1) * first, :]
    factor = stage_ref[levels]
    column = lax.broadcasted_iota(jnp.int32, (width, nsep), 0)
    target = lax.broadcasted_iota(jnp.int32, (width, nsep), 1)
    row = lax.broadcasted_iota(jnp.int32, (nsep, nsep), 0)
    lane = lax.broadcasted_iota(jnp.int32, (nsep, nsep), 1)

    def block_diagonal(offset, size):
        choose = jnp.where(column == offset + target % size, 1.0, 0.0).astype(BF16)
        spread = dot_nn(factor, choose)
        return jnp.where(row // size == lane // size, spread, 0.0).astype(BF16)

    weights, couplings, z_blocks = [], [], []
    residual = stage_ref[0]
    for level in range(1, levels + 1):
        size = sep_block * 2**level
        offset = level_offset(sep_block, level)
        weight = block_diagonal(offset, size)
        coupling = None
        if level >= 2:
            coupling = block_diagonal(offset + size, size)
            residual = (stage_ref[level - 1].astype(F32) - dot_nn(coupling, residual)).astype(BF16)
        choose = jnp.where(column == cols + level - 1, 1.0, 0.0).astype(BF16)
        scale = dot_nn(factor, choose)
        scale = jnp.concatenate([scale] * (width // nsep), axis=1)
        z_blocks.append((scale * dot_nn(weight, residual)).astype(BF16))
        weights.append(weight)
        couplings.append(coupling)
    current = None
    for level in range(levels, 0, -1):
        value = dot_tn(weights[level - 1], z_blocks[level - 1])
        if level < levels:
            value = value - dot_tn(couplings[level], current.astype(BF16))
        current = value
        val_ref[...] = value
        lanes = pl.ds(pl.multiple_of(me * slice_width, slice_width), slice_width)
        mine = val_ref[pl.ds(pl.multiple_of(leaf * sep_block, sep_block), sep_block), lanes]
        sol_ref[level - 1] = mine
    first_ref[...] = val_ref[pl.ds(pl.multiple_of(pair * first, first), first), :].astype(BF16)


def arrange_body(dest_ref, factor_ref, *refs):
    outs, (turned_ref, sorted_ref) = refs[:-2], refs[-2:]
    step = pl.program_id(0)
    rows, width = factor_ref.shape
    tiles = rows // LANES
    turned = factor_ref[...].astype(F32).T
    for tile in range(tiles):
        turned_ref[pl.ds(tile, width, stride=tiles), :] = turned[:, tile * LANES : (tile + 1) * LANES]

    def move(group, carry):
        for lane in range(UNROLL):
            source = group * UNROLL + lane
            target = dest_ref[step * width + source]
            sorted_ref[pl.ds(pl.multiple_of(target * tiles, tiles), tiles), :] = turned_ref[
                pl.ds(pl.multiple_of(source * tiles, tiles), tiles), :
            ]
        return carry

    lax.fori_loop(0, width // UNROLL, move, 0)

    @pl.when(step == pl.num_programs(0) - 1)
    def _():
        for index, out_ref in enumerate(outs):
            count = out_ref.shape[0]
            chunk = min(count, 256)

            def write(part, carry, index=index, out_ref=out_ref, count=count, chunk=chunk):
                base = index * count * tiles + part * chunk * tiles
                for tile in range(tiles):
                    out_ref[
                        pl.ds(pl.multiple_of(part * chunk, chunk), chunk),
                        tile * LANES : (tile + 1) * LANES,
                    ] = sorted_ref[pl.ds(base + tile, chunk, stride=tiles), :].astype(BF16)
                return carry

            lax.fori_loop(0, count // chunk, write, 0)


def arrange(factor, dest, count):
    rows, cols = factor.shape
    width = math.gcd(cols, 4 * LANES)
    part = cols // count
    return call(
        arrange_body,
        (dest, pltpu.with_memory_space_constraint(factor, pltpu.HBM)),
        [smem(), pl.BlockSpec((rows, width), lambda step: (0, step))],
        [jax.ShapeDtypeStruct((part, rows), BF16)] * count,
        grant=26,
        grid=(cols // width,),
        scratch_shapes=[
            pltpu.VMEM((width * rows // LANES, LANES), F32),
            pltpu.VMEM((cols * rows // LANES, LANES), F32),
        ],
    )


def split_body(rhs_ref, low_ref, high_ref, sems):
    half = low_ref.shape[0]
    copies = [
        pltpu.make_async_copy(rhs_ref.at[pl.ds(index * half, half), :], ref, sems.at[index])
        for index, ref in enumerate((low_ref, high_ref))
    ]
    for copy in copies:
        copy.start()
    for copy in copies:
        copy.wait()


def cut_body(*refs):
    half = len(refs) // 3
    for index, ref in enumerate(refs[:half]):
        width = ref.shape[1] // 2
        for part in range(2):
            refs[half + 2 * index + part][...] = ref[:, part * width : (part + 1) * width]


def forward_body(own_ref, x_ref, y_ref, *refs):
    pieces, (out_0_ref, out_1_ref, factor_ref, loads_ref) = refs[:-4], refs[-4:]
    rows = own_ref.shape[0]
    half = rows // 2
    width = out_0_ref.shape[1]
    for index, ref in enumerate((own_ref, x_ref, y_ref)):
        factor_ref[index * rows : (index + 1) * rows, :] = ref[...]
    for index, ref in enumerate(pieces):
        loads_ref[index * half : (index + 1) * half, :] = ref[...]
    out_0_ref[...] = dot_tn(factor_ref[...], loads_ref[:, :width])
    out_1_ref[...] = dot_tn(factor_ref[...], loads_ref[:, width:])


def far_body(
    far_ref, low_ref, high_ref, near_ref, dinv_ref, z_ref, relay_low_ref, relay_high_ref, loads_ref, part_ref
):
    half = low_ref.shape[0]
    loads_ref[:half, :] = low_ref[...]
    loads_ref[half:, :] = high_ref[...]
    part_ref[...] = near_ref[...] + dot_tn(far_ref[...], loads_ref[...])
    pivots = dinv_ref[...].astype(F32)
    width = part_ref.shape[1]
    for tile in range(pivots.shape[0]):
        rows = slice(tile * LANES, (tile + 1) * LANES)
        scale = jnp.broadcast_to(pivots[tile : tile + 1, :], (LANES, LANES)).T
        scale = jnp.concatenate([scale] * (width // LANES), axis=1)
        z_ref[rows, :] = (scale * part_ref[rows, :]).astype(BF16)
    relay_low_ref[...] = dot_nn(far_ref[:half, :], z_ref[...]).astype(BF16)
    relay_high_ref[...] = dot_nn(far_ref[half:, :], z_ref[...]).astype(BF16)


def near_body(own_ref, x_ref, y_ref, z_0_ref, z_1_ref, x_low_ref, y_high_ref, *refs):
    highs, lows, out_ref = refs[:2], refs[2:4], refs[4]
    half = x_low_ref.shape[0]
    for part, z_ref in enumerate((z_0_ref, z_1_ref)):
        width = z_ref.shape[1]
        cols = slice(part * width, (part + 1) * width)
        x_low_ref[:, cols] = dot_nn(x_ref[:half, :], z_ref[...]).astype(BF16)
        y_high_ref[:, cols] = dot_nn(y_ref[half:, :], z_ref[...]).astype(BF16)
        highs[part][...] = dot_nn(x_ref[half:, :], z_ref[...])
        lows[part][...] = dot_nn(y_ref[:half, :], z_ref[...])
        out_ref[:, cols] = dot_nn(own_ref[...], z_ref[...])


def add_body(near_ref, relay_ref, out_ref):
    out_ref[...] = (near_ref[...] + relay_ref[...].astype(F32)).astype(BF16)


def base_body(own_ref, link_ref, first_ref, x_low_ref, y_high_ref, out_0_ref, out_1_ref):
    half = x_low_ref.shape[0]
    width = out_0_ref.shape[1]
    for part, ref in enumerate((out_0_ref, out_1_ref)):
        cols = slice(part * width, (part + 1) * width)
        ref[...] = own_ref[:, cols] - dot_tn(link_ref[...], first_ref[:, cols])
        ref[:half, :] += x_low_ref[:, cols].astype(F32)
        ref[half:, :] += y_high_ref[:, cols].astype(F32)


def last_body(base_ref, low_ref, high_ref, out_ref):
    block = out_ref.shape[0]
    step = pl.program_id(0)
    per_half = low_ref.shape[0] // block
    rows = pl.ds(pl.multiple_of(step * block, block), block)
    part = pl.ds(pl.multiple_of(step % per_half * block, block), block)

    @pl.when(step < per_half)
    def _():
        out_ref[...] = base_ref[rows, :] + low_ref[part, :].astype(F32)

    @pl.when(step >= per_half)
    def _():
        out_ref[...] = base_ref[rows, :] + high_ref[part, :].astype(F32)


def local_pairs(leaf_rhs, leaf_inv, ordering, leaf_dinv, leaf_link, sep_rhs, sep_factor, sep_dinv):
    rows, width = leaf_rhs.shape
    half = rows // 2
    group = lax.axis_size("grp")
    levels, slice_width, sep_block = sep_rhs.shape
    first = leaf_link.shape[1]
    fac_rows, cols = sep_factor.shape
    me = lax.axis_index("grp").astype(jnp.int32)
    link_turned = leaf_link.T
    half_bf16 = jax.ShapeDtypeStruct((half, width), BF16)
    full_f32 = jax.ShapeDtypeStruct((rows, width), F32)

    low, high = call(
        split_body,
        (pltpu.with_memory_space_constraint(leaf_rhs, pltpu.HBM),),
        [pl.BlockSpec(memory_space=pltpu.HBM)],
        (half_bf16, half_bf16),
        scratch_shapes=[pltpu.SemaphoreType.DMA((2,))],
    )
    x_low = exchange(low, "grp", 1)
    y_high = exchange(high, "grp", 2)
    x_high = exchange(high, "grp", 1)
    y_low = exchange(low, "grp", 2)
    dest = (ordering[0] // rows ^ me) * rows + ordering[0] % rows
    blocks = arrange(leaf_inv, dest, group)
    parts = range(2)
    part_bf16 = jax.ShapeDtypeStruct((half, width // 2), BF16)
    part_f32 = jax.ShapeDtypeStruct((half, width // 2), F32)
    tall_bf16 = jax.ShapeDtypeStruct((rows, width // 2), BF16)
    tall_f32 = jax.ShapeDtypeStruct((rows, width // 2), F32)
    *x_cut, y_cut_0, y_cut_1 = call(
        cut_body, (x_low, y_high), [vmem()] * 2, [part_bf16] * 4, after=(blocks[0],)
    )
    d_low = [exchange(x_cut[part], "grp", 2) for part in parts]
    d_high = [exchange((y_cut_0, y_cut_1)[part], "grp", 1) for part in parts]

    aux = call(
        pack_body,
        (low, high, link_turned, jnp.swapaxes(sep_rhs, 1, 2), sep_factor),
        [vmem()] * 5,
        jax.ShapeDtypeStruct((first + sep_block, width), BF16),
        after=(x_low, y_high),
    )
    aux_parts = [aux] + [exchange(aux, "grp", mask) for mask in range(1, group)]

    part_y = call(
        forward_body,
        (*blocks[:3], low, high, x_low, x_high, y_low, y_high),
        [vmem()] * 9,
        [tall_f32] * 2,
        after=(aux,),
        scratch_shapes=[pltpu.VMEM((3 * rows, rows), BF16), pltpu.VMEM((3 * rows, width), BF16)],
    )
    leaf_z, relay_low, relay_high = [], [], []
    for part in parts:
        z_part, far_low, far_high = call(
            far_body,
            (blocks[3], d_low[part], d_high[part], part_y[part], leaf_dinv.reshape(-1, LANES)),
            [vmem()] * 5,
            (tall_bf16, part_bf16, part_bf16),
            scratch_shapes=[pltpu.VMEM((rows, width // 2), BF16), pltpu.VMEM((rows, width // 2), F32)],
        )
        leaf_z.append(z_part)
        relay_low.append(exchange(far_low, "grp", 1))
        relay_high.append(exchange(far_high, "grp", 2))

    leaf_block = call(
        functools.partial(leaf_body, first=first, levels=levels, rows=fac_rows, cols=cols),
        (*aux_parts, sep_dinv),
        [vmem()] * 5,
        jax.ShapeDtypeStruct((first + (levels + 1) * sep_block, width), BF16),
        after=(leaf_z[1],),
    )
    partner = exchange(leaf_block, "leaf", 1)
    near_x_low, near_y_high, *near, own = call(
        near_body,
        (*blocks[:3], *leaf_z),
        [vmem()] * 5,
        [half_bf16] * 2 + [part_f32] * 4 + [full_f32],
        after=(leaf_block,),
    )
    sum_x_low = exchange(near_x_low, "grp", 1)
    sum_y_high = exchange(near_y_high, "grp", 2)
    pair_block = call(
        functools.partial(pair_body, first=first, levels=levels, sep_block=sep_block),
        (leaf_block, partner),
        [vmem(), vmem()],
        jax.ShapeDtypeStruct(((levels + 1) * first, width), BF16),
        after=(own,),
    )
    count = lax.axis_size("leaf") // 2
    pairs = [pair_block] + [exchange(pair_block, "leaf", 2 * mask) for mask in range(1, count)]
    nsep = count * first
    first_all, sep_turned = call(
        functools.partial(
            tree_body,
            count=count,
            first=first,
            levels=levels,
            sep_block=sep_block,
            cols=cols,
            slice_width=slice_width,
        ),
        pairs,
        [vmem()] * count,
        (
            jax.ShapeDtypeStruct((first, width), BF16),
            jax.ShapeDtypeStruct((levels, sep_block, slice_width), F32),
        ),
        scratch_shapes=[pltpu.VMEM((levels + 1, nsep, width), BF16), pltpu.VMEM((nsep, width), F32)],
    )
    sum_x_high, sum_y_low = [], []
    for part in parts:
        for mask, kept, relay, into in (
            (1, near[part], relay_high[part], sum_x_high),
            (2, near[2 + part], relay_low[part], sum_y_low),
        ):
            total = call(add_body, (kept, relay), [vmem()] * 2, part_bf16)
            into.append(exchange(total, "grp", mask))
    base = call(
        base_body,
        (own, link_turned, first_all, sum_x_low, sum_y_high),
        [vmem()] * 5,
        [tall_f32] * 2,
    )
    block = rows // 4
    leaf_x = ()
    for part in parts:
        leaf_x = (
            call(
                last_body,
                (base[part], sum_y_low[part], sum_x_high[part]),
                [vmem()] * 3,
                full_f32,
                after=leaf_x,
                grid=(rows // block,),
                out_specs=pl.BlockSpec((block, width // 2), lambda step, part=part: (step, part)),
                input_output_aliases={0: 0} if leaf_x else {},
            ),
        )
    leaf_x = leaf_x[0]
    return leaf_x, jnp.swapaxes(sep_turned, 1, 2)


def fits(leaf_rhs, leaf_inv, sep_rhs, sep_factor, leaf_link):
    levels, slice_width, sep_block = sep_rhs.shape
    width = leaf_rhs.shape[1]
    count = lax.axis_size("grp")
    leaves = lax.axis_size("leaf")
    return (
        count == 2**2
        and leaf_inv.shape[1] == count * leaf_rhs.shape[0]
        and leaf_rhs.shape[0] % 256 == 0
        and leaf_rhs.shape[0] // LANES == 8
        and leaf_link.shape[1] == 2 * sep_block
        and sep_block % 16 == 0
        and slice_width % 128 == 0
        and levels <= count
        and sep_block % sep_factor.shape[0] == 0
        and sep_factor.shape[1] + levels <= width
        and width == (levels + 1) * slice_width == sep_block // sep_factor.shape[0] * LANES
        and slice_width == LANES
        and width % (leaves * sep_block) == 0
    )


def local(*args):
    leaf_rhs, leaf_inv, _, _, leaf_link, sep_rhs, sep_factor, _ = args
    if fits(leaf_rhs, leaf_inv, sep_rhs, sep_factor, leaf_link):
        return local_pairs(*args)
    return local_general(*args)


def solution(mesh):
    placed = (
        P(("leaf", "grp"), None),
        P(("leaf", "grp"), None),
        P("leaf", None),
        P(("leaf", "grp")),
        P(("leaf", "grp"), None),
        P(None, "grp", "leaf"),
        P(("leaf", "grp"), None),
        P(None, "leaf"),
    )
    return jax.shard_map(
        local,
        mesh=mesh,
        in_specs=placed,
        out_specs=(P(("leaf", "grp"), None), P(None, "grp", "leaf")),
        check_vma=False,
    )
```

```python
import functools
import math

import jax
import jax.numpy as jnp
from jax import lax
from jax.experimental import pallas as pl
from jax.experimental.pallas import tpu as pltpu
from jax.sharding import PartitionSpec as P


F32 = jnp.float32
BF16 = jnp.bfloat16
LANES = 128
UNROLL = 32


def exchange(block, axis, mask):
    count = lax.axis_size(axis)
    return lax.ppermute(block, axis, [(low, low ^ mask) for low in range(count)])


def level_offset(sep_block, tree_level):
    if tree_level >= 2:
        return sep_block * (2 ** (tree_level + 1) - 6)
    return 0


def dot_tn(lhs, rhs):
    return lax.dot_general(lhs, rhs, (((0,), (0,)), ((), ())), preferred_element_type=F32)


def dot_nn(lhs, rhs):
    return jnp.dot(lhs, rhs, preferred_element_type=F32)


def vmem():
    return pl.BlockSpec(memory_space=pltpu.VMEM)


def smem():
    return pl.BlockSpec(memory_space=pltpu.SMEM)


def call(body, ops, specs, out_shape, after=(), grant=16, **rest):
    skip = len(after)
    rest.setdefault("out_specs", jax.tree.map(lambda _: vmem(), out_shape))

    def skipping(*refs):
        body(*refs[skip:])

    return pl.pallas_call(
        skipping,
        out_shape=out_shape,
        in_specs=[pl.BlockSpec(memory_space=pl.ANY)] * skip + specs,
        compiler_params=pltpu.CompilerParams(vmem_limit_bytes=grant * 2**20),
        **rest,
    )(*after, *ops)


def from_partner(block, axis, distance):
    count = lax.axis_size(axis)
    route = []
    for low in range(count):
        high = low | 1 << distance
        if high != low and high < count:
            route += [(low, high), (high, low)]
    return lax.ppermute(block, axis, route)


def partner(values, level_bit):
    return from_partner(values.astype(jnp.bfloat16), "leaf", level_bit).astype(values.dtype)


def leaf_bit(level_bit):
    return jnp.right_shift(lax.axis_index("leaf"), level_bit) % 2


def spread(values, first_bit, last_bit):
    for level_bit in range(first_bit, last_bit):
        partner_rows = partner(values.astype(jnp.float32), level_bit).astype(jnp.bfloat16)
        low_first = jnp.concatenate([values, partner_rows], axis=-1)
        high_first = jnp.concatenate([partner_rows, values], axis=-1)
        values = jnp.where(leaf_bit(level_bit) == 0, low_first, high_first)
    return values


def halve_sum(values, bit_list):
    for level_bit in bit_list:
        half_width = values.shape[-1] // 2
        low_half = values[..., :half_width]
        high_half = values[..., half_width:]
        is_upper = leaf_bit(level_bit) == 1
        keep_half = jnp.where(is_upper, high_half, low_half)
        send_half = jnp.where(is_upper, low_half, high_half)
        values = keep_half + partner(send_half, level_bit)
    return values


def group_rows(values):
    return lax.all_gather(values, "grp", axis=0, tiled=True)


def level_width(sep_block, tree_level):
    if tree_level >= 2:
        return 2 * sep_block * 2**tree_level
    return sep_block * 2**tree_level


def local_general(leaf_rhs, leaf_inv, ordering, leaf_dinv, leaf_link, sep_rhs, sep_factor, sep_dinv):
    levels = sep_rhs.shape[0]
    sep_block = sep_rhs.shape[2]
    inverse = jnp.argsort(ordering[0])
    picked = jnp.take(leaf_inv, inverse, axis=1)
    leaf_y = jnp.dot(
        picked,
        lax.all_gather(leaf_rhs, "grp", axis=0, tiled=True),
        preferred_element_type=jnp.float32,
    )
    partial_sum = jnp.einsum("rk,rc->kc", leaf_rhs, leaf_link, preferred_element_type=jnp.float32)
    crossing = lax.psum_scatter(
        partial_sum.astype(jnp.bfloat16), "grp", scatter_dimension=0, tiled=True
    ).astype(jnp.float32)
    leaf_z = (leaf_dinv.astype(jnp.float32)[:, None] * leaf_y).astype(jnp.bfloat16)
    crossing = halve_sum(crossing, [0])
    sep_r = (sep_rhs[0].astype(jnp.float32) - crossing).astype(jnp.bfloat16)
    gathered = group_rows(sep_factor)

    def level_rows(tree_level):
        offset = level_offset(sep_block, tree_level)
        return lax.slice_in_dim(
            gathered, offset, offset + level_width(sep_block, tree_level), axis=1
        )

    z_blocks = []
    full_prev = sep_r
    for tree_level in range(1, levels + 1):
        rows_here = level_rows(tree_level)
        size_here = sep_block * 2**tree_level
        if tree_level >= 2:
            children = spread(full_prev, tree_level - 1, tree_level)
            link_rows = rows_here[:, size_here:]
            coupled = jnp.einsum(
                "kc,qc->kq", children, link_rows, preferred_element_type=jnp.float32
            )
            sep_r = (sep_rhs[tree_level - 1].astype(jnp.float32) - coupled).astype(jnp.bfloat16)
        full_prev = spread(sep_r, 0, tree_level)
        sep_y = jnp.einsum(
            "kc,qc->kq", full_prev, rows_here[:, :size_here], preferred_element_type=jnp.float32
        )
        z_blocks.append(
            (sep_dinv[tree_level - 1].astype(jnp.float32)[None, :] * sep_y).astype(jnp.bfloat16)
        )
    solution = [None] * levels
    upper_rows = level_rows(levels)
    size_top = sep_block * 2**levels
    partial_value = jnp.einsum(
        "kq,qc->kc",
        z_blocks[levels - 1],
        upper_rows[:, :size_top],
        preferred_element_type=jnp.float32,
    )
    current = halve_sum(partial_value, list(range(levels - 1, -1, -1)))
    solution[levels - 1] = current
    for tree_level in range(levels - 1, 0, -1):
        size_here = sep_block * 2**tree_level
        link_rows = upper_rows[:, 2 * size_here :]
        rows_here = level_rows(tree_level)
        pushed = -jnp.einsum(
            "kq,qc->kc", current.astype(jnp.bfloat16), link_rows, preferred_element_type=jnp.float32
        )
        pushed = halve_sum(pushed, [tree_level])
        pushed = pushed + jnp.einsum(
            "kq,qc->kc",
            z_blocks[tree_level - 1],
            rows_here[:, :size_here],
            preferred_element_type=jnp.float32,
        )
        current = halve_sum(pushed, list(range(tree_level - 1, -1, -1)))
        solution[tree_level - 1] = current
        upper_rows = rows_here
    first_full = spread(current.astype(jnp.bfloat16), 0, 1)
    first_all = group_rows(first_full)
    picked = jnp.take(leaf_inv, inverse, axis=1)
    leaf_x = lax.psum_scatter(
        jnp.einsum("rm,rk->mk", picked, leaf_z, preferred_element_type=jnp.float32).astype(
            jnp.bfloat16
        ),
        "grp",
        scatter_dimension=0,
        tiled=True,
    ).astype(jnp.float32)
    leaf_x = leaf_x - jnp.einsum(
        "rc,kc->rk", leaf_link, first_all, preferred_element_type=jnp.float32
    )
    return (leaf_x, jnp.stack(solution, axis=0))


def pack_body(low_ref, high_ref, link_ref, fac_ref, *refs):
    outs, crossing_ref = refs[:-1], refs[-1]
    first = link_ref.shape[0]
    rows, cols = fac_ref.shape
    split = low_ref.shape[0]
    crossing = dot_nn(link_ref[:, :split], low_ref[...]) + dot_nn(link_ref[:, split:], high_ref[...])
    crossing_ref[...] = crossing
    tiles = (outs[0].shape[0] - first) // rows
    factor = fac_ref[...].astype(F32)
    factor = jnp.concatenate([factor, jnp.zeros((rows, tiles * LANES - cols), F32)], axis=1)
    folded = [factor[:, tile * LANES : (tile + 1) * LANES] for tile in range(tiles)]
    folded = jnp.concatenate(folded, axis=0).astype(BF16)
    me = lax.axis_index("grp")
    for mask, ref in enumerate(outs):
        lanes = pl.ds(pl.multiple_of((me ^ mask) * LANES, LANES), LANES)
        ref[:first, :] = crossing_ref[:, lanes].astype(BF16)
        ref[first:, :] = folded


def leaf_body(own_ref, x_ref, y_ref, d_ref, sep_ref, dinv_ref, out_ref, *, rows, cols):
    levels, sep_block, _ = sep_ref.shape
    parts = (own_ref, x_ref, y_ref, d_ref)
    first = own_ref.shape[0] - sep_block
    tiles = sep_block // rows
    me = lax.axis_index("grp")
    total = own_ref[:first, :].astype(F32)
    for part in parts[1:]:
        total = total + part[:first, :].astype(F32)
    out_ref[:first, :] = total.astype(BF16)
    for level in range(levels):
        out_ref[first + level * sep_block : first + (level + 1) * sep_block, :] = sep_ref[level]
    row_owner = lax.broadcasted_iota(jnp.int32, (sep_block, tiles * LANES), 0) // rows
    lane = lax.broadcasted_iota(jnp.int32, (sep_block, tiles * LANES), 1)
    factor = jnp.zeros((sep_block, tiles * LANES), F32)
    for index, part in enumerate(parts):
        folded = part[first:, :].astype(F32)
        block = [folded[tile * rows : (tile + 1) * rows, :] for tile in range(tiles)]
        block = jnp.concatenate(block, axis=1)
        tiled = jnp.concatenate([block] * (sep_block // rows), axis=0)
        factor = factor + jnp.where(row_owner == (me ^ index), tiled, 0.0)
    pivots = dinv_ref[...].astype(F32).T
    for level in range(levels):
        column = jnp.broadcast_to(pivots[:, level : level + 1], factor.shape)
        factor = jnp.where(lane == cols + level, column, factor)
    base = first + levels * sep_block
    for tile in range(tiles):
        out_ref[base + tile * sep_block : base + (tile + 1) * sep_block, :] = factor[
            :, tile * LANES : (tile + 1) * LANES
        ].astype(BF16)


def pair_body(own_ref, other_ref, out_ref, *, first, sep_block):
    is_odd = lax.axis_index("leaf") % 2 == 1
    own = own_ref[...].astype(F32)
    other = other_ref[...].astype(F32)
    even = jnp.where(is_odd, other, own)
    odd = jnp.where(is_odd, own, other)
    crossing = even[0:first] + odd[0:first]
    for index in range((own.shape[0] - first) // sep_block):
        base = first + index * sep_block
        both = jnp.concatenate([even[base : base + sep_block], odd[base : base + sep_block]], axis=0)
        if index == 0:
            both = both - crossing
        out_ref[index * first : (index + 1) * first, :] = both.astype(BF16)


def tree_body(*refs, count, first, levels, sep_block, cols):
    pairs = refs[:count]
    first_ref, sol_ref, stage_ref, factor_ref, val_ref = refs[count:]
    leaf = lax.axis_index("leaf")
    pair = leaf // 2
    nsep, width = factor_ref.shape
    for index, ref in enumerate(pairs):
        place = pl.ds(pl.multiple_of((pair ^ index) * first, first), first)
        for level in range(levels):
            stage_ref[level, place, :] = ref[level * first : (level + 1) * first, :]
        for tile in range(width // LANES):
            base = (levels + tile) * first
            factor_ref[place, tile * LANES : (tile + 1) * LANES] = ref[base : base + first, :]
    factor = factor_ref[...]
    column = lax.broadcasted_iota(jnp.int32, (width, nsep), 0)
    target = lax.broadcasted_iota(jnp.int32, (width, nsep), 1)
    row = lax.broadcasted_iota(jnp.int32, (nsep, nsep), 0)
    lane = lax.broadcasted_iota(jnp.int32, (nsep, nsep), 1)

    def block_diagonal(offset, size):
        choose = jnp.where(column == offset + target % size, 1.0, 0.0).astype(BF16)
        spread = dot_nn(factor, choose)
        return jnp.where(row // size == lane // size, spread, 0.0).astype(BF16)

    weights, couplings, z_blocks = [], [], []
    residual = stage_ref[0]
    for level in range(1, levels + 1):
        size = sep_block * 2**level
        offset = level_offset(sep_block, level)
        weight = block_diagonal(offset, size)
        coupling = None
        if level >= 2:
            coupling = block_diagonal(offset + size, size)
            residual = (stage_ref[level - 1].astype(F32) - dot_nn(coupling, residual)).astype(BF16)
        pick = lax.broadcasted_iota(jnp.int32, (width, LANES), 0) == cols + level - 1
        scale = dot_nn(factor, jnp.where(pick, 1.0, 0.0).astype(BF16))
        z_blocks.append((scale * dot_nn(weight, residual)).astype(BF16))
        weights.append(weight)
        couplings.append(coupling)
    current = None
    for level in range(levels, 0, -1):
        value = dot_tn(weights[level - 1], z_blocks[level - 1])
        if level < levels:
            value = value - dot_tn(couplings[level], current.astype(BF16))
        current = value
        val_ref[...] = value
        sol_ref[level - 1] = val_ref[pl.ds(pl.multiple_of(leaf * sep_block, sep_block), sep_block), :]
    first_ref[...] = val_ref[pl.ds(pl.multiple_of(pair * first, first), first), :].astype(BF16)


def arrange_body(dest_ref, factor_ref, *refs):
    outs, (turned_ref, sorted_ref) = refs[:-2], refs[-2:]
    step = pl.program_id(0)
    rows, width = factor_ref.shape
    tiles = rows // LANES
    turned = factor_ref[...].astype(F32).T
    for tile in range(tiles):
        turned_ref[pl.ds(tile, width, stride=tiles), :] = turned[:, tile * LANES : (tile + 1) * LANES]

    def move(group, carry):
        for lane in range(UNROLL):
            source = group * UNROLL + lane
            target = dest_ref[step * width + source]
            sorted_ref[pl.ds(pl.multiple_of(target * tiles, tiles), tiles), :] = turned_ref[
                pl.ds(pl.multiple_of(source * tiles, tiles), tiles), :
            ]
        return carry

    lax.fori_loop(0, width // UNROLL, move, 0)

    @pl.when(step == pl.num_programs(0) - 1)
    def _():
        for index, out_ref in enumerate(outs):
            count = out_ref.shape[0]
            chunk = min(count, 256)

            def write(part, carry, index=index, out_ref=out_ref, count=count, chunk=chunk):
                base = index * count * tiles + part * chunk * tiles
                for tile in range(tiles):
                    out_ref[
                        pl.ds(pl.multiple_of(part * chunk, chunk), chunk),
                        tile * LANES : (tile + 1) * LANES,
                    ] = sorted_ref[pl.ds(base + tile, chunk, stride=tiles), :].astype(BF16)
                return carry

            lax.fori_loop(0, count // chunk, write, 0)


def arrange(factor, dest, count):
    rows, cols = factor.shape
    width = math.gcd(cols, 4 * LANES)
    part = cols // count
    return call(
        arrange_body,
        (dest, pltpu.with_memory_space_constraint(factor, pltpu.HBM)),
        [smem(), pl.BlockSpec((rows, width), lambda step: (0, step))],
        [jax.ShapeDtypeStruct((part, rows), BF16)] * count,
        grant=26,
        grid=(cols // width,),
        scratch_shapes=[
            pltpu.VMEM((width * rows // LANES, LANES), F32),
            pltpu.VMEM((cols * rows // LANES, LANES), F32),
        ],
    )


def split_body(rhs_ref, low_ref, high_ref, sems):
    split = low_ref.shape[0]
    copies = [
        pltpu.make_async_copy(rhs_ref.at[pl.ds(index * split, ref.shape[0]), :], ref, sems.at[index])
        for index, ref in enumerate((low_ref, high_ref))
    ]
    for copy in copies:
        copy.start()
    for copy in copies:
        copy.wait()


def cut_body(whole_ref, *outs):
    for part, ref in enumerate(outs):
        height, width = ref.shape
        ref[...] = whole_ref[:height, part * width : (part + 1) * width]


def forward_body(own_ref, x_ref, y_ref, *refs):
    pieces, (out_0_ref, out_1_ref, factor_ref, loads_ref) = refs[:-4], refs[-4:]
    rows = own_ref.shape[0]
    width = out_0_ref.shape[1]
    for index, ref in enumerate((own_ref, x_ref, y_ref)):
        factor_ref[index * rows : (index + 1) * rows, :] = ref[...]
    start = 0
    for ref in pieces:
        loads_ref[start : start + ref.shape[0], :] = ref[...]
        start += ref.shape[0]
    out_0_ref[...] = dot_tn(factor_ref[...], loads_ref[:, :width])
    out_1_ref[...] = dot_tn(factor_ref[...], loads_ref[:, width:])


def far_body(
    far_ref, low_ref, high_ref, near_ref, dinv_ref, z_ref, relay_low_ref, relay_high_ref, loads_ref, part_ref
):
    split, half = low_ref.shape[0], relay_low_ref.shape[0]
    loads_ref[:split, :] = low_ref[...]
    loads_ref[split:, :] = high_ref[...]
    part_ref[...] = near_ref[...] + dot_tn(far_ref[...], loads_ref[...])
    pivots = dinv_ref[...].astype(F32)
    width = part_ref.shape[1]
    for tile in range(pivots.shape[0]):
        rows = slice(tile * LANES, (tile + 1) * LANES)
        scale = jnp.broadcast_to(pivots[tile : tile + 1, :], (LANES, LANES)).T
        scale = jnp.concatenate([scale] * (width // LANES), axis=1)
        z_ref[rows, :] = (scale * part_ref[rows, :]).astype(BF16)
    relay_low_ref[...] = dot_nn(far_ref[:half, :], z_ref[...]).astype(BF16)
    relay_high_ref[...] = dot_nn(far_ref[half:, :], z_ref[...]).astype(BF16)


def near_body(own_ref, x_ref, y_ref, z_0_ref, z_1_ref, x_low_ref, y_high_ref, x_high_ref, y_low_ref, out_ref, z_ref):
    half, split = x_low_ref.shape[0], z_0_ref.shape[1]
    z_ref[:, :split] = z_0_ref[...]
    z_ref[:, split:] = z_1_ref[...]
    x_low_ref[...] = dot_nn(x_ref[:half, :], z_ref[...]).astype(BF16)
    y_high_ref[...] = dot_nn(y_ref[half:, :], z_ref[...]).astype(BF16)
    x_high_ref[...] = dot_nn(x_ref[half:, :], z_ref[...])
    y_low_ref[...] = dot_nn(y_ref[:half, :], z_ref[...])
    out_ref[...] = dot_nn(own_ref[...], z_ref[...])


def add_body(near_ref, relay_0_ref, relay_1_ref, out_0_ref, out_1_ref):
    relay = jnp.concatenate([relay_0_ref[...], relay_1_ref[...]], axis=1).astype(F32)
    total = (near_ref[...] + relay).astype(BF16)
    split = out_0_ref.shape[1]
    out_0_ref[...] = total[:, :split]
    out_1_ref[...] = total[:, split:]


def base_body(own_ref, link_ref, mine_ref, x_ref, y_ref, d_ref, x_low_ref, y_high_ref, out_0_ref, out_1_ref, first_ref):
    half = x_low_ref.shape[0]
    me = lax.axis_index("grp")
    for mask, ref in enumerate((mine_ref, x_ref, y_ref, d_ref)):
        lanes = pl.ds(pl.multiple_of((me ^ mask) * LANES, LANES), LANES)
        first_ref[:, lanes] = ref[...]
    start = 0
    for ref in (out_0_ref, out_1_ref):
        cols = slice(start, start + ref.shape[1])
        start += ref.shape[1]
        ref[...] = own_ref[:, cols] - dot_tn(link_ref[...], first_ref[:, cols])
        ref[:half, :] += x_low_ref[:, cols].astype(F32)
        ref[half:, :] += y_high_ref[:, cols].astype(F32)


def last_body(base_ref, low_ref, high_ref, out_ref):
    block = out_ref.shape[0]
    step = pl.program_id(0)
    per_half = low_ref.shape[0] // block
    rows = pl.ds(pl.multiple_of(step * block, block), block)
    part = pl.ds(pl.multiple_of(step % per_half * block, block), block)

    @pl.when(step < per_half)
    def _():
        out_ref[...] = base_ref[rows, :] + low_ref[part, :].astype(F32)

    @pl.when(step >= per_half)
    def _():
        out_ref[...] = base_ref[rows, :] + high_ref[part, :].astype(F32)


def local_pairs(leaf_rhs, leaf_inv, ordering, leaf_dinv, leaf_link, sep_rhs, sep_factor, sep_dinv):
    rows, width = leaf_rhs.shape
    half, split, quarter = rows // 2, rows // 16 * 7, width // 4
    group = lax.axis_size("grp")
    levels, slice_width, sep_block = sep_rhs.shape
    first = leaf_link.shape[1]
    fac_rows, cols = sep_factor.shape
    tiles = sep_block // fac_rows
    parts = range(2)
    me = lax.axis_index("grp").astype(jnp.int32)
    link_turned = leaf_link.T

    def bf16(height, breadth):
        return jax.ShapeDtypeStruct((height, breadth), BF16)

    def f32(height, breadth):
        return jax.ShapeDtypeStruct((height, breadth), F32)

    x_all = exchange(leaf_rhs, "grp", 1)
    low, high = call(
        split_body,
        (pltpu.with_memory_space_constraint(leaf_rhs, pltpu.HBM),),
        [pl.BlockSpec(memory_space=pltpu.HBM)],
        (bf16(split, width), bf16(rows - split, width)),
        scratch_shapes=[pltpu.SemaphoreType.DMA((2,))],
    )
    y_high = exchange(high, "grp", 2)
    y_low = exchange(low, "grp", 2)
    dest = (ordering[0] // rows ^ me) * rows + ordering[0] % rows
    blocks = arrange(leaf_inv, dest, group)

    aux = call(
        pack_body,
        (low, high, link_turned, sep_factor),
        [vmem()] * 4,
        [bf16(first + sep_block, LANES)] * group,
        after=(blocks[0],),
        scratch_shapes=[pltpu.VMEM((first, width), F32)],
    )
    high_cut = call(cut_body, (y_high,), [vmem()], [bf16(rows - split, width // 2)] * 2, after=(blocks[0],))
    d_high = [exchange(high_cut[part], "grp", 1) for part in parts]
    low_cut = call(cut_body, (x_all,), [vmem()], [bf16(split, width // 2)] * 2, after=(blocks[0],))
    d_low = [exchange(low_cut[part], "grp", 2) for part in parts]
    aux_parts = [aux[0]] + [exchange(aux[mask], "grp", mask) for mask in range(1, group)]

    part_y = call(
        forward_body,
        (*blocks[:3], low, high, x_all, y_low, y_high),
        [vmem()] * 8,
        [f32(rows, width // 2)] * 2,
        scratch_shapes=[pltpu.VMEM((3 * rows, rows), BF16), pltpu.VMEM((3 * rows, width), BF16)],
    )
    leaf_z, relay_low, relay_high = [], [], []
    for part in parts:
        z_part, far_low, far_high = call(
            far_body,
            (blocks[3], d_low[part], d_high[part], part_y[part], leaf_dinv.reshape(-1, LANES)),
            [vmem()] * 5,
            (bf16(rows, width // 2), bf16(half, width // 2), bf16(half, width // 2)),
            scratch_shapes=[pltpu.VMEM((rows, width // 2), BF16), pltpu.VMEM((rows, width // 2), F32)],
        )
        leaf_z.append(z_part)
        relay_low.append(exchange(far_low, "grp", 1))
        relay_high.append(exchange(far_high, "grp", 2))

    leaf_block = call(
        functools.partial(leaf_body, rows=fac_rows, cols=cols),
        (*aux_parts, jnp.swapaxes(sep_rhs, 1, 2), sep_dinv),
        [vmem()] * 6,
        bf16(first + (levels + tiles) * sep_block, LANES),
        after=(leaf_z[1],),
    )
    partner = exchange(leaf_block, "leaf", 1)
    near_x_low, near_y_high, near_x_high, near_y_low, own = call(
        near_body,
        (*blocks[:3], *leaf_z),
        [vmem()] * 5,
        [bf16(half, width)] * 2 + [f32(half, width)] * 2 + [f32(rows, width)],
        after=(leaf_block,),
        scratch_shapes=[pltpu.VMEM((rows, width), BF16)],
    )
    sum_x_low = exchange(near_x_low, "grp", 1)
    sum_y_high = exchange(near_y_high, "grp", 2)
    pair_block = call(
        functools.partial(pair_body, first=first, sep_block=sep_block),
        (leaf_block, partner),
        [vmem(), vmem()],
        bf16((levels + tiles) * first, LANES),
        after=(own,),
    )
    count = lax.axis_size("leaf") // 2
    pairs = [pair_block] + [exchange(pair_block, "leaf", 2 * mask) for mask in range(1, count)]
    nsep = count * first
    first_here, sep_turned = call(
        functools.partial(
            tree_body, count=count, first=first, levels=levels, sep_block=sep_block, cols=cols
        ),
        pairs,
        [vmem()] * count,
        (bf16(first, LANES), jax.ShapeDtypeStruct((levels, sep_block, slice_width), F32)),
        scratch_shapes=[
            pltpu.VMEM((levels, nsep, LANES), BF16),
            pltpu.VMEM((nsep, tiles * LANES), BF16),
            pltpu.VMEM((nsep, LANES), F32),
        ],
    )
    first_all = [first_here] + [exchange(first_here, "grp", mask) for mask in range(1, group)]
    breadths = (width - quarter, quarter)
    into = [bf16(half, breadth) for breadth in breadths]
    x_sums = call(add_body, (near_x_high, *relay_high), [vmem()] * 3, into)
    y_sums = call(add_body, (near_y_low, *relay_low), [vmem()] * 3, into)
    sum_x_high = [exchange(x_sums[part], "grp", 1) for part in parts]
    sum_y_low = [exchange(y_sums[part], "grp", 2) for part in parts]
    base = call(
        base_body,
        (own, link_turned, *first_all, sum_x_low, sum_y_high),
        [vmem()] * (4 + group),
        [f32(rows, breadth) for breadth in breadths],
        scratch_shapes=[pltpu.VMEM((first, width), BF16)],
    )
    block = rows // 4
    leaf_x = ()
    for part, start in zip(parts, (0, breadths[0] // breadths[1])):
        leaf_x = (
            call(
                last_body,
                (base[part], sum_y_low[part], sum_x_high[part]),
                [vmem()] * 3,
                f32(rows, width),
                after=leaf_x,
                grid=(rows // block,),
                out_specs=pl.BlockSpec((block, breadths[part]), lambda step, start=start: (step, start)),
                input_output_aliases={0: 0} if leaf_x else {},
            ),
        )
    return leaf_x[0], jnp.swapaxes(sep_turned, 1, 2)


def fits(leaf_rhs, leaf_inv, sep_rhs, sep_factor, leaf_link):
    levels, slice_width, sep_block = sep_rhs.shape
    width = leaf_rhs.shape[1]
    count = lax.axis_size("grp")
    leaves = lax.axis_size("leaf")
    return (
        count == 2**2
        and leaf_inv.shape[1] == count * leaf_rhs.shape[0]
        and leaf_rhs.shape[0] % 256 == 0
        and leaf_rhs.shape[0] // LANES == 8
        and leaf_link.shape[1] == 2 * sep_block
        and sep_block % 16 == 0
        and slice_width % 128 == 0
        and sep_block % sep_factor.shape[0] == 0
        and sep_factor.shape[1] + levels <= sep_block // sep_factor.shape[0] * LANES
        and width == count * slice_width
        and slice_width == LANES
        and width % (leaves * sep_block) == 0
    )


def local(*args):
    leaf_rhs, leaf_inv, _, _, leaf_link, sep_rhs, sep_factor, _ = args
    if fits(leaf_rhs, leaf_inv, sep_rhs, sep_factor, leaf_link):
        return local_pairs(*args)
    return local_general(*args)


def solution(mesh):
    placed = (
        P(("leaf", "grp"), None),
        P(("leaf", "grp"), None),
        P("leaf", None),
        P(("leaf", "grp")),
        P(("leaf", "grp"), None),
        P(None, "grp", "leaf"),
        P(("leaf", "grp"), None),
        P(None, "leaf"),
    )
    return jax.shard_map(
        local,
        mesh=mesh,
        in_specs=placed,
        out_specs=(P(("leaf", "grp"), None), P(None, "grp", "leaf")),
        check_vma=False,
    )
```

```python
import functools
import math

import jax
import jax.numpy as jnp
from jax import lax
from jax.experimental import pallas as pl
from jax.experimental.pallas import tpu as pltpu
from jax.sharding import PartitionSpec as P


F32 = jnp.float32
BF16 = jnp.bfloat16
LANES = 128
UNROLL = 32


def exchange(block, axis, mask):
    count = lax.axis_size(axis)
    return lax.ppermute(block, axis, [(low, low ^ mask) for low in range(count)])


def level_offset(sep_block, tree_level):
    if tree_level >= 2:
        return sep_block * (2 ** (tree_level + 1) - 6)
    return 0


def dot_tn(lhs, rhs):
    return lax.dot_general(lhs, rhs, (((0,), (0,)), ((), ())), preferred_element_type=F32)


def dot_nn(lhs, rhs):
    return jnp.dot(lhs, rhs, preferred_element_type=F32)


def vmem():
    return pl.BlockSpec(memory_space=pltpu.VMEM)


def smem():
    return pl.BlockSpec(memory_space=pltpu.SMEM)


def call(body, ops, specs, out_shape, after=(), grant=16, **rest):
    skip = len(after)
    rest.setdefault("out_specs", jax.tree.map(lambda _: vmem(), out_shape))

    def skipping(*refs):
        body(*refs[skip:])

    return pl.pallas_call(
        skipping,
        out_shape=out_shape,
        in_specs=[pl.BlockSpec(memory_space=pl.ANY)] * skip + specs,
        compiler_params=pltpu.CompilerParams(vmem_limit_bytes=grant * 2**20),
        **rest,
    )(*after, *ops)


def from_partner(block, axis, distance):
    count = lax.axis_size(axis)
    route = []
    for low in range(count):
        high = low | 1 << distance
        if high != low and high < count:
            route += [(low, high), (high, low)]
    return lax.ppermute(block, axis, route)


def partner(values, level_bit):
    return from_partner(values.astype(jnp.bfloat16), "leaf", level_bit).astype(values.dtype)


def leaf_bit(level_bit):
    return jnp.right_shift(lax.axis_index("leaf"), level_bit) % 2


def spread(values, first_bit, last_bit):
    for level_bit in range(first_bit, last_bit):
        partner_rows = partner(values.astype(jnp.float32), level_bit).astype(jnp.bfloat16)
        low_first = jnp.concatenate([values, partner_rows], axis=-1)
        high_first = jnp.concatenate([partner_rows, values], axis=-1)
        values = jnp.where(leaf_bit(level_bit) == 0, low_first, high_first)
    return values


def halve_sum(values, bit_list):
    for level_bit in bit_list:
        half_width = values.shape[-1] // 2
        low_half = values[..., :half_width]
        high_half = values[..., half_width:]
        is_upper = leaf_bit(level_bit) == 1
        keep_half = jnp.where(is_upper, high_half, low_half)
        send_half = jnp.where(is_upper, low_half, high_half)
        values = keep_half + partner(send_half, level_bit)
    return values


def group_rows(values):
    return lax.all_gather(values, "grp", axis=0, tiled=True)


def level_width(sep_block, tree_level):
    if tree_level >= 2:
        return 2 * sep_block * 2**tree_level
    return sep_block * 2**tree_level


def local_general(leaf_rhs, leaf_inv, ordering, leaf_dinv, leaf_link, sep_rhs, sep_factor, sep_dinv):
    levels = sep_rhs.shape[0]
    sep_block = sep_rhs.shape[2]
    inverse = jnp.argsort(ordering[0])
    picked = jnp.take(leaf_inv, inverse, axis=1)
    leaf_y = jnp.dot(
        picked,
        lax.all_gather(leaf_rhs, "grp", axis=0, tiled=True),
        preferred_element_type=jnp.float32,
    )
    partial_sum = jnp.einsum("rk,rc->kc", leaf_rhs, leaf_link, preferred_element_type=jnp.float32)
    crossing = lax.psum_scatter(
        partial_sum.astype(jnp.bfloat16), "grp", scatter_dimension=0, tiled=True
    ).astype(jnp.float32)
    leaf_z = (leaf_dinv.astype(jnp.float32)[:, None] * leaf_y).astype(jnp.bfloat16)
    crossing = halve_sum(crossing, [0])
    sep_r = (sep_rhs[0].astype(jnp.float32) - crossing).astype(jnp.bfloat16)
    gathered = group_rows(sep_factor)

    def level_rows(tree_level):
        offset = level_offset(sep_block, tree_level)
        return lax.slice_in_dim(
            gathered, offset, offset + level_width(sep_block, tree_level), axis=1
        )

    z_blocks = []
    full_prev = sep_r
    for tree_level in range(1, levels + 1):
        rows_here = level_rows(tree_level)
        size_here = sep_block * 2**tree_level
        if tree_level >= 2:
            children = spread(full_prev, tree_level - 1, tree_level)
            link_rows = rows_here[:, size_here:]
            coupled = jnp.einsum(
                "kc,qc->kq", children, link_rows, preferred_element_type=jnp.float32
            )
            sep_r = (sep_rhs[tree_level - 1].astype(jnp.float32) - coupled).astype(jnp.bfloat16)
        full_prev = spread(sep_r, 0, tree_level)
        sep_y = jnp.einsum(
            "kc,qc->kq", full_prev, rows_here[:, :size_here], preferred_element_type=jnp.float32
        )
        z_blocks.append(
            (sep_dinv[tree_level - 1].astype(jnp.float32)[None, :] * sep_y).astype(jnp.bfloat16)
        )
    solution = [None] * levels
    upper_rows = level_rows(levels)
    size_top = sep_block * 2**levels
    partial_value = jnp.einsum(
        "kq,qc->kc",
        z_blocks[levels - 1],
        upper_rows[:, :size_top],
        preferred_element_type=jnp.float32,
    )
    current = halve_sum(partial_value, list(range(levels - 1, -1, -1)))
    solution[levels - 1] = current
    for tree_level in range(levels - 1, 0, -1):
        size_here = sep_block * 2**tree_level
        link_rows = upper_rows[:, 2 * size_here :]
        rows_here = level_rows(tree_level)
        pushed = -jnp.einsum(
            "kq,qc->kc", current.astype(jnp.bfloat16), link_rows, preferred_element_type=jnp.float32
        )
        pushed = halve_sum(pushed, [tree_level])
        pushed = pushed + jnp.einsum(
            "kq,qc->kc",
            z_blocks[tree_level - 1],
            rows_here[:, :size_here],
            preferred_element_type=jnp.float32,
        )
        current = halve_sum(pushed, list(range(tree_level - 1, -1, -1)))
        solution[tree_level - 1] = current
        upper_rows = rows_here
    first_full = spread(current.astype(jnp.bfloat16), 0, 1)
    first_all = group_rows(first_full)
    picked = jnp.take(leaf_inv, inverse, axis=1)
    leaf_x = lax.psum_scatter(
        jnp.einsum("rm,rk->mk", picked, leaf_z, preferred_element_type=jnp.float32).astype(
            jnp.bfloat16
        ),
        "grp",
        scatter_dimension=0,
        tiled=True,
    ).astype(jnp.float32)
    leaf_x = leaf_x - jnp.einsum(
        "rc,kc->rk", leaf_link, first_all, preferred_element_type=jnp.float32
    )
    return (leaf_x, jnp.stack(solution, axis=0))


def send_body(whole_ref, low_ref, high_ref, link_ref, fac_ref, out_0_ref, out_1_ref, kept_ref, crossing_ref):
    height, width = out_1_ref.shape
    out_0_ref[:height, :] = whole_ref[:, :width]
    out_1_ref[...] = whole_ref[:, width:]
    first = link_ref.shape[0]
    rows, cols = fac_ref.shape
    split = low_ref.shape[0]
    crossing = dot_nn(link_ref[:, :split], low_ref[...]) + dot_nn(link_ref[:, split:], high_ref[...])
    crossing_ref[...] = crossing
    tiles = (kept_ref.shape[0] - first) // rows
    factor = fac_ref[...].astype(F32)
    factor = jnp.concatenate([factor, jnp.zeros((rows, tiles * LANES - cols), F32)], axis=1)
    folded = [factor[:, tile * LANES : (tile + 1) * LANES] for tile in range(tiles)]
    folded = jnp.concatenate(folded, axis=0)
    me = lax.axis_index("grp")
    kept_ref[first:, :] = jnp.concatenate([folded, folded], axis=1)
    out_0_ref[height + first :, :] = jnp.concatenate([folded, folded], axis=1).astype(BF16)
    for index, (mine, sent) in enumerate(((0, 1), (2, 3))):
        place = slice(index * LANES, (index + 1) * LANES)
        lanes = pl.ds(pl.multiple_of((me ^ mine) * LANES, LANES), LANES)
        kept_ref[:first, place] = crossing_ref[:, lanes]
        lanes = pl.ds(pl.multiple_of((me ^ sent) * LANES, LANES), LANES)
        out_0_ref[height : height + first, place] = crossing_ref[:, lanes].astype(BF16)


def leaf_body(kept_ref, x_ref, y_ref, sep_ref, dinv_ref, out_ref, *, rows, cols):
    levels, sep_block, _ = sep_ref.shape
    first = kept_ref.shape[0] - sep_block
    tiles = sep_block // rows
    me = lax.axis_index("grp")
    x_part = x_ref[x_ref.shape[0] - first - sep_block :, :].astype(F32)
    y_part = y_ref[y_ref.shape[0] - first :, :].astype(F32)
    total = kept_ref[:first, :LANES] + x_part[:first, :LANES] + y_part[:, :LANES]
    out_ref[:first, :] = total.astype(BF16)
    for level in range(levels):
        out_ref[first + level * sep_block : first + (level + 1) * sep_block, :] = sep_ref[level]
    row_owner = lax.broadcasted_iota(jnp.int32, (sep_block, tiles * LANES), 0) // rows
    lane = lax.broadcasted_iota(jnp.int32, (sep_block, tiles * LANES), 1)
    factor = jnp.zeros((sep_block, tiles * LANES), F32)
    folds = (
        kept_ref[first:, :LANES],
        x_part[first:, :LANES],
        y_part[:sep_block, LANES:],
        y_part[sep_block : 2 * sep_block, LANES:],
    )
    for index, folded in enumerate(folds):
        block = [folded[tile * rows : (tile + 1) * rows, :] for tile in range(tiles)]
        block = jnp.concatenate(block, axis=1)
        tiled = jnp.concatenate([block] * (sep_block // rows), axis=0)
        factor = factor + jnp.where(row_owner == (me ^ index), tiled, 0.0)
    pivots = dinv_ref[...].astype(F32).T
    for level in range(levels):
        column = jnp.broadcast_to(pivots[:, level : level + 1], factor.shape)
        factor = jnp.where(lane == cols + level, column, factor)
    base = first + levels * sep_block
    for tile in range(tiles):
        out_ref[base + tile * sep_block : base + (tile + 1) * sep_block, :] = factor[
            :, tile * LANES : (tile + 1) * LANES
        ].astype(BF16)


def pair_body(own_ref, other_ref, out_ref, *, first, sep_block):
    is_odd = lax.axis_index("leaf") % 2 == 1
    own = own_ref[...].astype(F32)
    other = other_ref[...].astype(F32)
    even = jnp.where(is_odd, other, own)
    odd = jnp.where(is_odd, own, other)
    crossing = even[0:first] + odd[0:first]
    for index in range((own.shape[0] - first) // sep_block):
        base = first + index * sep_block
        both = jnp.concatenate([even[base : base + sep_block], odd[base : base + sep_block]], axis=0)
        if index == 0:
            both = both - crossing
        out_ref[index * first : (index + 1) * first, :] = both.astype(BF16)


def tree_body(*refs, count, first, levels, sep_block, cols):
    pairs = refs[:count]
    first_ref, sol_ref, stage_ref, factor_ref, val_ref = refs[count:]
    leaf = lax.axis_index("leaf")
    pair = leaf // 2
    nsep, width = factor_ref.shape
    for index, ref in enumerate(pairs):
        place = pl.ds(pl.multiple_of((pair ^ index) * first, first), first)
        for level in range(levels):
            stage_ref[level, place, :] = ref[level * first : (level + 1) * first, :]
        for tile in range(width // LANES):
            base = (levels + tile) * first
            factor_ref[place, tile * LANES : (tile + 1) * LANES] = ref[base : base + first, :]
    factor = factor_ref[...]
    column = lax.broadcasted_iota(jnp.int32, (width, nsep), 0)
    target = lax.broadcasted_iota(jnp.int32, (width, nsep), 1)
    row = lax.broadcasted_iota(jnp.int32, (nsep, nsep), 0)
    lane = lax.broadcasted_iota(jnp.int32, (nsep, nsep), 1)

    def block_diagonal(offset, size):
        choose = jnp.where(column == offset + target % size, 1.0, 0.0).astype(BF16)
        spread = dot_nn(factor, choose)
        return jnp.where(row // size == lane // size, spread, 0.0).astype(BF16)

    weights, couplings, z_blocks = [], [], []
    residual = stage_ref[0]
    for level in range(1, levels + 1):
        size = sep_block * 2**level
        offset = level_offset(sep_block, level)
        weight = block_diagonal(offset, size)
        coupling = None
        if level >= 2:
            coupling = block_diagonal(offset + size, size)
            residual = (stage_ref[level - 1].astype(F32) - dot_nn(coupling, residual)).astype(BF16)
        pick = lax.broadcasted_iota(jnp.int32, (width, LANES), 0) == cols + level - 1
        scale = dot_nn(factor, jnp.where(pick, 1.0, 0.0).astype(BF16))
        z_blocks.append((scale * dot_nn(weight, residual)).astype(BF16))
        weights.append(weight)
        couplings.append(coupling)
    current = None
    for level in range(levels, 0, -1):
        value = dot_tn(weights[level - 1], z_blocks[level - 1])
        if level < levels:
            value = value - dot_tn(couplings[level], current.astype(BF16))
        current = value
        val_ref[...] = value
        sol_ref[level - 1] = val_ref[pl.ds(pl.multiple_of(leaf * sep_block, sep_block), sep_block), :]
    first_ref[...] = val_ref[pl.ds(pl.multiple_of(pair * first, first), first), :].astype(BF16)


def arrange_body(dest_ref, factor_ref, *refs):
    outs, (turned_ref, sorted_ref) = refs[:-2], refs[-2:]
    step = pl.program_id(0)
    rows, width = factor_ref.shape
    tiles = rows // LANES
    turned = factor_ref[...].astype(F32).T
    for tile in range(tiles):
        turned_ref[pl.ds(tile, width, stride=tiles), :] = turned[:, tile * LANES : (tile + 1) * LANES]

    def move(group, carry):
        for lane in range(UNROLL):
            source = group * UNROLL + lane
            target = dest_ref[step * width + source]
            sorted_ref[pl.ds(pl.multiple_of(target * tiles, tiles), tiles), :] = turned_ref[
                pl.ds(pl.multiple_of(source * tiles, tiles), tiles), :
            ]
        return carry

    lax.fori_loop(0, width // UNROLL, move, 0)

    @pl.when(step == pl.num_programs(0) - 1)
    def _():
        for index, out_ref in enumerate(outs):
            count = out_ref.shape[0]
            chunk = min(count, 256)

            def write(part, carry, index=index, out_ref=out_ref, count=count, chunk=chunk):
                base = index * count * tiles + part * chunk * tiles
                for tile in range(tiles):
                    out_ref[
                        pl.ds(pl.multiple_of(part * chunk, chunk), chunk),
                        tile * LANES : (tile + 1) * LANES,
                    ] = sorted_ref[pl.ds(base + tile, chunk, stride=tiles), :].astype(BF16)
                return carry

            lax.fori_loop(0, count // chunk, write, 0)


def arrange(factor, dest, count):
    rows, cols = factor.shape
    width = math.gcd(cols, 4 * LANES)
    part = cols // count
    return call(
        arrange_body,
        (dest, pltpu.with_memory_space_constraint(factor, pltpu.HBM)),
        [smem(), pl.BlockSpec((rows, width), lambda step: (0, step))],
        [jax.ShapeDtypeStruct((part, rows), BF16)] * count,
        grant=26,
        grid=(cols // width,),
        scratch_shapes=[
            pltpu.VMEM((width * rows // LANES, LANES), F32),
            pltpu.VMEM((cols * rows // LANES, LANES), F32),
        ],
    )


def split_body(rhs_ref, low_ref, high_ref, sems):
    split = low_ref.shape[0]
    copies = [
        pltpu.make_async_copy(rhs_ref.at[pl.ds(index * split, ref.shape[0]), :], ref, sems.at[index])
        for index, ref in enumerate((low_ref, high_ref))
    ]
    for copy in copies:
        copy.start()
    for copy in copies:
        copy.wait()


def cut_body(whole_ref, *outs):
    for part, ref in enumerate(outs):
        height, width = ref.shape
        ref[...] = whole_ref[:height, part * width : (part + 1) * width]


def forward_body(own_ref, x_ref, y_ref, *refs):
    pieces, (out_0_ref, out_1_ref, factor_ref, loads_ref) = refs[:-4], refs[-4:]
    rows = own_ref.shape[0]
    width = out_0_ref.shape[1]
    for index, ref in enumerate((own_ref, x_ref, y_ref)):
        factor_ref[index * rows : (index + 1) * rows, :] = ref[...]
    start = 0
    for ref in pieces:
        loads_ref[start : start + ref.shape[0], :] = ref[...]
        start += ref.shape[0]
    out_0_ref[...] = dot_tn(factor_ref[...], loads_ref[:, :width])
    out_1_ref[...] = dot_tn(factor_ref[...], loads_ref[:, width:])


def far_body(far_ref, low_ref, high_ref, near_ref, dinv_ref, *refs, first):
    kept = refs[:-5]
    z_ref, relay_low_ref, relay_high_ref, loads_ref, part_ref = refs[-5:]
    split, half = low_ref.shape[0], relay_low_ref.shape[0]
    rest = loads_ref.shape[0] - split
    loads_ref[:split, :] = low_ref[...]
    loads_ref[split:, :] = high_ref[:rest, :]
    part_ref[...] = near_ref[...] + dot_tn(far_ref[...], loads_ref[...])
    pivots = dinv_ref[...].astype(F32)
    width = part_ref.shape[1]
    for tile in range(pivots.shape[0]):
        rows = slice(tile * LANES, (tile + 1) * LANES)
        scale = jnp.broadcast_to(pivots[tile : tile + 1, :], (LANES, LANES)).T
        scale = jnp.concatenate([scale] * (width // LANES), axis=1)
        z_ref[rows, :] = (scale * part_ref[rows, :]).astype(BF16)
    relay_low_ref[...] = dot_nn(far_ref[:half, :], z_ref[...]).astype(BF16)
    relay_high_ref[:half, :] = dot_nn(far_ref[half:, :], z_ref[...]).astype(BF16)
    for kept_ref in kept:
        crossing = kept_ref[:first, LANES:] + high_ref[rest : rest + first, LANES:].astype(F32)
        relay_high_ref[half:, :LANES] = crossing.astype(BF16)
        folds = [kept_ref[first:, LANES:], high_ref[rest + first :, :LANES].astype(F32)]
        relay_high_ref[half:, LANES:] = jnp.concatenate(folds, axis=0).astype(BF16)


def near_body(own_ref, x_ref, y_ref, z_0_ref, z_1_ref, x_low_ref, y_high_ref, x_high_ref, y_low_ref, out_ref, z_ref):
    half, split = x_low_ref.shape[0], z_0_ref.shape[1]
    z_ref[:, :split] = z_0_ref[...]
    z_ref[:, split:] = z_1_ref[...]
    x_low_ref[...] = dot_nn(x_ref[:half, :], z_ref[...]).astype(BF16)
    y_high_ref[...] = dot_nn(y_ref[half:, :], z_ref[...]).astype(BF16)
    x_high_ref[...] = dot_nn(x_ref[half:, :], z_ref[...])
    y_low_ref[...] = dot_nn(y_ref[:half, :], z_ref[...])
    out_ref[...] = dot_nn(own_ref[...], z_ref[...])


def add_body(near_ref, relay_0_ref, relay_1_ref, out_0_ref, out_1_ref):
    half = near_ref.shape[0]
    relay = jnp.concatenate([relay_0_ref[:half, :], relay_1_ref[:half, :]], axis=1).astype(F32)
    total = (near_ref[...] + relay).astype(BF16)
    split = out_0_ref.shape[1]
    out_0_ref[...] = total[:, :split]
    out_1_ref[...] = total[:, split:]


def base_body(own_ref, link_ref, mine_ref, x_ref, y_ref, d_ref, x_low_ref, y_high_ref, out_0_ref, out_1_ref, first_ref):
    half = x_low_ref.shape[0]
    me = lax.axis_index("grp")
    for mask, ref in enumerate((mine_ref, x_ref, y_ref, d_ref)):
        lanes = pl.ds(pl.multiple_of((me ^ mask) * LANES, LANES), LANES)
        first_ref[:, lanes] = ref[...]
    start = 0
    for ref in (out_0_ref, out_1_ref):
        cols = slice(start, start + ref.shape[1])
        start += ref.shape[1]
        ref[...] = own_ref[:, cols] - dot_tn(link_ref[...], first_ref[:, cols])
        ref[:half, :] += x_low_ref[:, cols].astype(F32)
        ref[half:, :] += y_high_ref[:, cols].astype(F32)


def last_body(base_ref, low_ref, high_ref, out_ref):
    block = out_ref.shape[0]
    step = pl.program_id(0)
    per_half = low_ref.shape[0] // block
    rows = pl.ds(pl.multiple_of(step * block, block), block)
    part = pl.ds(pl.multiple_of(step % per_half * block, block), block)

    @pl.when(step < per_half)
    def _():
        out_ref[...] = base_ref[rows, :] + low_ref[part, :].astype(F32)

    @pl.when(step >= per_half)
    def _():
        out_ref[...] = base_ref[rows, :] + high_ref[part, :].astype(F32)


def local_pairs(leaf_rhs, leaf_inv, ordering, leaf_dinv, leaf_link, sep_rhs, sep_factor, sep_dinv):
    rows, width = leaf_rhs.shape
    half, split = rows // 2, rows // 16 * 7
    group = lax.axis_size("grp")
    levels, slice_width, sep_block = sep_rhs.shape
    first = leaf_link.shape[1]
    fac_rows, cols = sep_factor.shape
    tiles = sep_block // fac_rows
    parts = range(2)
    me = lax.axis_index("grp").astype(jnp.int32)
    link_turned = leaf_link.T

    def bf16(height, breadth):
        return jax.ShapeDtypeStruct((height, breadth), BF16)

    def f32(height, breadth):
        return jax.ShapeDtypeStruct((height, breadth), F32)

    x_all = exchange(leaf_rhs, "grp", 1)
    low, high = call(
        split_body,
        (pltpu.with_memory_space_constraint(leaf_rhs, pltpu.HBM),),
        [pl.BlockSpec(memory_space=pltpu.HBM)],
        (bf16(split, width), bf16(rows - split, width)),
        scratch_shapes=[pltpu.SemaphoreType.DMA((2,))],
    )
    y_high = exchange(high, "grp", 2)
    y_low = exchange(low, "grp", 2)
    dest = (ordering[0] // rows ^ me) * rows + ordering[0] % rows
    blocks = arrange(leaf_inv, dest, group)

    *high_cut, kept = call(
        send_body,
        (y_high, low, high, link_turned, sep_factor),
        [vmem()] * 5,
        [
            bf16(rows - split + first + sep_block, width // 2),
            bf16(rows - split, width // 2),
            f32(first + sep_block, 2 * LANES),
        ],
        after=(blocks[0],),
        scratch_shapes=[pltpu.VMEM((first, width), F32)],
    )
    d_high = [exchange(high_cut[part], "grp", 1) for part in parts]
    low_cut = call(cut_body, (x_all,), [vmem()], [bf16(split, width // 2)] * 2, after=(blocks[0],))
    d_low = [exchange(low_cut[part], "grp", 2) for part in parts]

    part_y = call(
        forward_body,
        (*blocks[:3], low, high, x_all, y_low, y_high),
        [vmem()] * 8,
        [f32(rows, width // 2)] * 2,
        scratch_shapes=[pltpu.VMEM((3 * rows, rows), BF16), pltpu.VMEM((3 * rows, width), BF16)],
    )
    leaf_z, relay_low, relay_high = [], [], []
    for part in parts:
        shared = (kept,) if part == 0 else ()
        z_part, far_low, far_high = call(
            functools.partial(far_body, first=first),
            (blocks[3], d_low[part], d_high[part], part_y[part], leaf_dinv.reshape(-1, LANES), *shared),
            [vmem()] * (5 + len(shared)),
            (
                bf16(rows, width // 2),
                bf16(half, width // 2),
                bf16(half + first * len(shared), width // 2),
            ),
            scratch_shapes=[pltpu.VMEM((rows, width // 2), BF16), pltpu.VMEM((rows, width // 2), F32)],
        )
        leaf_z.append(z_part)
        relay_low.append(exchange(far_low, "grp", 1))
        relay_high.append(exchange(far_high, "grp", 2))

    near_x_low, near_y_high, near_x_high, near_y_low, own = call(
        near_body,
        (*blocks[:3], *leaf_z),
        [vmem()] * 5,
        [bf16(half, width)] * 2 + [f32(half, width)] * 2 + [f32(rows, width)],
        scratch_shapes=[pltpu.VMEM((rows, width), BF16)],
    )
    leaf_block = call(
        functools.partial(leaf_body, rows=fac_rows, cols=cols),
        (kept, d_high[0], relay_high[0], jnp.swapaxes(sep_rhs, 1, 2), sep_dinv),
        [vmem()] * 5,
        bf16(first + (levels + tiles) * sep_block, LANES),
        after=(own,),
    )
    partner = exchange(leaf_block, "leaf", 1)
    sum_x_low = exchange(near_x_low, "grp", 1)
    sum_y_high = exchange(near_y_high, "grp", 2)
    pair_block = call(
        functools.partial(pair_body, first=first, sep_block=sep_block),
        (leaf_block, partner),
        [vmem(), vmem()],
        bf16((levels + tiles) * first, LANES),
    )
    count = lax.axis_size("leaf") // 2
    pairs = [pair_block] + [exchange(pair_block, "leaf", 2 * mask) for mask in range(1, count)]
    nsep = count * first
    first_here, sep_turned = call(
        functools.partial(
            tree_body, count=count, first=first, levels=levels, sep_block=sep_block, cols=cols
        ),
        pairs,
        [vmem()] * count,
        (bf16(first, LANES), jax.ShapeDtypeStruct((levels, sep_block, slice_width), F32)),
        scratch_shapes=[
            pltpu.VMEM((levels, nsep, LANES), BF16),
            pltpu.VMEM((nsep, tiles * LANES), BF16),
            pltpu.VMEM((nsep, LANES), F32),
        ],
    )
    first_all = [first_here] + [exchange(first_here, "grp", mask) for mask in range(1, group)]
    breadths = (width // 2, width // 2)
    into = [bf16(half, breadth) for breadth in breadths]
    x_sums = call(add_body, (near_x_high, *relay_high), [vmem()] * 3, into)
    y_sums = call(add_body, (near_y_low, *relay_low), [vmem()] * 3, into)
    sum_x_high = [exchange(x_sums[part], "grp", 1) for part in parts]
    sum_y_low = [exchange(y_sums[part], "grp", 2) for part in parts]
    base = call(
        base_body,
        (own, link_turned, *first_all, sum_x_low, sum_y_high),
        [vmem()] * (4 + group),
        [f32(rows, breadth) for breadth in breadths],
        scratch_shapes=[pltpu.VMEM((first, width), BF16)],
    )
    block = rows // 4
    leaf_x = ()
    for part, start in zip(parts, (0, breadths[0] // breadths[1])):
        leaf_x = (
            call(
                last_body,
                (base[part], sum_y_low[part], sum_x_high[part]),
                [vmem()] * 3,
                f32(rows, width),
                after=leaf_x,
                grid=(rows // block,),
                out_specs=pl.BlockSpec((block, breadths[part]), lambda step, start=start: (step, start)),
                input_output_aliases={0: 0} if leaf_x else {},
            ),
        )
    return leaf_x[0], jnp.swapaxes(sep_turned, 1, 2)


def fits(leaf_rhs, leaf_inv, sep_rhs, sep_factor, leaf_link):
    levels, slice_width, sep_block = sep_rhs.shape
    width = leaf_rhs.shape[1]
    count = lax.axis_size("grp")
    leaves = lax.axis_size("leaf")
    return (
        count == 2**2
        and leaf_inv.shape[1] == count * leaf_rhs.shape[0]
        and leaf_rhs.shape[0] % 256 == 0
        and leaf_rhs.shape[0] // LANES == 8
        and leaf_link.shape[1] == 2 * sep_block
        and sep_block % 16 == 0
        and slice_width % 128 == 0
        and sep_block % sep_factor.shape[0] == 0
        and sep_factor.shape[1] + levels <= sep_block // sep_factor.shape[0] * LANES
        and width == count * slice_width
        and slice_width == LANES
        and width % (leaves * sep_block) == 0
    )


def local(*args):
    leaf_rhs, leaf_inv, _, _, leaf_link, sep_rhs, sep_factor, _ = args
    if fits(leaf_rhs, leaf_inv, sep_rhs, sep_factor, leaf_link):
        return local_pairs(*args)
    return local_general(*args)


def solution(mesh):
    placed = (
        P(("leaf", "grp"), None),
        P(("leaf", "grp"), None),
        P("leaf", None),
        P(("leaf", "grp")),
        P(("leaf", "grp"), None),
        P(None, "grp", "leaf"),
        P(("leaf", "grp"), None),
        P(None, "leaf"),
    )
    return jax.shard_map(
        local,
        mesh=mesh,
        in_specs=placed,
        out_specs=(P(("leaf", "grp"), None), P(None, "grp", "leaf")),
        check_vma=False,
    )
```

```python
import functools
import math

import jax
import jax.numpy as jnp
from jax import lax
from jax.experimental import pallas as pl
from jax.experimental.pallas import tpu as pltpu
from jax.sharding import PartitionSpec as P


F32 = jnp.float32
BF16 = jnp.bfloat16
LANES = 128
UNROLL = 32


def exchange(block, axis, mask):
    count = lax.axis_size(axis)
    return lax.ppermute(block, axis, [(low, low ^ mask) for low in range(count)])


def level_offset(sep_block, tree_level):
    if tree_level >= 2:
        return sep_block * (2 ** (tree_level + 1) - 6)
    return 0


def dot_tn(lhs, rhs):
    return lax.dot_general(lhs, rhs, (((0,), (0,)), ((), ())), preferred_element_type=F32)


def dot_nn(lhs, rhs):
    return jnp.dot(lhs, rhs, preferred_element_type=F32)


def vmem():
    return pl.BlockSpec(memory_space=pltpu.VMEM)


def smem():
    return pl.BlockSpec(memory_space=pltpu.SMEM)


def call(body, ops, specs, out_shape, after=(), grant=16, **rest):
    skip = len(after)
    rest.setdefault("out_specs", jax.tree.map(lambda _: vmem(), out_shape))

    def skipping(*refs):
        body(*refs[skip:])

    return pl.pallas_call(
        skipping,
        out_shape=out_shape,
        in_specs=[pl.BlockSpec(memory_space=pl.ANY)] * skip + specs,
        compiler_params=pltpu.CompilerParams(vmem_limit_bytes=grant * 2**20),
        **rest,
    )(*after, *ops)


def from_partner(block, axis, distance):
    count = lax.axis_size(axis)
    route = []
    for low in range(count):
        high = low | 1 << distance
        if high != low and high < count:
            route += [(low, high), (high, low)]
    return lax.ppermute(block, axis, route)


def partner(values, level_bit):
    return from_partner(values.astype(jnp.bfloat16), "leaf", level_bit).astype(values.dtype)


def leaf_bit(level_bit):
    return jnp.right_shift(lax.axis_index("leaf"), level_bit) % 2


def spread(values, first_bit, last_bit):
    for level_bit in range(first_bit, last_bit):
        partner_rows = partner(values.astype(jnp.float32), level_bit).astype(jnp.bfloat16)
        low_first = jnp.concatenate([values, partner_rows], axis=-1)
        high_first = jnp.concatenate([partner_rows, values], axis=-1)
        values = jnp.where(leaf_bit(level_bit) == 0, low_first, high_first)
    return values


def halve_sum(values, bit_list):
    for level_bit in bit_list:
        half_width = values.shape[-1] // 2
        low_half = values[..., :half_width]
        high_half = values[..., half_width:]
        is_upper = leaf_bit(level_bit) == 1
        keep_half = jnp.where(is_upper, high_half, low_half)
        send_half = jnp.where(is_upper, low_half, high_half)
        values = keep_half + partner(send_half, level_bit)
    return values


def group_rows(values):
    return lax.all_gather(values, "grp", axis=0, tiled=True)


def level_width(sep_block, tree_level):
    if tree_level >= 2:
        return 2 * sep_block * 2**tree_level
    return sep_block * 2**tree_level


def local_general(leaf_rhs, leaf_inv, ordering, leaf_dinv, leaf_link, sep_rhs, sep_factor, sep_dinv):
    levels = sep_rhs.shape[0]
    sep_block = sep_rhs.shape[2]
    inverse = jnp.argsort(ordering[0])
    picked = jnp.take(leaf_inv, inverse, axis=1)
    leaf_y = jnp.dot(
        picked,
        lax.all_gather(leaf_rhs, "grp", axis=0, tiled=True),
        preferred_element_type=jnp.float32,
    )
    partial_sum = jnp.einsum("rk,rc->kc", leaf_rhs, leaf_link, preferred_element_type=jnp.float32)
    crossing = lax.psum_scatter(
        partial_sum.astype(jnp.bfloat16), "grp", scatter_dimension=0, tiled=True
    ).astype(jnp.float32)
    leaf_z = (leaf_dinv.astype(jnp.float32)[:, None] * leaf_y).astype(jnp.bfloat16)
    crossing = halve_sum(crossing, [0])
    sep_r = (sep_rhs[0].astype(jnp.float32) - crossing).astype(jnp.bfloat16)
    gathered = group_rows(sep_factor)

    def level_rows(tree_level):
        offset = level_offset(sep_block, tree_level)
        return lax.slice_in_dim(
            gathered, offset, offset + level_width(sep_block, tree_level), axis=1
        )

    z_blocks = []
    full_prev = sep_r
    for tree_level in range(1, levels + 1):
        rows_here = level_rows(tree_level)
        size_here = sep_block * 2**tree_level
        if tree_level >= 2:
            children = spread(full_prev, tree_level - 1, tree_level)
            link_rows = rows_here[:, size_here:]
            coupled = jnp.einsum(
                "kc,qc->kq", children, link_rows, preferred_element_type=jnp.float32
            )
            sep_r = (sep_rhs[tree_level - 1].astype(jnp.float32) - coupled).astype(jnp.bfloat16)
        full_prev = spread(sep_r, 0, tree_level)
        sep_y = jnp.einsum(
            "kc,qc->kq", full_prev, rows_here[:, :size_here], preferred_element_type=jnp.float32
        )
        z_blocks.append(
            (sep_dinv[tree_level - 1].astype(jnp.float32)[None, :] * sep_y).astype(jnp.bfloat16)
        )
    solution = [None] * levels
    upper_rows = level_rows(levels)
    size_top = sep_block * 2**levels
    partial_value = jnp.einsum(
        "kq,qc->kc",
        z_blocks[levels - 1],
        upper_rows[:, :size_top],
        preferred_element_type=jnp.float32,
    )
    current = halve_sum(partial_value, list(range(levels - 1, -1, -1)))
    solution[levels - 1] = current
    for tree_level in range(levels - 1, 0, -1):
        size_here = sep_block * 2**tree_level
        link_rows = upper_rows[:, 2 * size_here :]
        rows_here = level_rows(tree_level)
        pushed = -jnp.einsum(
            "kq,qc->kc", current.astype(jnp.bfloat16), link_rows, preferred_element_type=jnp.float32
        )
        pushed = halve_sum(pushed, [tree_level])
        pushed = pushed + jnp.einsum(
            "kq,qc->kc",
            z_blocks[tree_level - 1],
            rows_here[:, :size_here],
            preferred_element_type=jnp.float32,
        )
        current = halve_sum(pushed, list(range(tree_level - 1, -1, -1)))
        solution[tree_level - 1] = current
        upper_rows = rows_here
    first_full = spread(current.astype(jnp.bfloat16), 0, 1)
    first_all = group_rows(first_full)
    picked = jnp.take(leaf_inv, inverse, axis=1)
    leaf_x = lax.psum_scatter(
        jnp.einsum("rm,rk->mk", picked, leaf_z, preferred_element_type=jnp.float32).astype(
            jnp.bfloat16
        ),
        "grp",
        scatter_dimension=0,
        tiled=True,
    ).astype(jnp.float32)
    leaf_x = leaf_x - jnp.einsum(
        "rc,kc->rk", leaf_link, first_all, preferred_element_type=jnp.float32
    )
    return (leaf_x, jnp.stack(solution, axis=0))


def send_body(whole_ref, low_ref, high_ref, link_ref, fac_ref, out_0_ref, out_1_ref, kept_ref, crossing_ref):
    height, width = out_1_ref.shape
    out_0_ref[:height, :] = whole_ref[:, :width]
    out_1_ref[...] = whole_ref[:, width:]
    first = link_ref.shape[0]
    rows, cols = fac_ref.shape
    split = low_ref.shape[0]
    crossing = dot_nn(link_ref[:, :split], low_ref[...]) + dot_nn(link_ref[:, split:], high_ref[...])
    crossing_ref[...] = crossing
    tiles = (kept_ref.shape[0] - first) // rows
    factor = fac_ref[...].astype(F32)
    factor = jnp.concatenate([factor, jnp.zeros((rows, tiles * LANES - cols), F32)], axis=1)
    folded = [factor[:, tile * LANES : (tile + 1) * LANES] for tile in range(tiles)]
    folded = jnp.concatenate(folded, axis=0)
    me = lax.axis_index("grp")
    kept_ref[first:, :] = jnp.concatenate([folded, folded], axis=1)
    out_0_ref[height + first :, :] = jnp.concatenate([folded, folded], axis=1).astype(BF16)
    for index, (mine, sent) in enumerate(((0, 1), (2, 3))):
        place = slice(index * LANES, (index + 1) * LANES)
        lanes = pl.ds(pl.multiple_of((me ^ mine) * LANES, LANES), LANES)
        kept_ref[:first, place] = crossing_ref[:, lanes]
        lanes = pl.ds(pl.multiple_of((me ^ sent) * LANES, LANES), LANES)
        out_0_ref[height : height + first, place] = crossing_ref[:, lanes].astype(BF16)


def leaf_body(kept_ref, x_ref, y_ref, sep_ref, dinv_ref, out_ref, *, rows, cols):
    levels, sep_block, _ = sep_ref.shape
    first = kept_ref.shape[0] - sep_block
    tiles = sep_block // rows
    me = lax.axis_index("grp")
    x_part = x_ref[x_ref.shape[0] - first - sep_block :, :].astype(F32)
    y_part = y_ref[y_ref.shape[0] - first :, :].astype(F32)
    total = kept_ref[:first, :LANES] + x_part[:first, :LANES] + y_part[:, :LANES]
    out_ref[:first, :] = total.astype(BF16)
    for level in range(levels):
        out_ref[first + level * sep_block : first + (level + 1) * sep_block, :] = sep_ref[level]
    row_owner = lax.broadcasted_iota(jnp.int32, (sep_block, tiles * LANES), 0) // rows
    lane = lax.broadcasted_iota(jnp.int32, (sep_block, tiles * LANES), 1)
    factor = jnp.zeros((sep_block, tiles * LANES), F32)
    folds = (
        kept_ref[first:, :LANES],
        x_part[first:, :LANES],
        y_part[:sep_block, LANES:],
        y_part[sep_block : 2 * sep_block, LANES:],
    )
    for index, folded in enumerate(folds):
        block = [folded[tile * rows : (tile + 1) * rows, :] for tile in range(tiles)]
        block = jnp.concatenate(block, axis=1)
        tiled = jnp.concatenate([block] * (sep_block // rows), axis=0)
        factor = factor + jnp.where(row_owner == (me ^ index), tiled, 0.0)
    pivots = dinv_ref[...].astype(F32).T
    for level in range(levels):
        column = jnp.broadcast_to(pivots[:, level : level + 1], factor.shape)
        factor = jnp.where(lane == cols + level, column, factor)
    base = first + levels * sep_block
    for tile in range(tiles):
        out_ref[base + tile * sep_block : base + (tile + 1) * sep_block, :] = factor[
            :, tile * LANES : (tile + 1) * LANES
        ].astype(BF16)


def pair_body(own_ref, other_ref, out_ref, *, first, sep_block):
    is_odd = lax.axis_index("leaf") % 2 == 1
    own = own_ref[...].astype(F32)
    other = other_ref[...].astype(F32)
    even = jnp.where(is_odd, other, own)
    odd = jnp.where(is_odd, own, other)
    crossing = even[0:first] + odd[0:first]
    for index in range((own.shape[0] - first) // sep_block):
        base = first + index * sep_block
        both = jnp.concatenate([even[base : base + sep_block], odd[base : base + sep_block]], axis=0)
        if index == 0:
            both = both - crossing
        out_ref[index * first : (index + 1) * first, :] = both.astype(BF16)


def tree_body(*refs, count, first, levels, sep_block, cols):
    pairs = refs[:count]
    first_ref, sol_ref, stage_ref, factor_ref, val_ref = refs[count:]
    leaf = lax.axis_index("leaf")
    pair = leaf // 2
    nsep, width = factor_ref.shape
    for index, ref in enumerate(pairs):
        place = pl.ds(pl.multiple_of((pair ^ index) * first, first), first)
        for level in range(levels):
            stage_ref[level, place, :] = ref[level * first : (level + 1) * first, :]
        for tile in range(width // LANES):
            base = (levels + tile) * first
            factor_ref[place, tile * LANES : (tile + 1) * LANES] = ref[base : base + first, :]
    factor = factor_ref[...]
    column = lax.broadcasted_iota(jnp.int32, (width, nsep), 0)
    target = lax.broadcasted_iota(jnp.int32, (width, nsep), 1)
    row = lax.broadcasted_iota(jnp.int32, (nsep, nsep), 0)
    lane = lax.broadcasted_iota(jnp.int32, (nsep, nsep), 1)

    def block_diagonal(offset, size):
        choose = jnp.where(column == offset + target % size, 1.0, 0.0).astype(BF16)
        spread = dot_nn(factor, choose)
        return jnp.where(row // size == lane // size, spread, 0.0).astype(BF16)

    weights, couplings, z_blocks = [], [], []
    residual = stage_ref[0]
    for level in range(1, levels + 1):
        size = sep_block * 2**level
        offset = level_offset(sep_block, level)
        weight = block_diagonal(offset, size)
        coupling = None
        if level >= 2:
            coupling = block_diagonal(offset + size, size)
            residual = (stage_ref[level - 1].astype(F32) - dot_nn(coupling, residual)).astype(BF16)
        pick = lax.broadcasted_iota(jnp.int32, (width, LANES), 0) == cols + level - 1
        scale = dot_nn(factor, jnp.where(pick, 1.0, 0.0).astype(BF16))
        z_blocks.append((scale * dot_nn(weight, residual)).astype(BF16))
        weights.append(weight)
        couplings.append(coupling)
    current = None
    for level in range(levels, 0, -1):
        value = dot_tn(weights[level - 1], z_blocks[level - 1])
        if level < levels:
            value = value - dot_tn(couplings[level], current.astype(BF16))
        current = value
        val_ref[...] = value
        sol_ref[level - 1] = val_ref[pl.ds(pl.multiple_of(leaf * sep_block, sep_block), sep_block), :]
    first_ref[...] = val_ref[pl.ds(pl.multiple_of(pair * first, first), first), :].astype(BF16)


def arrange_body(dest_ref, factor_ref, *refs):
    outs, (turned_ref, sorted_ref) = refs[:-2], refs[-2:]
    step = pl.program_id(0)
    rows, width = factor_ref.shape
    tiles = rows // LANES
    turned = factor_ref[...].astype(F32).T
    for tile in range(tiles):
        turned_ref[pl.ds(tile, width, stride=tiles), :] = turned[:, tile * LANES : (tile + 1) * LANES]

    def move(group, carry):
        for lane in range(UNROLL):
            source = group * UNROLL + lane
            target = dest_ref[step * width + source]
            sorted_ref[pl.ds(pl.multiple_of(target * tiles, tiles), tiles), :] = turned_ref[
                pl.ds(pl.multiple_of(source * tiles, tiles), tiles), :
            ]
        return carry

    lax.fori_loop(0, width // UNROLL, move, 0)

    @pl.when(step == pl.num_programs(0) - 1)
    def _():
        for index, out_ref in enumerate(outs):
            count = out_ref.shape[0]
            chunk = min(count, 256)

            def write(part, carry, index=index, out_ref=out_ref, count=count, chunk=chunk):
                base = index * count * tiles + part * chunk * tiles
                for tile in range(tiles):
                    out_ref[
                        pl.ds(pl.multiple_of(part * chunk, chunk), chunk),
                        tile * LANES : (tile + 1) * LANES,
                    ] = sorted_ref[pl.ds(base + tile, chunk, stride=tiles), :].astype(BF16)
                return carry

            lax.fori_loop(0, count // chunk, write, 0)


def arrange(factor, dest, count):
    rows, cols = factor.shape
    width = math.gcd(cols, 4 * LANES)
    part = cols // count
    return call(
        arrange_body,
        (dest, pltpu.with_memory_space_constraint(factor, pltpu.HBM)),
        [smem(), pl.BlockSpec((rows, width), lambda step: (0, step))],
        [jax.ShapeDtypeStruct((part, rows), BF16)] * count,
        grant=26,
        grid=(cols // width,),
        scratch_shapes=[
            pltpu.VMEM((width * rows // LANES, LANES), F32),
            pltpu.VMEM((cols * rows // LANES, LANES), F32),
        ],
    )


def split_body(rhs_ref, low_ref, high_ref, sems):
    split = low_ref.shape[0]
    copies = [
        pltpu.make_async_copy(rhs_ref.at[pl.ds(index * split, ref.shape[0]), :], ref, sems.at[index])
        for index, ref in enumerate((low_ref, high_ref))
    ]
    for copy in copies:
        copy.start()
    for copy in copies:
        copy.wait()


def cut_body(whole_ref, *outs):
    for part, ref in enumerate(outs):
        height, width = ref.shape
        ref[...] = whole_ref[:height, part * width : (part + 1) * width]


def forward_body(own_ref, x_ref, y_ref, far_ref, *refs):
    pieces, (out_0_ref, out_1_ref, turned_ref, factor_ref, loads_ref) = refs[:-5], refs[-5:]
    rows = own_ref.shape[0]
    width = out_0_ref.shape[1]
    for index, ref in enumerate((own_ref, x_ref, y_ref)):
        factor_ref[index * rows : (index + 1) * rows, :] = ref[...]
    start = 0
    for ref in pieces:
        loads_ref[start : start + ref.shape[0], :] = ref[...]
        start += ref.shape[0]
    out_0_ref[...] = dot_tn(factor_ref[...], loads_ref[:, :width])
    out_1_ref[...] = dot_tn(factor_ref[...], loads_ref[:, width:])
    turned_ref[...] = far_ref[...].T


def far_body(far_ref, turned_ref, low_ref, high_ref, near_ref, dinv_ref, *refs, first):
    kept = refs[:-5]
    z_ref, relay_low_ref, relay_high_ref, loads_ref, part_ref = refs[-5:]
    split, half = low_ref.shape[0], relay_low_ref.shape[0]
    rest = loads_ref.shape[0] - split
    loads_ref[:split, :] = low_ref[...]
    loads_ref[split:, :] = high_ref[:rest, :]
    part_ref[...] = near_ref[...] + dot_nn(turned_ref[...], loads_ref[...])
    pivots = dinv_ref[...].astype(F32)
    width = part_ref.shape[1]
    for tile in range(pivots.shape[0]):
        rows = slice(tile * LANES, (tile + 1) * LANES)
        scale = jnp.broadcast_to(pivots[tile : tile + 1, :], (LANES, LANES)).T
        scale = jnp.concatenate([scale] * (width // LANES), axis=1)
        z_ref[rows, :] = (scale * part_ref[rows, :]).astype(BF16)
    relay_low_ref[...] = dot_nn(far_ref[:half, :], z_ref[...]).astype(BF16)
    relay_high_ref[:half, :] = dot_nn(far_ref[half:, :], z_ref[...]).astype(BF16)
    for kept_ref in kept:
        crossing = kept_ref[:first, LANES:] + high_ref[rest : rest + first, LANES:].astype(F32)
        relay_high_ref[half:, :LANES] = crossing.astype(BF16)
        folds = [kept_ref[first:, LANES:], high_ref[rest + first :, :LANES].astype(F32)]
        relay_high_ref[half:, LANES:] = jnp.concatenate(folds, axis=0).astype(BF16)


def near_body(own_ref, x_ref, y_ref, z_0_ref, z_1_ref, x_low_ref, y_high_ref, x_high_ref, y_low_ref, out_ref, z_ref):
    half, split = x_low_ref.shape[0], z_0_ref.shape[1]
    z_ref[:, :split] = z_0_ref[...]
    z_ref[:, split:] = z_1_ref[...]
    x_low_ref[...] = dot_nn(x_ref[:half, :], z_ref[...]).astype(BF16)
    y_high_ref[...] = dot_nn(y_ref[half:, :], z_ref[...]).astype(BF16)
    x_high_ref[...] = dot_nn(x_ref[half:, :], z_ref[...])
    y_low_ref[...] = dot_nn(y_ref[:half, :], z_ref[...])
    out_ref[...] = dot_nn(own_ref[...], z_ref[...])


def add_body(near_ref, relay_0_ref, relay_1_ref, out_0_ref, out_1_ref):
    half = near_ref.shape[0]
    relay = jnp.concatenate([relay_0_ref[:half, :], relay_1_ref[:half, :]], axis=1).astype(F32)
    total = (near_ref[...] + relay).astype(BF16)
    split = out_0_ref.shape[1]
    out_0_ref[...] = total[:, :split]
    out_1_ref[...] = total[:, split:]


def base_body(own_ref, link_ref, mine_ref, x_ref, y_ref, d_ref, x_low_ref, y_high_ref, out_0_ref, out_1_ref, first_ref):
    half = x_low_ref.shape[0]
    me = lax.axis_index("grp")
    for mask, ref in enumerate((mine_ref, x_ref, y_ref, d_ref)):
        lanes = pl.ds(pl.multiple_of((me ^ mask) * LANES, LANES), LANES)
        first_ref[:, lanes] = ref[...]
    start = 0
    for ref in (out_0_ref, out_1_ref):
        cols = slice(start, start + ref.shape[1])
        start += ref.shape[1]
        ref[...] = own_ref[:, cols] - dot_tn(link_ref[...], first_ref[:, cols])
        ref[:half, :] += x_low_ref[:, cols].astype(F32)
        ref[half:, :] += y_high_ref[:, cols].astype(F32)


def last_body(base_ref, low_ref, high_ref, out_ref, sum_ref, sems, *, start, chunks):
    rows, width = base_ref.shape
    half, height = low_ref.shape[0], rows // chunks
    copies = []
    for chunk in range(chunks):
        top = chunk * height
        place = slice(top, top + height)
        piece_ref, base = (low_ref, top) if top < half else (high_ref, top - half)
        sum_ref[place, :] = base_ref[place, :] + piece_ref[base : base + height, :].astype(F32)
        copy = pltpu.make_async_copy(
            sum_ref.at[pl.ds(top, height), :],
            out_ref.at[pl.ds(top, height), pl.ds(start, width)],
            sems.at[chunk],
        )
        copy.start()
        copies.append(copy)
    for copy in copies:
        copy.wait()


def local_pairs(leaf_rhs, leaf_inv, ordering, leaf_dinv, leaf_link, sep_rhs, sep_factor, sep_dinv):
    rows, width = leaf_rhs.shape
    half, split = rows // 2, rows // 16 * 7
    group = lax.axis_size("grp")
    levels, slice_width, sep_block = sep_rhs.shape
    first = leaf_link.shape[1]
    fac_rows, cols = sep_factor.shape
    tiles = sep_block // fac_rows
    parts = range(2)
    me = lax.axis_index("grp").astype(jnp.int32)
    link_turned = leaf_link.T

    def bf16(height, breadth):
        return jax.ShapeDtypeStruct((height, breadth), BF16)

    def f32(height, breadth):
        return jax.ShapeDtypeStruct((height, breadth), F32)

    x_all = exchange(leaf_rhs, "grp", 1)
    low, high = call(
        split_body,
        (pltpu.with_memory_space_constraint(leaf_rhs, pltpu.HBM),),
        [pl.BlockSpec(memory_space=pltpu.HBM)],
        (bf16(split, width), bf16(rows - split, width)),
        scratch_shapes=[pltpu.SemaphoreType.DMA((2,))],
    )
    y_high = exchange(high, "grp", 2)
    y_low = exchange(low, "grp", 2)
    dest = (ordering[0] // rows ^ me) * rows + ordering[0] % rows
    blocks = arrange(leaf_inv, dest, group)

    *high_cut, kept = call(
        send_body,
        (y_high, low, high, link_turned, sep_factor),
        [vmem()] * 5,
        [
            bf16(rows - split + first + sep_block, width // 2),
            bf16(rows - split, width // 2),
            f32(first + sep_block, 2 * LANES),
        ],
        after=(blocks[0],),
        scratch_shapes=[pltpu.VMEM((first, width), F32)],
    )
    d_high = [exchange(high_cut[part], "grp", 1) for part in parts]
    low_cut = call(cut_body, (x_all,), [vmem()], [bf16(split, width // 2)] * 2, after=(blocks[0],))
    d_low = [exchange(low_cut[part], "grp", 2) for part in parts]

    *part_y, turned = call(
        forward_body,
        (*blocks, low, high, x_all, y_low, y_high),
        [vmem()] * 9,
        [f32(rows, width // 2)] * 2 + [bf16(rows, rows)],
        scratch_shapes=[pltpu.VMEM((3 * rows, rows), BF16), pltpu.VMEM((3 * rows, width), BF16)],
    )
    leaf_z, relay_low, relay_high = [], [], []
    for part in parts:
        shared = (kept,) if part == 0 else ()
        z_part, far_low, far_high = call(
            functools.partial(far_body, first=first),
            (
                blocks[3],
                turned,
                d_low[part],
                d_high[part],
                part_y[part],
                leaf_dinv.reshape(-1, LANES),
                *shared,
            ),
            [vmem()] * (6 + len(shared)),
            (
                bf16(rows, width // 2),
                bf16(half, width // 2),
                bf16(half + first * len(shared), width // 2),
            ),
            scratch_shapes=[pltpu.VMEM((rows, width // 2), BF16), pltpu.VMEM((rows, width // 2), F32)],
        )
        leaf_z.append(z_part)
        relay_low.append(exchange(far_low, "grp", 1))
        relay_high.append(exchange(far_high, "grp", 2))

    near_x_low, near_y_high, near_x_high, near_y_low, own = call(
        near_body,
        (*blocks[:3], *leaf_z),
        [vmem()] * 5,
        [bf16(half, width)] * 2 + [f32(half, width)] * 2 + [f32(rows, width)],
        scratch_shapes=[pltpu.VMEM((rows, width), BF16)],
    )
    leaf_block = call(
        functools.partial(leaf_body, rows=fac_rows, cols=cols),
        (kept, d_high[0], relay_high[0], jnp.swapaxes(sep_rhs, 1, 2), sep_dinv),
        [vmem()] * 5,
        bf16(first + (levels + tiles) * sep_block, LANES),
        after=(own,),
    )
    partner = exchange(leaf_block, "leaf", 1)
    sum_x_low = exchange(near_x_low, "grp", 1)
    sum_y_high = exchange(near_y_high, "grp", 2)
    pair_block = call(
        functools.partial(pair_body, first=first, sep_block=sep_block),
        (leaf_block, partner),
        [vmem(), vmem()],
        bf16((levels + tiles) * first, LANES),
    )
    count = lax.axis_size("leaf") // 2
    pairs = [pair_block] + [exchange(pair_block, "leaf", 2 * mask) for mask in range(1, count)]
    nsep = count * first
    first_here, sep_turned = call(
        functools.partial(
            tree_body, count=count, first=first, levels=levels, sep_block=sep_block, cols=cols
        ),
        pairs,
        [vmem()] * count,
        (bf16(first, LANES), jax.ShapeDtypeStruct((levels, sep_block, slice_width), F32)),
        scratch_shapes=[
            pltpu.VMEM((levels, nsep, LANES), BF16),
            pltpu.VMEM((nsep, tiles * LANES), BF16),
            pltpu.VMEM((nsep, LANES), F32),
        ],
    )
    first_all = [first_here] + [exchange(first_here, "grp", mask) for mask in range(1, group)]
    breadths = (width // 2, width // 2)
    into = [bf16(half, breadth) for breadth in breadths]
    x_sums = call(add_body, (near_x_high, *relay_high), [vmem()] * 3, into)
    y_sums = call(add_body, (near_y_low, *relay_low), [vmem()] * 3, into)
    sum_x_high = [exchange(x_sums[part], "grp", 1) for part in parts]
    sum_y_low = [exchange(y_sums[part], "grp", 2) for part in parts]
    base = call(
        base_body,
        (own, link_turned, *first_all, sum_x_low, sum_y_high),
        [vmem()] * (4 + group),
        [f32(rows, breadth) for breadth in breadths],
        scratch_shapes=[pltpu.VMEM((first, width), BF16)],
    )
    chunks = 4
    leaf_x, start = (), 0
    for part, breadth in zip(parts, breadths):
        leaf_x = (
            call(
                functools.partial(last_body, start=start, chunks=chunks),
                (base[part], sum_y_low[part], sum_x_high[part]),
                [vmem()] * 3,
                f32(rows, width),
                after=leaf_x,
                out_specs=pl.BlockSpec(memory_space=pltpu.HBM),
                scratch_shapes=[pltpu.VMEM((rows, breadth), F32), pltpu.SemaphoreType.DMA((chunks,))],
                input_output_aliases={0: 0} if leaf_x else {},
            ),
        )
        start += breadth
    return leaf_x[0], jnp.swapaxes(sep_turned, 1, 2)


def fits(leaf_rhs, leaf_inv, sep_rhs, sep_factor, leaf_link):
    levels, slice_width, sep_block = sep_rhs.shape
    width = leaf_rhs.shape[1]
    count = lax.axis_size("grp")
    leaves = lax.axis_size("leaf")
    return (
        count == 2**2
        and leaf_inv.shape[1] == count * leaf_rhs.shape[0]
        and leaf_rhs.shape[0] % 256 == 0
        and leaf_rhs.shape[0] // LANES == 8
        and leaf_link.shape[1] == 2 * sep_block
        and sep_block % 16 == 0
        and slice_width % 128 == 0
        and sep_block % sep_factor.shape[0] == 0
        and sep_factor.shape[1] + levels <= sep_block // sep_factor.shape[0] * LANES
        and width == count * slice_width
        and slice_width == LANES
        and width % (leaves * sep_block) == 0
    )


def local(*args):
    leaf_rhs, leaf_inv, _, _, leaf_link, sep_rhs, sep_factor, _ = args
    if fits(leaf_rhs, leaf_inv, sep_rhs, sep_factor, leaf_link):
        return local_pairs(*args)
    return local_general(*args)


def solution(mesh):
    placed = (
        P(("leaf", "grp"), None),
        P(("leaf", "grp"), None),
        P("leaf", None),
        P(("leaf", "grp")),
        P(("leaf", "grp"), None),
        P(None, "grp", "leaf"),
        P(("leaf", "grp"), None),
        P(None, "leaf"),
    )
    return jax.shard_map(
        local,
        mesh=mesh,
        in_specs=placed,
        out_specs=(P(("leaf", "grp"), None), P(None, "grp", "leaf")),
        check_vma=False,
    )
```

```python
import functools
import math

import jax
import jax.numpy as jnp
from jax import lax
from jax.experimental import pallas as pl
from jax.experimental.pallas import tpu as pltpu
from jax.sharding import PartitionSpec as P


F32 = jnp.float32
BF16 = jnp.bfloat16
LANES = 128
UNROLL = 32


def exchange(block, axis, mask):
    count = lax.axis_size(axis)
    return lax.ppermute(block, axis, [(low, low ^ mask) for low in range(count)])


def level_offset(sep_block, tree_level):
    if tree_level >= 2:
        return sep_block * (2 ** (tree_level + 1) - 6)
    return 0


def dot_tn(lhs, rhs):
    return lax.dot_general(lhs, rhs, (((0,), (0,)), ((), ())), preferred_element_type=F32)


def dot_nn(lhs, rhs):
    return jnp.dot(lhs, rhs, preferred_element_type=F32)


def vmem():
    return pl.BlockSpec(memory_space=pltpu.VMEM)


def smem():
    return pl.BlockSpec(memory_space=pltpu.SMEM)


def call(body, ops, specs, out_shape, after=(), grant=16, **rest):
    skip = len(after)
    rest.setdefault("out_specs", jax.tree.map(lambda _: vmem(), out_shape))

    def skipping(*refs):
        body(*refs[skip:])

    return pl.pallas_call(
        skipping,
        out_shape=out_shape,
        in_specs=[pl.BlockSpec(memory_space=pl.ANY)] * skip + specs,
        compiler_params=pltpu.CompilerParams(vmem_limit_bytes=grant * 2**20),
        **rest,
    )(*after, *ops)


def from_partner(block, axis, distance):
    count = lax.axis_size(axis)
    route = []
    for low in range(count):
        high = low | 1 << distance
        if high != low and high < count:
            route += [(low, high), (high, low)]
    return lax.ppermute(block, axis, route)


def partner(values, level_bit):
    return from_partner(values.astype(jnp.bfloat16), "leaf", level_bit).astype(values.dtype)


def leaf_bit(level_bit):
    return jnp.right_shift(lax.axis_index("leaf"), level_bit) % 2


def spread(values, first_bit, last_bit):
    for level_bit in range(first_bit, last_bit):
        partner_rows = partner(values.astype(jnp.float32), level_bit).astype(jnp.bfloat16)
        low_first = jnp.concatenate([values, partner_rows], axis=-1)
        high_first = jnp.concatenate([partner_rows, values], axis=-1)
        values = jnp.where(leaf_bit(level_bit) == 0, low_first, high_first)
    return values


def halve_sum(values, bit_list):
    for level_bit in bit_list:
        half_width = values.shape[-1] // 2
        low_half = values[..., :half_width]
        high_half = values[..., half_width:]
        is_upper = leaf_bit(level_bit) == 1
        keep_half = jnp.where(is_upper, high_half, low_half)
        send_half = jnp.where(is_upper, low_half, high_half)
        values = keep_half + partner(send_half, level_bit)
    return values


def group_rows(values):
    return lax.all_gather(values, "grp", axis=0, tiled=True)


def level_width(sep_block, tree_level):
    if tree_level >= 2:
        return 2 * sep_block * 2**tree_level
    return sep_block * 2**tree_level


def local_general(leaf_rhs, leaf_inv, ordering, leaf_dinv, leaf_link, sep_rhs, sep_factor, sep_dinv):
    levels = sep_rhs.shape[0]
    sep_block = sep_rhs.shape[2]
    inverse = jnp.argsort(ordering[0])
    picked = jnp.take(leaf_inv, inverse, axis=1)
    leaf_y = jnp.dot(
        picked,
        lax.all_gather(leaf_rhs, "grp", axis=0, tiled=True),
        preferred_element_type=jnp.float32,
    )
    partial_sum = jnp.einsum("rk,rc->kc", leaf_rhs, leaf_link, preferred_element_type=jnp.float32)
    crossing = lax.psum_scatter(
        partial_sum.astype(jnp.bfloat16), "grp", scatter_dimension=0, tiled=True
    ).astype(jnp.float32)
    leaf_z = (leaf_dinv.astype(jnp.float32)[:, None] * leaf_y).astype(jnp.bfloat16)
    crossing = halve_sum(crossing, [0])
    sep_r = (sep_rhs[0].astype(jnp.float32) - crossing).astype(jnp.bfloat16)
    gathered = group_rows(sep_factor)

    def level_rows(tree_level):
        offset = level_offset(sep_block, tree_level)
        return lax.slice_in_dim(
            gathered, offset, offset + level_width(sep_block, tree_level), axis=1
        )

    z_blocks = []
    full_prev = sep_r
    for tree_level in range(1, levels + 1):
        rows_here = level_rows(tree_level)
        size_here = sep_block * 2**tree_level
        if tree_level >= 2:
            children = spread(full_prev, tree_level - 1, tree_level)
            link_rows = rows_here[:, size_here:]
            coupled = jnp.einsum(
                "kc,qc->kq", children, link_rows, preferred_element_type=jnp.float32
            )
            sep_r = (sep_rhs[tree_level - 1].astype(jnp.float32) - coupled).astype(jnp.bfloat16)
        full_prev = spread(sep_r, 0, tree_level)
        sep_y = jnp.einsum(
            "kc,qc->kq", full_prev, rows_here[:, :size_here], preferred_element_type=jnp.float32
        )
        z_blocks.append(
            (sep_dinv[tree_level - 1].astype(jnp.float32)[None, :] * sep_y).astype(jnp.bfloat16)
        )
    solution = [None] * levels
    upper_rows = level_rows(levels)
    size_top = sep_block * 2**levels
    partial_value = jnp.einsum(
        "kq,qc->kc",
        z_blocks[levels - 1],
        upper_rows[:, :size_top],
        preferred_element_type=jnp.float32,
    )
    current = halve_sum(partial_value, list(range(levels - 1, -1, -1)))
    solution[levels - 1] = current
    for tree_level in range(levels - 1, 0, -1):
        size_here = sep_block * 2**tree_level
        link_rows = upper_rows[:, 2 * size_here :]
        rows_here = level_rows(tree_level)
        pushed = -jnp.einsum(
            "kq,qc->kc", current.astype(jnp.bfloat16), link_rows, preferred_element_type=jnp.float32
        )
        pushed = halve_sum(pushed, [tree_level])
        pushed = pushed + jnp.einsum(
            "kq,qc->kc",
            z_blocks[tree_level - 1],
            rows_here[:, :size_here],
            preferred_element_type=jnp.float32,
        )
        current = halve_sum(pushed, list(range(tree_level - 1, -1, -1)))
        solution[tree_level - 1] = current
        upper_rows = rows_here
    first_full = spread(current.astype(jnp.bfloat16), 0, 1)
    first_all = group_rows(first_full)
    picked = jnp.take(leaf_inv, inverse, axis=1)
    leaf_x = lax.psum_scatter(
        jnp.einsum("rm,rk->mk", picked, leaf_z, preferred_element_type=jnp.float32).astype(
            jnp.bfloat16
        ),
        "grp",
        scatter_dimension=0,
        tiled=True,
    ).astype(jnp.float32)
    leaf_x = leaf_x - jnp.einsum(
        "rc,kc->rk", leaf_link, first_all, preferred_element_type=jnp.float32
    )
    return (leaf_x, jnp.stack(solution, axis=0))


def send_body(whole_ref, low_ref, high_ref, link_ref, fac_ref, out_0_ref, out_1_ref, kept_ref, crossing_ref):
    height, width = out_1_ref.shape
    out_0_ref[:height, :] = whole_ref[:, :width]
    out_1_ref[...] = whole_ref[:, width:]
    first = link_ref.shape[0]
    rows, cols = fac_ref.shape
    split = low_ref.shape[0]
    crossing = dot_nn(link_ref[:, :split], low_ref[...]) + dot_nn(link_ref[:, split:], high_ref[...])
    crossing_ref[...] = crossing
    tiles = (kept_ref.shape[0] - first) // rows
    factor = fac_ref[...].astype(F32)
    factor = jnp.concatenate([factor, jnp.zeros((rows, tiles * LANES - cols), F32)], axis=1)
    folded = [factor[:, tile * LANES : (tile + 1) * LANES] for tile in range(tiles)]
    folded = jnp.concatenate(folded, axis=0)
    me = lax.axis_index("grp")
    kept_ref[first:, :] = jnp.concatenate([folded, folded], axis=1)
    out_0_ref[height + first :, :] = jnp.concatenate([folded, folded], axis=1).astype(BF16)
    for index, (mine, sent) in enumerate(((0, 1), (2, 3))):
        place = slice(index * LANES, (index + 1) * LANES)
        lanes = pl.ds(pl.multiple_of((me ^ mine) * LANES, LANES), LANES)
        kept_ref[:first, place] = crossing_ref[:, lanes]
        lanes = pl.ds(pl.multiple_of((me ^ sent) * LANES, LANES), LANES)
        out_0_ref[height : height + first, place] = crossing_ref[:, lanes].astype(BF16)


def leaf_body(kept_ref, x_ref, y_ref, sep_ref, dinv_ref, out_ref, *, rows, cols):
    levels, sep_block, _ = sep_ref.shape
    first = kept_ref.shape[0] - sep_block
    tiles = sep_block // rows
    me = lax.axis_index("grp")
    x_part = x_ref[x_ref.shape[0] - first - sep_block :, :].astype(F32)
    y_part = y_ref[y_ref.shape[0] - first :, :].astype(F32)
    total = kept_ref[:first, :LANES] + x_part[:first, :LANES] + y_part[:, :LANES]
    out_ref[:first, :] = total.astype(BF16)
    for level in range(levels):
        out_ref[first + level * sep_block : first + (level + 1) * sep_block, :] = sep_ref[level]
    row_owner = lax.broadcasted_iota(jnp.int32, (sep_block, tiles * LANES), 0) // rows
    lane = lax.broadcasted_iota(jnp.int32, (sep_block, tiles * LANES), 1)
    factor = jnp.zeros((sep_block, tiles * LANES), F32)
    folds = (
        kept_ref[first:, :LANES],
        x_part[first:, :LANES],
        y_part[:sep_block, LANES:],
        y_part[sep_block : 2 * sep_block, LANES:],
    )
    for index, folded in enumerate(folds):
        block = [folded[tile * rows : (tile + 1) * rows, :] for tile in range(tiles)]
        block = jnp.concatenate(block, axis=1)
        tiled = jnp.concatenate([block] * (sep_block // rows), axis=0)
        factor = factor + jnp.where(row_owner == (me ^ index), tiled, 0.0)
    pivots = dinv_ref[...].astype(F32).T
    for level in range(levels):
        column = jnp.broadcast_to(pivots[:, level : level + 1], factor.shape)
        factor = jnp.where(lane == cols + level, column, factor)
    base = first + levels * sep_block
    for tile in range(tiles):
        out_ref[base + tile * sep_block : base + (tile + 1) * sep_block, :] = factor[
            :, tile * LANES : (tile + 1) * LANES
        ].astype(BF16)


def pair_body(own_ref, other_ref, out_ref, *, first, sep_block):
    is_odd = lax.axis_index("leaf") % 2 == 1
    own = own_ref[...].astype(F32)
    other = other_ref[...].astype(F32)
    even = jnp.where(is_odd, other, own)
    odd = jnp.where(is_odd, own, other)
    crossing = even[0:first] + odd[0:first]
    for index in range((own.shape[0] - first) // sep_block):
        base = first + index * sep_block
        both = jnp.concatenate([even[base : base + sep_block], odd[base : base + sep_block]], axis=0)
        if index == 0:
            both = both - crossing
        out_ref[index * first : (index + 1) * first, :] = both.astype(BF16)


def tree_body(*refs, count, first, levels, sep_block, cols):
    pairs = refs[:count]
    first_ref, sol_ref, stage_ref, factor_ref, val_ref = refs[count:]
    leaf = lax.axis_index("leaf")
    pair = leaf // 2
    nsep, width = factor_ref.shape
    for index, ref in enumerate(pairs):
        place = pl.ds(pl.multiple_of((pair ^ index) * first, first), first)
        for level in range(levels):
            stage_ref[level, place, :] = ref[level * first : (level + 1) * first, :]
        for tile in range(width // LANES):
            base = (levels + tile) * first
            factor_ref[place, tile * LANES : (tile + 1) * LANES] = ref[base : base + first, :]
    factor = factor_ref[...]
    column = lax.broadcasted_iota(jnp.int32, (width, nsep), 0)
    target = lax.broadcasted_iota(jnp.int32, (width, nsep), 1)
    row = lax.broadcasted_iota(jnp.int32, (nsep, nsep), 0)
    lane = lax.broadcasted_iota(jnp.int32, (nsep, nsep), 1)

    def block_diagonal(offset, size):
        choose = jnp.where(column == offset + target % size, 1.0, 0.0).astype(BF16)
        spread = dot_nn(factor, choose)
        return jnp.where(row // size == lane // size, spread, 0.0).astype(BF16)

    weights, couplings, z_blocks = [], [], []
    residual = stage_ref[0]
    for level in range(1, levels + 1):
        size = sep_block * 2**level
        offset = level_offset(sep_block, level)
        weight = block_diagonal(offset, size)
        coupling = None
        if level >= 2:
            coupling = block_diagonal(offset + size, size)
            residual = (stage_ref[level - 1].astype(F32) - dot_nn(coupling, residual)).astype(BF16)
        pick = lax.broadcasted_iota(jnp.int32, (width, LANES), 0) == cols + level - 1
        scale = dot_nn(factor, jnp.where(pick, 1.0, 0.0).astype(BF16))
        z_blocks.append((scale * dot_nn(weight, residual)).astype(BF16))
        weights.append(weight)
        couplings.append(coupling)
    current = None
    for level in range(levels, 0, -1):
        value = dot_tn(weights[level - 1], z_blocks[level - 1])
        if level < levels:
            value = value - dot_tn(couplings[level], current.astype(BF16))
        current = value
        val_ref[...] = value
        sol_ref[level - 1] = val_ref[pl.ds(pl.multiple_of(leaf * sep_block, sep_block), sep_block), :]
    first_ref[...] = val_ref[pl.ds(pl.multiple_of(pair * first, first), first), :].astype(BF16)


def arrange_body(dest_ref, factor_ref, *refs):
    outs, (turned_ref, sorted_ref) = refs[:-2], refs[-2:]
    step = pl.program_id(0)
    rows, width = factor_ref.shape
    tiles = rows // LANES
    turned = factor_ref[...].astype(F32).T
    for tile in range(tiles):
        turned_ref[pl.ds(tile, width, stride=tiles), :] = turned[:, tile * LANES : (tile + 1) * LANES]

    def move(group, carry):
        for lane in range(UNROLL):
            source = group * UNROLL + lane
            target = dest_ref[step * width + source]
            sorted_ref[pl.ds(pl.multiple_of(target * tiles, tiles), tiles), :] = turned_ref[
                pl.ds(pl.multiple_of(source * tiles, tiles), tiles), :
            ]
        return carry

    lax.fori_loop(0, width // UNROLL, move, 0)

    @pl.when(step == pl.num_programs(0) - 1)
    def _():
        for index, out_ref in enumerate(outs):
            count = out_ref.shape[0]
            chunk = min(count, 256)

            def write(part, carry, index=index, out_ref=out_ref, count=count, chunk=chunk):
                base = index * count * tiles + part * chunk * tiles
                for tile in range(tiles):
                    out_ref[
                        pl.ds(pl.multiple_of(part * chunk, chunk), chunk),
                        tile * LANES : (tile + 1) * LANES,
                    ] = sorted_ref[pl.ds(base + tile, chunk, stride=tiles), :].astype(BF16)
                return carry

            lax.fori_loop(0, count // chunk, write, 0)


def arrange(factor, dest, count):
    rows, cols = factor.shape
    width = math.gcd(cols, 4 * LANES)
    part = cols // count
    return call(
        arrange_body,
        (dest, pltpu.with_memory_space_constraint(factor, pltpu.HBM)),
        [smem(), pl.BlockSpec((rows, width), lambda step: (0, step))],
        [jax.ShapeDtypeStruct((part, rows), BF16)] * count,
        grant=26,
        grid=(cols // width,),
        scratch_shapes=[
            pltpu.VMEM((width * rows // LANES, LANES), F32),
            pltpu.VMEM((cols * rows // LANES, LANES), F32),
        ],
    )


def split_body(rhs_ref, out_ref, sem, *, top):
    copy = pltpu.make_async_copy(rhs_ref.at[pl.ds(top, out_ref.shape[0]), :], out_ref, sem)
    copy.start()
    copy.wait()


def cut_body(whole_ref, *outs):
    for part, ref in enumerate(outs):
        height, width = ref.shape
        ref[...] = whole_ref[:height, part * width : (part + 1) * width]


def row_blocks(rows):
    height = math.gcd(rows, 2 * LANES)
    return [slice(top, top + height) for top in range(0, rows, height)]


def forward_body(own_ref, x_ref, y_ref, far_ref, dinv_ref, *refs):
    pieces, (out_0_ref, out_1_ref, turned_ref, scale_ref, factor_ref, loads_ref) = refs[:-6], refs[-6:]
    rows = own_ref.shape[0]
    width = out_0_ref.shape[1]
    for index, ref in enumerate((own_ref, x_ref, y_ref)):
        factor_ref[index * rows : (index + 1) * rows, :] = ref[...]
    start = 0
    for ref in pieces:
        loads_ref[start : start + ref.shape[0], :] = ref[...]
        start += ref.shape[0]
    for block in row_blocks(rows):
        product = dot_tn(factor_ref[:, block], loads_ref[...])
        out_0_ref[block, :] = product[:, :width]
        out_1_ref[block, :] = product[:, width:]
    turned_ref[...] = far_ref[...].T
    pivots = dinv_ref[...].astype(F32)
    for tile in range(pivots.shape[0]):
        block = slice(tile * LANES, (tile + 1) * LANES)
        scale_ref[block, :] = jnp.broadcast_to(pivots[tile : tile + 1, :], (LANES, LANES)).T


def far_body(far_ref, turned_ref, low_ref, high_ref, near_ref, scale_ref, *refs, first):
    kept = refs[:-4]
    z_ref, relay_low_ref, relay_high_ref, loads_ref = refs[-4:]
    split, half = low_ref.shape[0], relay_low_ref.shape[0]
    rows, width = z_ref.shape
    rest = rows - split
    loads_ref[:split, :] = low_ref[...]
    loads_ref[split:, :] = high_ref[:rest, :]
    for block in row_blocks(rows):
        leaf_y = near_ref[block, :] + dot_nn(turned_ref[block, :], loads_ref[...])
        scale = jnp.concatenate([scale_ref[block, :]] * (width // LANES), axis=1)
        z_ref[block, :] = (scale * leaf_y).astype(BF16)
    for block in row_blocks(half):
        relay_low_ref[block, :] = dot_nn(far_ref[block, :], z_ref[...]).astype(BF16)
    for block in row_blocks(half):
        below = slice(half + block.start, half + block.stop)
        relay_high_ref[block, :] = dot_nn(far_ref[below, :], z_ref[...]).astype(BF16)
    for kept_ref in kept:
        crossing = kept_ref[:first, LANES:] + high_ref[rest : rest + first, LANES:].astype(F32)
        relay_high_ref[half:, :LANES] = crossing.astype(BF16)
        folds = [kept_ref[first:, LANES:], high_ref[rest + first :, :LANES].astype(F32)]
        relay_high_ref[half:, LANES:] = jnp.concatenate(folds, axis=0).astype(BF16)


def near_body(own_ref, x_ref, y_ref, z_0_ref, z_1_ref, x_low_ref, y_high_ref, x_high_ref, y_low_ref, out_ref, z_ref):
    half, split = x_low_ref.shape[0], z_0_ref.shape[1]
    z_ref[:, :split] = z_0_ref[...]
    z_ref[:, split:] = z_1_ref[...]
    for factor_ref, top, ref in (
        (x_ref, 0, x_low_ref),
        (y_ref, half, y_high_ref),
        (x_ref, half, x_high_ref),
        (y_ref, 0, y_low_ref),
        (own_ref, 0, out_ref),
    ):
        for block in row_blocks(ref.shape[0]):
            part = slice(top + block.start, top + block.stop)
            ref[block, :] = dot_nn(factor_ref[part, :], z_ref[...]).astype(ref.dtype)


def add_body(near_ref, relay_0_ref, relay_1_ref, out_0_ref, out_1_ref):
    half = near_ref.shape[0]
    relay = jnp.concatenate([relay_0_ref[:half, :], relay_1_ref[:half, :]], axis=1).astype(F32)
    total = (near_ref[...] + relay).astype(BF16)
    split = out_0_ref.shape[1]
    out_0_ref[...] = total[:, :split]
    out_1_ref[...] = total[:, split:]


def base_body(own_ref, link_ref, mine_ref, x_ref, y_ref, d_ref, x_low_ref, y_high_ref, out_0_ref, out_1_ref, first_ref):
    half = x_low_ref.shape[0]
    me = lax.axis_index("grp")
    for mask, ref in enumerate((mine_ref, x_ref, y_ref, d_ref)):
        lanes = pl.ds(pl.multiple_of((me ^ mask) * LANES, LANES), LANES)
        first_ref[:, lanes] = ref[...]
    start = 0
    for ref in (out_0_ref, out_1_ref):
        cols = slice(start, start + ref.shape[1])
        start += ref.shape[1]
        ref[...] = own_ref[:, cols] - dot_tn(link_ref[...], first_ref[:, cols])
        ref[:half, :] += x_low_ref[:, cols].astype(F32)
        ref[half:, :] += y_high_ref[:, cols].astype(F32)


def last_body(base_ref, low_ref, high_ref, out_ref, sum_ref, sems, *, start, chunks):
    rows, width = base_ref.shape
    half, height = low_ref.shape[0], rows // chunks
    copies = []
    for chunk in range(chunks):
        top = chunk * height
        place = slice(top, top + height)
        piece_ref, base = (low_ref, top) if top < half else (high_ref, top - half)
        sum_ref[place, :] = base_ref[place, :] + piece_ref[base : base + height, :].astype(F32)
        copy = pltpu.make_async_copy(
            sum_ref.at[pl.ds(top, height), :],
            out_ref.at[pl.ds(top, height), pl.ds(start, width)],
            sems.at[chunk],
        )
        copy.start()
        copies.append(copy)
    for copy in copies:
        copy.wait()


def local_pairs(leaf_rhs, leaf_inv, ordering, leaf_dinv, leaf_link, sep_rhs, sep_factor, sep_dinv):
    rows, width = leaf_rhs.shape
    half, split = rows // 2, rows // 16 * 7
    group = lax.axis_size("grp")
    levels, slice_width, sep_block = sep_rhs.shape
    first = leaf_link.shape[1]
    fac_rows, cols = sep_factor.shape
    tiles = sep_block // fac_rows
    parts = range(2)
    me = lax.axis_index("grp").astype(jnp.int32)
    link_turned = leaf_link.T

    def bf16(height, breadth):
        return jax.ShapeDtypeStruct((height, breadth), BF16)

    def f32(height, breadth):
        return jax.ShapeDtypeStruct((height, breadth), F32)

    x_all = exchange(leaf_rhs, "grp", 1)
    loads = pltpu.with_memory_space_constraint(leaf_rhs, pltpu.HBM)
    high, low = (
        call(
            functools.partial(split_body, top=top),
            (loads,),
            [pl.BlockSpec(memory_space=pltpu.HBM)],
            bf16(height, width),
            scratch_shapes=[pltpu.SemaphoreType.DMA],
        )
        for top, height in ((split, rows - split), (0, split))
    )
    y_high = exchange(high, "grp", 2)
    y_low = exchange(low, "grp", 2)
    dest = (ordering[0] // rows ^ me) * rows + ordering[0] % rows
    blocks = arrange(leaf_inv, dest, group)

    *high_cut, kept = call(
        send_body,
        (y_high, low, high, link_turned, sep_factor),
        [vmem()] * 5,
        [
            bf16(rows - split + first + sep_block, width // 2),
            bf16(rows - split, width // 2),
            f32(first + sep_block, 2 * LANES),
        ],
        after=(blocks[0],),
        scratch_shapes=[pltpu.VMEM((first, width), F32)],
    )
    d_high = [exchange(high_cut[part], "grp", 1) for part in parts]
    low_cut = call(cut_body, (x_all,), [vmem()], [bf16(split, width // 2)] * 2, after=(blocks[0],))
    d_low = [exchange(low_cut[part], "grp", 2) for part in parts]

    *part_y, turned, scale = call(
        forward_body,
        (*blocks, leaf_dinv.reshape(-1, LANES), low, high, x_all, y_low, y_high),
        [vmem()] * 10,
        [f32(rows, width // 2)] * 2 + [bf16(rows, rows), f32(rows, LANES)],
        scratch_shapes=[pltpu.VMEM((3 * rows, rows), BF16), pltpu.VMEM((3 * rows, width), BF16)],
    )
    leaf_z, relay_low, relay_high = [], [], []
    for part in parts:
        shared = (kept,) if part == 0 else ()
        z_part, far_low, far_high = call(
            functools.partial(far_body, first=first),
            (
                blocks[3],
                turned,
                d_low[part],
                d_high[part],
                part_y[part],
                scale,
                *shared,
            ),
            [vmem()] * (6 + len(shared)),
            (
                bf16(rows, width // 2),
                bf16(half, width // 2),
                bf16(half + first * len(shared), width // 2),
            ),
            scratch_shapes=[pltpu.VMEM((rows, width // 2), BF16)],
        )
        leaf_z.append(z_part)
        relay_low.append(exchange(far_low, "grp", 1))
        relay_high.append(exchange(far_high, "grp", 2))

    near_x_low, near_y_high, near_x_high, near_y_low, own = call(
        near_body,
        (*blocks[:3], *leaf_z),
        [vmem()] * 5,
        [bf16(half, width)] * 2 + [f32(half, width)] * 2 + [f32(rows, width)],
        scratch_shapes=[pltpu.VMEM((rows, width), BF16)],
    )
    leaf_block = call(
        functools.partial(leaf_body, rows=fac_rows, cols=cols),
        (kept, d_high[0], relay_high[0], jnp.swapaxes(sep_rhs, 1, 2), sep_dinv),
        [vmem()] * 5,
        bf16(first + (levels + tiles) * sep_block, LANES),
        after=(own,),
    )
    partner = exchange(leaf_block, "leaf", 1)
    sum_x_low = exchange(near_x_low, "grp", 1)
    sum_y_high = exchange(near_y_high, "grp", 2)
    pair_block = call(
        functools.partial(pair_body, first=first, sep_block=sep_block),
        (leaf_block, partner),
        [vmem(), vmem()],
        bf16((levels + tiles) * first, LANES),
    )
    count = lax.axis_size("leaf") // 2
    pairs = [pair_block] + [exchange(pair_block, "leaf", 2 * mask) for mask in range(1, count)]
    nsep = count * first
    first_here, sep_turned = call(
        functools.partial(
            tree_body, count=count, first=first, levels=levels, sep_block=sep_block, cols=cols
        ),
        pairs,
        [vmem()] * count,
        (bf16(first, LANES), jax.ShapeDtypeStruct((levels, sep_block, slice_width), F32)),
        scratch_shapes=[
            pltpu.VMEM((levels, nsep, LANES), BF16),
            pltpu.VMEM((nsep, tiles * LANES), BF16),
            pltpu.VMEM((nsep, LANES), F32),
        ],
    )
    first_all = [first_here] + [exchange(first_here, "grp", mask) for mask in range(1, group)]
    breadths = (width // 2, width // 2)
    into = [bf16(half, breadth) for breadth in breadths]
    x_sums = call(add_body, (near_x_high, *relay_high), [vmem()] * 3, into)
    y_sums = call(add_body, (near_y_low, *relay_low), [vmem()] * 3, into)
    sum_x_high = [exchange(x_sums[part], "grp", 1) for part in parts]
    sum_y_low = [exchange(y_sums[part], "grp", 2) for part in parts]
    base = call(
        base_body,
        (own, link_turned, *first_all, sum_x_low, sum_y_high),
        [vmem()] * (4 + group),
        [f32(rows, breadth) for breadth in breadths],
        scratch_shapes=[pltpu.VMEM((first, width), BF16)],
    )
    chunks = 4
    leaf_x, start = (), 0
    for part, breadth in zip(parts, breadths):
        leaf_x = (
            call(
                functools.partial(last_body, start=start, chunks=chunks),
                (base[part], sum_y_low[part], sum_x_high[part]),
                [vmem()] * 3,
                f32(rows, width),
                after=leaf_x,
                out_specs=pl.BlockSpec(memory_space=pltpu.HBM),
                scratch_shapes=[pltpu.VMEM((rows, breadth), F32), pltpu.SemaphoreType.DMA((chunks,))],
                input_output_aliases={0: 0} if leaf_x else {},
            ),
        )
        start += breadth
    return leaf_x[0], jnp.swapaxes(sep_turned, 1, 2)


def fits(leaf_rhs, leaf_inv, sep_rhs, sep_factor, leaf_link):
    levels, slice_width, sep_block = sep_rhs.shape
    width = leaf_rhs.shape[1]
    count = lax.axis_size("grp")
    leaves = lax.axis_size("leaf")
    return (
        count == 2**2
        and leaf_inv.shape[1] == count * leaf_rhs.shape[0]
        and leaf_rhs.shape[0] % 256 == 0
        and leaf_rhs.shape[0] // LANES == 8
        and leaf_link.shape[1] == 2 * sep_block
        and sep_block % 16 == 0
        and slice_width % 128 == 0
        and sep_block % sep_factor.shape[0] == 0
        and sep_factor.shape[1] + levels <= sep_block // sep_factor.shape[0] * LANES
        and width == count * slice_width
        and slice_width == LANES
        and width % (leaves * sep_block) == 0
    )


def local(*args):
    leaf_rhs, leaf_inv, _, _, leaf_link, sep_rhs, sep_factor, _ = args
    if fits(leaf_rhs, leaf_inv, sep_rhs, sep_factor, leaf_link):
        return local_pairs(*args)
    return local_general(*args)


def solution(mesh):
    placed = (
        P(("leaf", "grp"), None),
        P(("leaf", "grp"), None),
        P("leaf", None),
        P(("leaf", "grp")),
        P(("leaf", "grp"), None),
        P(None, "grp", "leaf"),
        P(("leaf", "grp"), None),
        P(None, "leaf"),
    )
    return jax.shard_map(
        local,
        mesh=mesh,
        in_specs=placed,
        out_specs=(P(("leaf", "grp"), None), P(None, "grp", "leaf")),
        check_vma=False,
    )
```

```python
import functools
import math

import jax
import jax.numpy as jnp
from jax import lax
from jax.experimental import pallas as pl
from jax.experimental.pallas import tpu as pltpu
from jax.sharding import PartitionSpec as P


F32 = jnp.float32
BF16 = jnp.bfloat16
LANES = 128
GRP, LEAF = "grp", "leaf"
UNROLL = 32


def exchange(block, axis, mask):
    count = lax.axis_size(axis)
    return lax.ppermute(block, axis, [(low, low ^ mask) for low in range(count)])


def level_offset(sep_block, tree_level):
    if tree_level >= 2:
        return sep_block * (2 ** (tree_level + 1) - 6)
    return 0


def dot_tn(lhs, rhs):
    return lax.dot_general(lhs, rhs, (((0,), (0,)), ((), ())), preferred_element_type=F32)


def dot_nn(lhs, rhs):
    return jnp.dot(lhs, rhs, preferred_element_type=F32)


def vmem():
    return pl.BlockSpec(memory_space=pltpu.VMEM)


def smem():
    return pl.BlockSpec(memory_space=pltpu.SMEM)


def call(body, ops, specs, out_shape, after=(), grant=16, **rest):
    skip = len(after)
    rest.setdefault("out_specs", jax.tree.map(lambda _: vmem(), out_shape))

    def skipping(*refs):
        body(*refs[skip:])

    return pl.pallas_call(
        skipping,
        out_shape=out_shape,
        in_specs=[pl.BlockSpec(memory_space=pl.ANY)] * skip + specs,
        compiler_params=pltpu.CompilerParams(vmem_limit_bytes=grant * 2**20),
        **rest,
    )(*after, *ops)


def from_partner(block, axis, distance):
    count = lax.axis_size(axis)
    route = []
    for low in range(count):
        high = low | 1 << distance
        if high != low and high < count:
            route += [(low, high), (high, low)]
    return lax.ppermute(block, axis, route)


def partner(values, level_bit):
    return from_partner(values.astype(jnp.bfloat16), LEAF, level_bit).astype(values.dtype)


def leaf_bit(level_bit):
    return jnp.right_shift(lax.axis_index(LEAF), level_bit) % 2


def spread(values, first_bit, last_bit):
    for level_bit in range(first_bit, last_bit):
        partner_rows = partner(values.astype(jnp.float32), level_bit).astype(jnp.bfloat16)
        low_first = jnp.concatenate([values, partner_rows], axis=-1)
        high_first = jnp.concatenate([partner_rows, values], axis=-1)
        values = jnp.where(leaf_bit(level_bit) == 0, low_first, high_first)
    return values


def halve_sum(values, bit_list):
    for level_bit in bit_list:
        half_width = values.shape[-1] // 2
        low_half = values[..., :half_width]
        high_half = values[..., half_width:]
        is_upper = leaf_bit(level_bit) == 1
        keep_half = jnp.where(is_upper, high_half, low_half)
        send_half = jnp.where(is_upper, low_half, high_half)
        values = keep_half + partner(send_half, level_bit)
    return values


def group_rows(values):
    return lax.all_gather(values, GRP, axis=0, tiled=True)


def level_width(sep_block, tree_level):
    if tree_level >= 2:
        return 2 * sep_block * 2**tree_level
    return sep_block * 2**tree_level


def local_general(leaf_rhs, leaf_inv, ordering, leaf_dinv, leaf_link, sep_rhs, sep_factor, sep_dinv):
    levels = sep_rhs.shape[0]
    sep_block = sep_rhs.shape[2]
    inverse = jnp.argsort(ordering[0])
    picked = jnp.take(leaf_inv, inverse, axis=1)
    leaf_y = jnp.dot(
        picked,
        lax.all_gather(leaf_rhs, GRP, axis=0, tiled=True),
        preferred_element_type=jnp.float32,
    )
    partial_sum = jnp.einsum("rk,rc->kc", leaf_rhs, leaf_link, preferred_element_type=jnp.float32)
    crossing = lax.psum_scatter(
        partial_sum.astype(jnp.bfloat16), GRP, scatter_dimension=0, tiled=True
    ).astype(jnp.float32)
    leaf_z = (leaf_dinv.astype(jnp.float32)[:, None] * leaf_y).astype(jnp.bfloat16)
    crossing = halve_sum(crossing, [0])
    sep_r = (sep_rhs[0].astype(jnp.float32) - crossing).astype(jnp.bfloat16)
    gathered = group_rows(sep_factor)

    def level_rows(tree_level):
        offset = level_offset(sep_block, tree_level)
        return lax.slice_in_dim(
            gathered, offset, offset + level_width(sep_block, tree_level), axis=1
        )

    z_blocks = []
    full_prev = sep_r
    for tree_level in range(1, levels + 1):
        rows_here = level_rows(tree_level)
        size_here = sep_block * 2**tree_level
        if tree_level >= 2:
            children = spread(full_prev, tree_level - 1, tree_level)
            link_rows = rows_here[:, size_here:]
            coupled = jnp.einsum(
                "kc,qc->kq", children, link_rows, preferred_element_type=jnp.float32
            )
            sep_r = (sep_rhs[tree_level - 1].astype(jnp.float32) - coupled).astype(jnp.bfloat16)
        full_prev = spread(sep_r, 0, tree_level)
        sep_y = jnp.einsum(
            "kc,qc->kq", full_prev, rows_here[:, :size_here], preferred_element_type=jnp.float32
        )
        z_blocks.append(
            (sep_dinv[tree_level - 1].astype(jnp.float32)[None, :] * sep_y).astype(jnp.bfloat16)
        )
    solution = [None] * levels
    upper_rows = level_rows(levels)
    size_top = sep_block * 2**levels
    partial_value = jnp.einsum(
        "kq,qc->kc",
        z_blocks[levels - 1],
        upper_rows[:, :size_top],
        preferred_element_type=jnp.float32,
    )
    current = halve_sum(partial_value, list(range(levels - 1, -1, -1)))
    solution[levels - 1] = current
    for tree_level in range(levels - 1, 0, -1):
        size_here = sep_block * 2**tree_level
        link_rows = upper_rows[:, 2 * size_here :]
        rows_here = level_rows(tree_level)
        pushed = -jnp.einsum(
            "kq,qc->kc", current.astype(jnp.bfloat16), link_rows, preferred_element_type=jnp.float32
        )
        pushed = halve_sum(pushed, [tree_level])
        pushed = pushed + jnp.einsum(
            "kq,qc->kc",
            z_blocks[tree_level - 1],
            rows_here[:, :size_here],
            preferred_element_type=jnp.float32,
        )
        current = halve_sum(pushed, list(range(tree_level - 1, -1, -1)))
        solution[tree_level - 1] = current
        upper_rows = rows_here
    first_full = spread(current.astype(jnp.bfloat16), 0, 1)
    first_all = group_rows(first_full)
    picked = jnp.take(leaf_inv, inverse, axis=1)
    leaf_x = lax.psum_scatter(
        jnp.einsum("rm,rk->mk", picked, leaf_z, preferred_element_type=jnp.float32).astype(
            jnp.bfloat16
        ),
        GRP,
        scatter_dimension=0,
        tiled=True,
    ).astype(jnp.float32)
    leaf_x = leaf_x - jnp.einsum(
        "rc,kc->rk", leaf_link, first_all, preferred_element_type=jnp.float32
    )
    return (leaf_x, jnp.stack(solution, axis=0))


def run_send(whole_ref, low_ref, high_ref, link_ref, fac_ref, out_0_ref, out_1_ref, kept_ref, crossing_ref):
    height, width = out_1_ref.shape
    out_0_ref[:height, :] = whole_ref[:, :width]
    out_1_ref[...] = whole_ref[:, width:]
    first = link_ref.shape[0]
    rows, cols = fac_ref.shape
    split = low_ref.shape[0]
    crossing = dot_nn(link_ref[:, :split], low_ref[...]) + dot_nn(link_ref[:, split:], high_ref[...])
    crossing_ref[...] = crossing
    tiles = (kept_ref.shape[0] - first) // rows
    factor = fac_ref[...].astype(F32)
    factor = jnp.concatenate([factor, jnp.zeros((rows, tiles * LANES - cols), F32)], axis=1)
    folded = [factor[:, tile * LANES : (tile + 1) * LANES] for tile in range(tiles)]
    folded = jnp.concatenate(folded, axis=0)
    me = lax.axis_index(GRP)
    kept_ref[first:, :] = jnp.concatenate([folded, folded], axis=1)
    out_0_ref[height + first :, :] = jnp.concatenate([folded, folded], axis=1).astype(BF16)
    for index, (mine, sent) in enumerate(((0, 1), (2, 3))):
        place = slice(index * LANES, (index + 1) * LANES)
        lanes = pl.ds(pl.multiple_of((me ^ mine) * LANES, LANES), LANES)
        kept_ref[:first, place] = crossing_ref[:, lanes]
        lanes = pl.ds(pl.multiple_of((me ^ sent) * LANES, LANES), LANES)
        out_0_ref[height : height + first, place] = crossing_ref[:, lanes].astype(BF16)


def run_leaf(kept_ref, x_ref, y_ref, sep_ref, dinv_ref, out_ref, *, rows, cols):
    levels, sep_block, _ = sep_ref.shape
    first = kept_ref.shape[0] - sep_block
    tiles = sep_block // rows
    me = lax.axis_index(GRP)
    x_part = x_ref[x_ref.shape[0] - first - sep_block :, :].astype(F32)
    y_part = y_ref[y_ref.shape[0] - first :, :].astype(F32)
    total = kept_ref[:first, :LANES] + x_part[:first, :LANES] + y_part[:, :LANES]
    out_ref[:first, :] = total.astype(BF16)
    for level in range(levels):
        out_ref[first + level * sep_block : first + (level + 1) * sep_block, :] = sep_ref[level]
    row_owner = lax.broadcasted_iota(jnp.int32, (sep_block, tiles * LANES), 0) // rows
    lane = lax.broadcasted_iota(jnp.int32, (sep_block, tiles * LANES), 1)
    factor = jnp.zeros((sep_block, tiles * LANES), F32)
    folds = (
        kept_ref[first:, :LANES],
        x_part[first:, :LANES],
        y_part[:sep_block, LANES:],
        y_part[sep_block : 2 * sep_block, LANES:],
    )
    for index, folded in enumerate(folds):
        block = [folded[tile * rows : (tile + 1) * rows, :] for tile in range(tiles)]
        block = jnp.concatenate(block, axis=1)
        tiled = jnp.concatenate([block] * (sep_block // rows), axis=0)
        factor = factor + jnp.where(row_owner == (me ^ index), tiled, 0.0)
    pivots = dinv_ref[...].astype(F32).T
    for level in range(levels):
        column = jnp.broadcast_to(pivots[:, level : level + 1], factor.shape)
        factor = jnp.where(lane == cols + level, column, factor)
    base = first + levels * sep_block
    for tile in range(tiles):
        out_ref[base + tile * sep_block : base + (tile + 1) * sep_block, :] = factor[
            :, tile * LANES : (tile + 1) * LANES
        ].astype(BF16)


def run_pair(own_ref, other_ref, out_ref, *, first, sep_block):
    is_odd = lax.axis_index(LEAF) % 2 == 1
    own = own_ref[...].astype(F32)
    other = other_ref[...].astype(F32)
    even = jnp.where(is_odd, other, own)
    odd = jnp.where(is_odd, own, other)
    crossing = even[0:first] + odd[0:first]
    for index in range((own.shape[0] - first) // sep_block):
        base = first + index * sep_block
        both = jnp.concatenate([even[base : base + sep_block], odd[base : base + sep_block]], axis=0)
        if index == 0:
            both = both - crossing
        out_ref[index * first : (index + 1) * first, :] = both.astype(BF16)


def run_tree(*refs, count, first, levels, sep_block, cols):
    pairs = refs[:count]
    first_ref, sol_ref, stage_ref, factor_ref, val_ref = refs[count:]
    leaf = lax.axis_index(LEAF)
    pair = leaf // 2
    nsep, width = factor_ref.shape
    for index, ref in enumerate(pairs):
        place = pl.ds(pl.multiple_of((pair ^ index) * first, first), first)
        for level in range(levels):
            stage_ref[level, place, :] = ref[level * first : (level + 1) * first, :]
        for tile in range(width // LANES):
            base = (levels + tile) * first
            factor_ref[place, tile * LANES : (tile + 1) * LANES] = ref[base : base + first, :]
    factor = factor_ref[...]
    column = lax.broadcasted_iota(jnp.int32, (width, nsep), 0)
    target = lax.broadcasted_iota(jnp.int32, (width, nsep), 1)
    row = lax.broadcasted_iota(jnp.int32, (nsep, nsep), 0)
    lane = lax.broadcasted_iota(jnp.int32, (nsep, nsep), 1)

    def block_diagonal(offset, size):
        choose = jnp.where(column == offset + target % size, 1.0, 0.0).astype(BF16)
        spread = dot_nn(factor, choose)
        return jnp.where(row // size == lane // size, spread, 0.0).astype(BF16)

    weights, couplings, z_blocks = [], [], []
    residual = stage_ref[0]
    for level in range(1, levels + 1):
        size = sep_block * 2**level
        offset = level_offset(sep_block, level)
        weight = block_diagonal(offset, size)
        coupling = None
        if level >= 2:
            coupling = block_diagonal(offset + size, size)
            residual = (stage_ref[level - 1].astype(F32) - dot_nn(coupling, residual)).astype(BF16)
        pick = lax.broadcasted_iota(jnp.int32, (width, LANES), 0) == cols + level - 1
        scale = dot_nn(factor, jnp.where(pick, 1.0, 0.0).astype(BF16))
        z_blocks.append((scale * dot_nn(weight, residual)).astype(BF16))
        weights.append(weight)
        couplings.append(coupling)
    current = None
    for level in range(levels, 0, -1):
        value = dot_tn(weights[level - 1], z_blocks[level - 1])
        if level < levels:
            value = value - dot_tn(couplings[level], current.astype(BF16))
        current = value
        val_ref[...] = value
        sol_ref[level - 1] = val_ref[pl.ds(pl.multiple_of(leaf * sep_block, sep_block), sep_block), :]
    first_ref[...] = val_ref[pl.ds(pl.multiple_of(pair * first, first), first), :].astype(BF16)


def run_arrange(dest_ref, factor_ref, *refs):
    outs, (turned_ref, sorted_ref) = refs[:-2], refs[-2:]
    step = pl.program_id(0)
    rows, width = factor_ref.shape
    tiles = rows // LANES
    turned = factor_ref[...].astype(F32).T
    for tile in range(tiles):
        turned_ref[pl.ds(tile, width, stride=tiles), :] = turned[:, tile * LANES : (tile + 1) * LANES]

    def move(group, carry):
        for lane in range(UNROLL):
            source = group * UNROLL + lane
            target = dest_ref[step * width + source]
            sorted_ref[pl.ds(pl.multiple_of(target * tiles, tiles), tiles), :] = turned_ref[
                pl.ds(pl.multiple_of(source * tiles, tiles), tiles), :
            ]
        return carry

    lax.fori_loop(0, width // UNROLL, move, 0)

    @pl.when(step == pl.num_programs(0) - 1)
    def _():
        for index, out_ref in enumerate(outs):
            count = out_ref.shape[0]
            chunk = min(count, 256)

            def write(part, carry, index=index, out_ref=out_ref, count=count, chunk=chunk):
                base = index * count * tiles + part * chunk * tiles
                for tile in range(tiles):
                    out_ref[
                        pl.ds(pl.multiple_of(part * chunk, chunk), chunk),
                        tile * LANES : (tile + 1) * LANES,
                    ] = sorted_ref[pl.ds(base + tile, chunk, stride=tiles), :].astype(BF16)
                return carry

            lax.fori_loop(0, count // chunk, write, 0)


def arrange(factor, dest, count):
    rows, cols = factor.shape
    width = math.gcd(cols, 4 * LANES)
    part = cols // count
    return call(
        run_arrange,
        (dest, pltpu.with_memory_space_constraint(factor, pltpu.HBM)),
        [smem(), pl.BlockSpec((rows, width), lambda step: (0, step))],
        [jax.ShapeDtypeStruct((part, rows), BF16)] * count,
        grant=26,
        grid=(cols // width,),
        scratch_shapes=[
            pltpu.VMEM((width * rows // LANES, LANES), F32),
            pltpu.VMEM((cols * rows // LANES, LANES), F32),
        ],
    )


def run_split(rhs_ref, out_ref, sem, *, top):
    copy = pltpu.make_async_copy(rhs_ref.at[pl.ds(top, out_ref.shape[0]), :], out_ref, sem)
    copy.start()
    copy.wait()


def run_cut(whole_ref, *outs):
    for part, ref in enumerate(outs):
        height, width = ref.shape
        ref[...] = whole_ref[:height, part * width : (part + 1) * width]


def row_blocks(rows):
    height = math.gcd(rows, 2 * LANES)
    return [slice(top, top + height) for top in range(0, rows, height)]


def run_forward(own_ref, x_ref, y_ref, far_ref, dinv_ref, *refs):
    pieces, (out_0_ref, out_1_ref, turned_ref, scale_ref, factor_ref, loads_ref) = refs[:-6], refs[-6:]
    rows = own_ref.shape[0]
    width = out_0_ref.shape[1]
    for index, ref in enumerate((own_ref, x_ref, y_ref)):
        factor_ref[index * rows : (index + 1) * rows, :] = ref[...]
    start = 0
    for ref in pieces:
        loads_ref[start : start + ref.shape[0], :] = ref[...]
        start += ref.shape[0]
    for block in row_blocks(rows):
        product = dot_tn(factor_ref[:, block], loads_ref[...])
        out_0_ref[block, :] = product[:, :width]
        out_1_ref[block, :] = product[:, width:]
    turned_ref[...] = far_ref[...].T
    pivots = dinv_ref[...].astype(F32)
    for tile in range(pivots.shape[0]):
        block = slice(tile * LANES, (tile + 1) * LANES)
        scale_ref[block, :] = jnp.broadcast_to(pivots[tile : tile + 1, :], (LANES, LANES)).T


def run_far(far_ref, turned_ref, low_ref, high_ref, near_ref, scale_ref, *refs, first):
    kept = refs[:-4]
    z_ref, relay_low_ref, relay_high_ref, loads_ref = refs[-4:]
    split, half = low_ref.shape[0], relay_low_ref.shape[0]
    rows, width = z_ref.shape
    rest = rows - split
    loads_ref[:split, :] = low_ref[...]
    loads_ref[split:, :] = high_ref[:rest, :]
    for block in row_blocks(rows):
        leaf_y = near_ref[block, :] + dot_nn(turned_ref[block, :], loads_ref[...])
        scale = jnp.concatenate([scale_ref[block, :]] * (width // LANES), axis=1)
        z_ref[block, :] = (scale * leaf_y).astype(BF16)
    for block in row_blocks(half):
        relay_low_ref[block, :] = dot_nn(far_ref[block, :], z_ref[...]).astype(BF16)
    for block in row_blocks(half):
        below = slice(half + block.start, half + block.stop)
        relay_high_ref[block, :] = dot_nn(far_ref[below, :], z_ref[...]).astype(BF16)
    for kept_ref in kept:
        crossing = kept_ref[:first, LANES:] + high_ref[rest : rest + first, LANES:].astype(F32)
        relay_high_ref[half:, :LANES] = crossing.astype(BF16)
        folds = [kept_ref[first:, LANES:], high_ref[rest + first :, :LANES].astype(F32)]
        relay_high_ref[half:, LANES:] = jnp.concatenate(folds, axis=0).astype(BF16)


def run_near(own_ref, x_ref, y_ref, z_0_ref, z_1_ref, x_low_ref, y_high_ref, x_high_ref, y_low_ref, out_ref, z_ref):
    half, split = x_low_ref.shape[0], z_0_ref.shape[1]
    z_ref[:, :split] = z_0_ref[...]
    z_ref[:, split:] = z_1_ref[...]
    for factor_ref, top, ref in (
        (x_ref, 0, x_low_ref),
        (y_ref, half, y_high_ref),
        (x_ref, half, x_high_ref),
        (y_ref, 0, y_low_ref),
        (own_ref, 0, out_ref),
    ):
        for block in row_blocks(ref.shape[0]):
            part = slice(top + block.start, top + block.stop)
            ref[block, :] = dot_nn(factor_ref[part, :], z_ref[...]).astype(ref.dtype)


def run_add(near_ref, relay_0_ref, relay_1_ref, out_0_ref, out_1_ref):
    half = near_ref.shape[0]
    relay = jnp.concatenate([relay_0_ref[:half, :], relay_1_ref[:half, :]], axis=1).astype(F32)
    total = (near_ref[...] + relay).astype(BF16)
    split = out_0_ref.shape[1]
    out_0_ref[...] = total[:, :split]
    out_1_ref[...] = total[:, split:]


def run_base(own_ref, link_ref, mine_ref, x_ref, y_ref, d_ref, x_low_ref, y_high_ref, out_0_ref, out_1_ref, first_ref):
    half = x_low_ref.shape[0]
    me = lax.axis_index(GRP)
    for mask, ref in enumerate((mine_ref, x_ref, y_ref, d_ref)):
        lanes = pl.ds(pl.multiple_of((me ^ mask) * LANES, LANES), LANES)
        first_ref[:, lanes] = ref[...]
    start = 0
    for ref in (out_0_ref, out_1_ref):
        cols = slice(start, start + ref.shape[1])
        start += ref.shape[1]
        ref[...] = own_ref[:, cols] - dot_tn(link_ref[...], first_ref[:, cols])
        ref[:half, :] += x_low_ref[:, cols].astype(F32)
        ref[half:, :] += y_high_ref[:, cols].astype(F32)


def run_last(base_ref, low_ref, high_ref, out_ref, sum_ref, sems, *, start, chunks):
    rows, width = base_ref.shape
    half, height = low_ref.shape[0], rows // chunks
    copies = []
    for chunk in range(chunks):
        top = chunk * height
        place = slice(top, top + height)
        piece_ref, base = (low_ref, top) if top < half else (high_ref, top - half)
        sum_ref[place, :] = base_ref[place, :] + piece_ref[base : base + height, :].astype(F32)
        copy = pltpu.make_async_copy(
            sum_ref.at[pl.ds(top, height), :],
            out_ref.at[pl.ds(top, height), pl.ds(start, width)],
            sems.at[chunk],
        )
        copy.start()
        copies.append(copy)
    for copy in copies:
        copy.wait()


def local_pairs(leaf_rhs, leaf_inv, ordering, leaf_dinv, leaf_link, sep_rhs, sep_factor, sep_dinv):
    rows, width = leaf_rhs.shape
    half, split = rows // 2, rows // 16 * 7
    group = lax.axis_size(GRP)
    levels, slice_width, sep_block = sep_rhs.shape
    first = leaf_link.shape[1]
    fac_rows, cols = sep_factor.shape
    tiles = sep_block // fac_rows
    parts = range(2)
    me = lax.axis_index(GRP).astype(jnp.int32)
    link_turned = leaf_link.T

    def bf16(height, breadth):
        return jax.ShapeDtypeStruct((height, breadth), BF16)

    def f32(height, breadth):
        return jax.ShapeDtypeStruct((height, breadth), F32)

    x_all = exchange(leaf_rhs, GRP, 1)
    loads = pltpu.with_memory_space_constraint(leaf_rhs, pltpu.HBM)
    high, low = (
        call(
            functools.partial(run_split, top=top),
            (loads,),
            [pl.BlockSpec(memory_space=pltpu.HBM)],
            bf16(height, width),
            scratch_shapes=[pltpu.SemaphoreType.DMA],
        )
        for top, height in ((split, rows - split), (0, split))
    )
    y_high = exchange(high, GRP, 2)
    y_low = exchange(low, GRP, 2)
    dest = (ordering[0] // rows ^ me) * rows + ordering[0] % rows
    blocks = arrange(leaf_inv, dest, group)

    *high_cut, kept = call(
        run_send,
        (y_high, low, high, link_turned, sep_factor),
        [vmem()] * 5,
        [
            bf16(rows - split + first + sep_block, width // 2),
            bf16(rows - split, width // 2),
            f32(first + sep_block, 2 * LANES),
        ],
        after=(blocks[0],),
        scratch_shapes=[pltpu.VMEM((first, width), F32)],
    )
    d_high = [exchange(high_cut[part], GRP, 1) for part in parts]
    low_cut = call(run_cut, (x_all,), [vmem()], [bf16(split, width // 2)] * 2, after=(blocks[0],))
    d_low = [exchange(low_cut[part], GRP, 2) for part in parts]

    *part_y, turned, scale = call(
        run_forward,
        (*blocks, leaf_dinv.reshape(-1, LANES), low, high, x_all, y_low, y_high),
        [vmem()] * 10,
        [f32(rows, width // 2)] * 2 + [bf16(rows, rows), f32(rows, LANES)],
        scratch_shapes=[pltpu.VMEM((3 * rows, rows), BF16), pltpu.VMEM((3 * rows, width), BF16)],
    )
    leaf_z, relay_low, relay_high = [], [], []
    for part in parts:
        shared = (kept,) if part == 0 else ()
        z_part, far_low, far_high = call(
            functools.partial(run_far, first=first),
            (
                blocks[3],
                turned,
                d_low[part],
                d_high[part],
                part_y[part],
                scale,
                *shared,
            ),
            [vmem()] * (6 + len(shared)),
            (
                bf16(rows, width // 2),
                bf16(half, width // 2),
                bf16(half + first * len(shared), width // 2),
            ),
            scratch_shapes=[pltpu.VMEM((rows, width // 2), BF16)],
        )
        leaf_z.append(z_part)
        relay_low.append(exchange(far_low, GRP, 1))
        relay_high.append(exchange(far_high, GRP, 2))

    near_x_low, near_y_high, near_x_high, near_y_low, own = call(
        run_near,
        (*blocks[:3], *leaf_z),
        [vmem()] * 5,
        [bf16(half, width)] * 2 + [f32(half, width)] * 2 + [f32(rows, width)],
        scratch_shapes=[pltpu.VMEM((rows, width), BF16)],
    )
    leaf_block = call(
        functools.partial(run_leaf, rows=fac_rows, cols=cols),
        (kept, d_high[0], relay_high[0], jnp.swapaxes(sep_rhs, 1, 2), sep_dinv),
        [vmem()] * 5,
        bf16(first + (levels + tiles) * sep_block, LANES),
        after=(own,),
    )
    partner = exchange(leaf_block, LEAF, 1)
    sum_x_low = exchange(near_x_low, GRP, 1)
    sum_y_high = exchange(near_y_high, GRP, 2)
    pair_block = call(
        functools.partial(run_pair, first=first, sep_block=sep_block),
        (leaf_block, partner),
        [vmem(), vmem()],
        bf16((levels + tiles) * first, LANES),
    )
    count = lax.axis_size(LEAF) // 2
    pairs = [pair_block] + [exchange(pair_block, LEAF, 2 * mask) for mask in range(1, count)]
    nsep = count * first
    first_here, sep_turned = call(
        functools.partial(
            run_tree, count=count, first=first, levels=levels, sep_block=sep_block, cols=cols
        ),
        pairs,
        [vmem()] * count,
        (bf16(first, LANES), jax.ShapeDtypeStruct((levels, sep_block, slice_width), F32)),
        scratch_shapes=[
            pltpu.VMEM((levels, nsep, LANES), BF16),
            pltpu.VMEM((nsep, tiles * LANES), BF16),
            pltpu.VMEM((nsep, LANES), F32),
        ],
    )
    first_all = [first_here] + [exchange(first_here, GRP, mask) for mask in range(1, group)]
    breadths = (width // 4 * 3, width // 4)
    into = [bf16(half, breadth) for breadth in breadths]
    x_sums = call(run_add, (near_x_high, *relay_high), [vmem()] * 3, into)
    y_sums = call(run_add, (near_y_low, *relay_low), [vmem()] * 3, into)
    sum_x_high = [exchange(x_sums[part], GRP, 1) for part in parts]
    sum_y_low = [exchange(y_sums[part], GRP, 2) for part in parts]
    base = call(
        run_base,
        (own, link_turned, *first_all, sum_x_low, sum_y_high),
        [vmem()] * (4 + group),
        [f32(rows, breadth) for breadth in breadths],
        scratch_shapes=[pltpu.VMEM((first, width), BF16)],
    )
    chunks = 4
    leaf_x, start = (), 0
    for part, breadth in zip(parts, breadths):
        leaf_x = (
            call(
                functools.partial(run_last, start=start, chunks=chunks),
                (base[part], sum_y_low[part], sum_x_high[part]),
                [vmem()] * 3,
                f32(rows, width),
                after=leaf_x,
                out_specs=pl.BlockSpec(memory_space=pltpu.HBM),
                scratch_shapes=[pltpu.VMEM((rows, breadth), F32), pltpu.SemaphoreType.DMA((chunks,))],
                input_output_aliases={0: 0} if leaf_x else {},
            ),
        )
        start += breadth
    return leaf_x[0], jnp.swapaxes(sep_turned, 1, 2)


def fits(leaf_rhs, leaf_inv, sep_rhs, sep_factor, leaf_link):
    levels, slice_width, sep_block = sep_rhs.shape
    width = leaf_rhs.shape[1]
    count = lax.axis_size(GRP)
    leaves = lax.axis_size(LEAF)
    return (
        count == 2**2
        and leaf_inv.shape[1] == count * leaf_rhs.shape[0]
        and leaf_rhs.shape[0] % 256 == 0
        and leaf_rhs.shape[0] // LANES == 8
        and leaf_link.shape[1] == 2 * sep_block
        and sep_block % 16 == 0
        and slice_width % 128 == 0
        and sep_block % sep_factor.shape[0] == 0
        and sep_factor.shape[1] + levels <= sep_block // sep_factor.shape[0] * LANES
        and width == count * slice_width
        and slice_width == LANES
        and width % (leaves * sep_block) == 0
    )


def local(*args):
    leaf_rhs, leaf_inv, _, _, leaf_link, sep_rhs, sep_factor, _ = args
    if fits(leaf_rhs, leaf_inv, sep_rhs, sep_factor, leaf_link):
        return local_pairs(*args)
    return local_general(*args)


def solution(mesh):
    placed = (
        P((LEAF, GRP), None),
        P((LEAF, GRP), None),
        P(LEAF, None),
        P((LEAF, GRP)),
        P((LEAF, GRP), None),
        P(None, GRP, LEAF),
        P((LEAF, GRP), None),
        P(None, LEAF),
    )
    return jax.shard_map(
        local,
        mesh=mesh,
        in_specs=placed,
        out_specs=(P((LEAF, GRP), None), P(None, GRP, LEAF)),
        check_vma=False,
    )
```

```python
import functools
import math

import jax
import jax.numpy as jnp
from jax import lax
from jax.experimental import pallas as pl
from jax.experimental.pallas import tpu as pltpu
from jax.sharding import PartitionSpec as P


F32 = jnp.float32
BF16 = jnp.bfloat16
LANES = 128
GRP, LEAF = "grp", "leaf"
UNROLL = 32


def group_mask(index, leaf):
    return index + (0, 1, -1, 0)[index] * (leaf % 2)


def exchange(block, axis, mask):
    count = lax.axis_size(axis)
    if axis == LEAF:
        return lax.ppermute(block, axis, [(low, low ^ mask) for low in range(count)])
    pairs = []
    for leaf in range(lax.axis_size(LEAF)):
        for low in range(count):
            base = leaf * count
            pairs.append((base + low, base + (low ^ group_mask(mask, leaf))))
    return lax.ppermute(block, (LEAF, axis), pairs)


def owner(index):
    return lax.axis_index(GRP) ^ group_mask(index, lax.axis_index(LEAF))


def level_offset(sep_block, tree_level):
    if tree_level >= 2:
        return sep_block * (2 ** (tree_level + 1) - 6)
    return 0


def dot_tn(lhs, rhs):
    return lax.dot_general(lhs, rhs, (((0,), (0,)), ((), ())), preferred_element_type=F32)


def dot_nn(lhs, rhs):
    return jnp.dot(lhs, rhs, preferred_element_type=F32)


def vmem():
    return pl.BlockSpec(memory_space=pltpu.VMEM)


def smem():
    return pl.BlockSpec(memory_space=pltpu.SMEM)


def call(body, ops, specs, out_shape, after=(), grant=16, **rest):
    skip = len(after)
    rest.setdefault("out_specs", jax.tree.map(lambda _: vmem(), out_shape))

    def skipping(*refs):
        body(*refs[skip:])

    return pl.pallas_call(
        skipping,
        out_shape=out_shape,
        in_specs=[pl.BlockSpec(memory_space=pl.ANY)] * skip + specs,
        compiler_params=pltpu.CompilerParams(vmem_limit_bytes=grant * 2**20),
        **rest,
    )(*after, *ops)


def from_partner(block, axis, distance):
    count = lax.axis_size(axis)
    route = []
    for low in range(count):
        high = low | 1 << distance
        if high != low and high < count:
            route += [(low, high), (high, low)]
    return lax.ppermute(block, axis, route)


def partner(values, level_bit):
    return from_partner(values.astype(jnp.bfloat16), LEAF, level_bit).astype(values.dtype)


def leaf_bit(level_bit):
    return jnp.right_shift(lax.axis_index(LEAF), level_bit) % 2


def spread(values, first_bit, last_bit):
    for level_bit in range(first_bit, last_bit):
        partner_rows = partner(values.astype(jnp.float32), level_bit).astype(jnp.bfloat16)
        low_first = jnp.concatenate([values, partner_rows], axis=-1)
        high_first = jnp.concatenate([partner_rows, values], axis=-1)
        values = jnp.where(leaf_bit(level_bit) == 0, low_first, high_first)
    return values


def halve_sum(values, bit_list):
    for level_bit in bit_list:
        half_width = values.shape[-1] // 2
        low_half = values[..., :half_width]
        high_half = values[..., half_width:]
        is_upper = leaf_bit(level_bit) == 1
        keep_half = jnp.where(is_upper, high_half, low_half)
        send_half = jnp.where(is_upper, low_half, high_half)
        values = keep_half + partner(send_half, level_bit)
    return values


def group_rows(values):
    return lax.all_gather(values, GRP, axis=0, tiled=True)


def level_width(sep_block, tree_level):
    if tree_level >= 2:
        return 2 * sep_block * 2**tree_level
    return sep_block * 2**tree_level


def local_general(leaf_rhs, leaf_inv, ordering, leaf_dinv, leaf_link, sep_rhs, sep_factor, sep_dinv):
    levels = sep_rhs.shape[0]
    sep_block = sep_rhs.shape[2]
    inverse = jnp.argsort(ordering[0])
    picked = jnp.take(leaf_inv, inverse, axis=1)
    leaf_y = jnp.dot(
        picked,
        lax.all_gather(leaf_rhs, GRP, axis=0, tiled=True),
        preferred_element_type=jnp.float32,
    )
    partial_sum = jnp.einsum("rk,rc->kc", leaf_rhs, leaf_link, preferred_element_type=jnp.float32)
    crossing = lax.psum_scatter(
        partial_sum.astype(jnp.bfloat16), GRP, scatter_dimension=0, tiled=True
    ).astype(jnp.float32)
    leaf_z = (leaf_dinv.astype(jnp.float32)[:, None] * leaf_y).astype(jnp.bfloat16)
    crossing = halve_sum(crossing, [0])
    sep_r = (sep_rhs[0].astype(jnp.float32) - crossing).astype(jnp.bfloat16)
    gathered = group_rows(sep_factor)

    def level_rows(tree_level):
        offset = level_offset(sep_block, tree_level)
        return lax.slice_in_dim(
            gathered, offset, offset + level_width(sep_block, tree_level), axis=1
        )

    z_blocks = []
    full_prev = sep_r
    for tree_level in range(1, levels + 1):
        rows_here = level_rows(tree_level)
        size_here = sep_block * 2**tree_level
        if tree_level >= 2:
            children = spread(full_prev, tree_level - 1, tree_level)
            link_rows = rows_here[:, size_here:]
            coupled = jnp.einsum(
                "kc,qc->kq", children, link_rows, preferred_element_type=jnp.float32
            )
            sep_r = (sep_rhs[tree_level - 1].astype(jnp.float32) - coupled).astype(jnp.bfloat16)
        full_prev = spread(sep_r, 0, tree_level)
        sep_y = jnp.einsum(
            "kc,qc->kq", full_prev, rows_here[:, :size_here], preferred_element_type=jnp.float32
        )
        z_blocks.append(
            (sep_dinv[tree_level - 1].astype(jnp.float32)[None, :] * sep_y).astype(jnp.bfloat16)
        )
    solution = [None] * levels
    upper_rows = level_rows(levels)
    size_top = sep_block * 2**levels
    partial_value = jnp.einsum(
        "kq,qc->kc",
        z_blocks[levels - 1],
        upper_rows[:, :size_top],
        preferred_element_type=jnp.float32,
    )
    current = halve_sum(partial_value, list(range(levels - 1, -1, -1)))
    solution[levels - 1] = current
    for tree_level in range(levels - 1, 0, -1):
        size_here = sep_block * 2**tree_level
        link_rows = upper_rows[:, 2 * size_here :]
        rows_here = level_rows(tree_level)
        pushed = -jnp.einsum(
            "kq,qc->kc", current.astype(jnp.bfloat16), link_rows, preferred_element_type=jnp.float32
        )
        pushed = halve_sum(pushed, [tree_level])
        pushed = pushed + jnp.einsum(
            "kq,qc->kc",
            z_blocks[tree_level - 1],
            rows_here[:, :size_here],
            preferred_element_type=jnp.float32,
        )
        current = halve_sum(pushed, list(range(tree_level - 1, -1, -1)))
        solution[tree_level - 1] = current
        upper_rows = rows_here
    first_full = spread(current.astype(jnp.bfloat16), 0, 1)
    first_all = group_rows(first_full)
    picked = jnp.take(leaf_inv, inverse, axis=1)
    leaf_x = lax.psum_scatter(
        jnp.einsum("rm,rk->mk", picked, leaf_z, preferred_element_type=jnp.float32).astype(
            jnp.bfloat16
        ),
        GRP,
        scatter_dimension=0,
        tiled=True,
    ).astype(jnp.float32)
    leaf_x = leaf_x - jnp.einsum(
        "rc,kc->rk", leaf_link, first_all, preferred_element_type=jnp.float32
    )
    return (leaf_x, jnp.stack(solution, axis=0))


def run_send(whole_ref, low_ref, high_ref, link_ref, fac_ref, out_0_ref, out_1_ref, kept_ref, crossing_ref):
    height, width = out_1_ref.shape
    out_0_ref[:height, :] = whole_ref[:, :width]
    out_1_ref[...] = whole_ref[:, width:]
    first = link_ref.shape[0]
    rows, cols = fac_ref.shape
    split = low_ref.shape[0]
    crossing = dot_nn(link_ref[:, :split], low_ref[...]) + dot_nn(link_ref[:, split:], high_ref[...])
    crossing_ref[...] = crossing
    tiles = (kept_ref.shape[0] - first) // rows
    factor = fac_ref[...].astype(F32)
    factor = jnp.concatenate([factor, jnp.zeros((rows, tiles * LANES - cols), F32)], axis=1)
    folded = [factor[:, tile * LANES : (tile + 1) * LANES] for tile in range(tiles)]
    folded = jnp.concatenate(folded, axis=0)
    kept_ref[first:, :] = jnp.concatenate([folded, folded], axis=1)
    out_0_ref[height + first :, :] = jnp.concatenate([folded, folded], axis=1).astype(BF16)
    for index, (mine, sent) in enumerate(((0, 1), (2, 3))):
        place = slice(index * LANES, (index + 1) * LANES)
        lanes = pl.ds(pl.multiple_of(owner(mine) * LANES, LANES), LANES)
        kept_ref[:first, place] = crossing_ref[:, lanes]
        lanes = pl.ds(pl.multiple_of(owner(sent) * LANES, LANES), LANES)
        out_0_ref[height : height + first, place] = crossing_ref[:, lanes].astype(BF16)


def run_leaf(kept_ref, x_ref, y_ref, sep_ref, dinv_ref, out_ref, *, rows, cols):
    levels, sep_block, _ = sep_ref.shape
    first = kept_ref.shape[0] - sep_block
    tiles = sep_block // rows
    x_part = x_ref[x_ref.shape[0] - first - sep_block :, :].astype(F32)
    y_part = y_ref[y_ref.shape[0] - first :, :].astype(F32)
    total = kept_ref[:first, :LANES] + x_part[:first, :LANES] + y_part[:, :LANES]
    out_ref[:first, :] = total.astype(BF16)
    for level in range(levels):
        out_ref[first + level * sep_block : first + (level + 1) * sep_block, :] = sep_ref[level]
    row_owner = lax.broadcasted_iota(jnp.int32, (sep_block, tiles * LANES), 0) // rows
    lane = lax.broadcasted_iota(jnp.int32, (sep_block, tiles * LANES), 1)
    factor = jnp.zeros((sep_block, tiles * LANES), F32)
    folds = (
        kept_ref[first:, :LANES],
        x_part[first:, :LANES],
        y_part[:sep_block, LANES:],
        y_part[sep_block : 2 * sep_block, LANES:],
    )
    for index, folded in enumerate(folds):
        block = [folded[tile * rows : (tile + 1) * rows, :] for tile in range(tiles)]
        block = jnp.concatenate(block, axis=1)
        tiled = jnp.concatenate([block] * (sep_block // rows), axis=0)
        factor = factor + jnp.where(row_owner == owner(index), tiled, 0.0)
    pivots = dinv_ref[...].astype(F32).T
    for level in range(levels):
        column = jnp.broadcast_to(pivots[:, level : level + 1], factor.shape)
        factor = jnp.where(lane == cols + level, column, factor)
    base = first + levels * sep_block
    for tile in range(tiles):
        out_ref[base + tile * sep_block : base + (tile + 1) * sep_block, :] = factor[
            :, tile * LANES : (tile + 1) * LANES
        ].astype(BF16)


def run_pair(own_ref, other_ref, out_ref, *, first, sep_block):
    is_odd = lax.axis_index(LEAF) % 2 == 1
    own = own_ref[...].astype(F32)
    other = other_ref[...].astype(F32)
    even = jnp.where(is_odd, other, own)
    odd = jnp.where(is_odd, own, other)
    crossing = even[0:first] + odd[0:first]
    for index in range((own.shape[0] - first) // sep_block):
        base = first + index * sep_block
        both = jnp.concatenate([even[base : base + sep_block], odd[base : base + sep_block]], axis=0)
        if index == 0:
            both = both - crossing
        out_ref[index * first : (index + 1) * first, :] = both.astype(BF16)


def run_tree(*refs, count, first, levels, sep_block, cols):
    pairs = refs[:count]
    first_ref, sol_ref, stage_ref, factor_ref, val_ref = refs[count:]
    leaf = lax.axis_index(LEAF)
    pair = leaf // 2
    nsep, width = factor_ref.shape
    for index, ref in enumerate(pairs):
        place = pl.ds(pl.multiple_of((pair ^ index) * first, first), first)
        for level in range(levels):
            stage_ref[level, place, :] = ref[level * first : (level + 1) * first, :]
        for tile in range(width // LANES):
            base = (levels + tile) * first
            factor_ref[place, tile * LANES : (tile + 1) * LANES] = ref[base : base + first, :]
    factor = factor_ref[...]
    column = lax.broadcasted_iota(jnp.int32, (width, nsep), 0)
    target = lax.broadcasted_iota(jnp.int32, (width, nsep), 1)
    row = lax.broadcasted_iota(jnp.int32, (nsep, nsep), 0)
    lane = lax.broadcasted_iota(jnp.int32, (nsep, nsep), 1)

    def block_diagonal(offset, size):
        choose = jnp.where(column == offset + target % size, 1.0, 0.0).astype(BF16)
        spread = dot_nn(factor, choose)
        return jnp.where(row // size == lane // size, spread, 0.0).astype(BF16)

    weights, couplings, z_blocks = [], [], []
    residual = stage_ref[0]
    for level in range(1, levels + 1):
        size = sep_block * 2**level
        offset = level_offset(sep_block, level)
        weight = block_diagonal(offset, size)
        coupling = None
        if level >= 2:
            coupling = block_diagonal(offset + size, size)
            residual = (stage_ref[level - 1].astype(F32) - dot_nn(coupling, residual)).astype(BF16)
        pick = lax.broadcasted_iota(jnp.int32, (width, LANES), 0) == cols + level - 1
        scale = dot_nn(factor, jnp.where(pick, 1.0, 0.0).astype(BF16))
        z_blocks.append((scale * dot_nn(weight, residual)).astype(BF16))
        weights.append(weight)
        couplings.append(coupling)
    current = None
    for level in range(levels, 0, -1):
        value = dot_tn(weights[level - 1], z_blocks[level - 1])
        if level < levels:
            value = value - dot_tn(couplings[level], current.astype(BF16))
        current = value
        val_ref[...] = value
        sol_ref[level - 1] = val_ref[pl.ds(pl.multiple_of(leaf * sep_block, sep_block), sep_block), :]
    first_ref[...] = val_ref[pl.ds(pl.multiple_of(pair * first, first), first), :].astype(BF16)


def run_arrange(dest_ref, factor_ref, *refs):
    outs, (turned_ref, sorted_ref) = refs[:-2], refs[-2:]
    step = pl.program_id(0)
    rows, width = factor_ref.shape
    tiles = rows // LANES
    turned = factor_ref[...].astype(F32).T
    for tile in range(tiles):
        turned_ref[pl.ds(tile, width, stride=tiles), :] = turned[:, tile * LANES : (tile + 1) * LANES]

    def move(group, carry):
        for lane in range(UNROLL):
            source = group * UNROLL + lane
            target = dest_ref[step * width + source]
            sorted_ref[pl.ds(pl.multiple_of(target * tiles, tiles), tiles), :] = turned_ref[
                pl.ds(pl.multiple_of(source * tiles, tiles), tiles), :
            ]
        return carry

    lax.fori_loop(0, width // UNROLL, move, 0)

    @pl.when(step == pl.num_programs(0) - 1)
    def _():
        for index, out_ref in enumerate(outs):
            count = out_ref.shape[0]
            chunk = min(count, 256)

            def write(part, carry, index=index, out_ref=out_ref, count=count, chunk=chunk):
                base = index * count * tiles + part * chunk * tiles
                for tile in range(tiles):
                    out_ref[
                        pl.ds(pl.multiple_of(part * chunk, chunk), chunk),
                        tile * LANES : (tile + 1) * LANES,
                    ] = sorted_ref[pl.ds(base + tile, chunk, stride=tiles), :].astype(BF16)
                return carry

            lax.fori_loop(0, count // chunk, write, 0)


def arrange(factor, dest, count):
    rows, cols = factor.shape
    width = math.gcd(cols, 4 * LANES)
    part = cols // count
    return call(
        run_arrange,
        (dest, pltpu.with_memory_space_constraint(factor, pltpu.HBM)),
        [smem(), pl.BlockSpec((rows, width), lambda step: (0, step))],
        [jax.ShapeDtypeStruct((part, rows), BF16)] * count,
        grant=26,
        grid=(cols // width,),
        scratch_shapes=[
            pltpu.VMEM((width * rows // LANES, LANES), F32),
            pltpu.VMEM((cols * rows // LANES, LANES), F32),
        ],
    )


def run_split(rhs_ref, out_ref, sem, *, top):
    copy = pltpu.make_async_copy(rhs_ref.at[pl.ds(top, out_ref.shape[0]), :], out_ref, sem)
    copy.start()
    copy.wait()


def run_cut(whole_ref, *outs):
    for part, ref in enumerate(outs):
        height, width = ref.shape
        ref[...] = whole_ref[:height, part * width : (part + 1) * width]


def row_blocks(rows):
    height = math.gcd(rows, 2 * LANES)
    return [slice(top, top + height) for top in range(0, rows, height)]


def run_forward(own_ref, x_ref, y_ref, far_ref, dinv_ref, *refs):
    pieces, (out_0_ref, out_1_ref, turned_ref, scale_ref, factor_ref, loads_ref) = refs[:-6], refs[-6:]
    rows = own_ref.shape[0]
    width = out_0_ref.shape[1]
    for index, ref in enumerate((own_ref, x_ref, y_ref)):
        factor_ref[index * rows : (index + 1) * rows, :] = ref[...]
    start = 0
    for ref in pieces:
        loads_ref[start : start + ref.shape[0], :] = ref[...]
        start += ref.shape[0]
    for block in row_blocks(rows):
        product = dot_tn(factor_ref[:, block], loads_ref[...])
        out_0_ref[block, :] = product[:, :width]
        out_1_ref[block, :] = product[:, width:]
    turned_ref[...] = far_ref[...].T
    pivots = dinv_ref[...].astype(F32)
    for tile in range(pivots.shape[0]):
        block = slice(tile * LANES, (tile + 1) * LANES)
        scale_ref[block, :] = jnp.broadcast_to(pivots[tile : tile + 1, :], (LANES, LANES)).T


def run_far(far_ref, turned_ref, low_ref, high_ref, near_ref, scale_ref, *refs, first):
    kept = refs[:-4]
    z_ref, relay_low_ref, relay_high_ref, loads_ref = refs[-4:]
    split, half = low_ref.shape[0], relay_low_ref.shape[0]
    rows, width = z_ref.shape
    rest = rows - split
    loads_ref[:split, :] = low_ref[...]
    loads_ref[split:, :] = high_ref[:rest, :]
    for block in row_blocks(rows):
        leaf_y = near_ref[block, :] + dot_nn(turned_ref[block, :], loads_ref[...])
        scale = jnp.concatenate([scale_ref[block, :]] * (width // LANES), axis=1)
        z_ref[block, :] = (scale * leaf_y).astype(BF16)
    for block in row_blocks(half):
        relay_low_ref[block, :] = dot_nn(far_ref[block, :], z_ref[...]).astype(BF16)
    for block in row_blocks(half):
        below = slice(half + block.start, half + block.stop)
        relay_high_ref[block, :] = dot_nn(far_ref[below, :], z_ref[...]).astype(BF16)
    for kept_ref in kept:
        crossing = kept_ref[:first, LANES:] + high_ref[rest : rest + first, LANES:].astype(F32)
        relay_high_ref[half:, :LANES] = crossing.astype(BF16)
        folds = [kept_ref[first:, LANES:], high_ref[rest + first :, :LANES].astype(F32)]
        relay_high_ref[half:, LANES:] = jnp.concatenate(folds, axis=0).astype(BF16)


def run_near(own_ref, x_ref, y_ref, z_0_ref, z_1_ref, x_low_ref, y_high_ref, x_high_ref, y_low_ref, out_ref, z_ref):
    half, split = x_low_ref.shape[0], z_0_ref.shape[1]
    z_ref[:, :split] = z_0_ref[...]
    z_ref[:, split:] = z_1_ref[...]
    for factor_ref, top, ref in (
        (x_ref, 0, x_low_ref),
        (y_ref, half, y_high_ref),
        (x_ref, half, x_high_ref),
        (y_ref, 0, y_low_ref),
        (own_ref, 0, out_ref),
    ):
        for block in row_blocks(ref.shape[0]):
            part = slice(top + block.start, top + block.stop)
            ref[block, :] = dot_nn(factor_ref[part, :], z_ref[...]).astype(ref.dtype)


def run_add(near_ref, relay_0_ref, relay_1_ref, out_0_ref, out_1_ref):
    half = near_ref.shape[0]
    relay = jnp.concatenate([relay_0_ref[:half, :], relay_1_ref[:half, :]], axis=1).astype(F32)
    total = (near_ref[...] + relay).astype(BF16)
    split = out_0_ref.shape[1]
    out_0_ref[...] = total[:, :split]
    out_1_ref[...] = total[:, split:]


def run_base(own_ref, link_ref, mine_ref, x_ref, y_ref, d_ref, x_low_ref, y_high_ref, out_0_ref, out_1_ref, first_ref):
    half = x_low_ref.shape[0]
    for mask, ref in enumerate((mine_ref, x_ref, y_ref, d_ref)):
        lanes = pl.ds(pl.multiple_of(owner(mask) * LANES, LANES), LANES)
        first_ref[:, lanes] = ref[...]
    start = 0
    for ref in (out_0_ref, out_1_ref):
        cols = slice(start, start + ref.shape[1])
        start += ref.shape[1]
        ref[...] = own_ref[:, cols] - dot_tn(link_ref[...], first_ref[:, cols])
        ref[:half, :] += x_low_ref[:, cols].astype(F32)
        ref[half:, :] += y_high_ref[:, cols].astype(F32)


def run_last(base_ref, low_ref, high_ref, out_ref, sum_ref, sems, *, start, chunks):
    rows, width = base_ref.shape
    half, height = low_ref.shape[0], rows // chunks
    copies = []
    for chunk in range(chunks):
        top = chunk * height
        place = slice(top, top + height)
        piece_ref, base = (low_ref, top) if top < half else (high_ref, top - half)
        sum_ref[place, :] = base_ref[place, :] + piece_ref[base : base + height, :].astype(F32)
        copy = pltpu.make_async_copy(
            sum_ref.at[pl.ds(top, height), :],
            out_ref.at[pl.ds(top, height), pl.ds(start, width)],
            sems.at[chunk],
        )
        copy.start()
        copies.append(copy)
    for copy in copies:
        copy.wait()


def local_pairs(leaf_rhs, leaf_inv, ordering, leaf_dinv, leaf_link, sep_rhs, sep_factor, sep_dinv):
    rows, width = leaf_rhs.shape
    half, split = rows // 2, rows // 2
    group = lax.axis_size(GRP)
    levels, slice_width, sep_block = sep_rhs.shape
    first = leaf_link.shape[1]
    fac_rows, cols = sep_factor.shape
    tiles = sep_block // fac_rows
    parts = range(2)
    me = lax.axis_index(GRP).astype(jnp.int32)
    link_turned = leaf_link.T

    def bf16(height, breadth):
        return jax.ShapeDtypeStruct((height, breadth), BF16)

    def f32(height, breadth):
        return jax.ShapeDtypeStruct((height, breadth), F32)

    x_all = exchange(leaf_rhs, GRP, 1)
    loads = pltpu.with_memory_space_constraint(leaf_rhs, pltpu.HBM)
    high, low = (
        call(
            functools.partial(run_split, top=top),
            (loads,),
            [pl.BlockSpec(memory_space=pltpu.HBM)],
            bf16(height, width),
            scratch_shapes=[pltpu.SemaphoreType.DMA],
        )
        for top, height in ((split, rows - split), (0, split))
    )
    y_high = exchange(high, GRP, 2)
    y_low = exchange(low, GRP, 2)
    distance = ordering[0] // rows ^ me
    swapped = (lax.axis_index(LEAF) % 2 == 1) & (distance % 3 != 0)
    dest = jnp.where(swapped, 3 - distance, distance) * rows + ordering[0] % rows
    blocks = arrange(leaf_inv, dest, group)

    *high_cut, kept = call(
        run_send,
        (y_high, low, high, link_turned, sep_factor),
        [vmem()] * 5,
        [
            bf16(rows - split + first + sep_block, width // 2),
            bf16(rows - split, width // 2),
            f32(first + sep_block, 2 * LANES),
        ],
        after=(blocks[0],),
        scratch_shapes=[pltpu.VMEM((first, width), F32)],
    )
    d_high = [exchange(high_cut[part], GRP, 1) for part in parts]
    low_cut = call(run_cut, (x_all,), [vmem()], [bf16(split, width // 2)] * 2, after=(blocks[0],))
    d_low = [exchange(low_cut[part], GRP, 2) for part in parts]

    *part_y, turned, scale = call(
        run_forward,
        (*blocks, leaf_dinv.reshape(-1, LANES), low, high, x_all, y_low, y_high),
        [vmem()] * 10,
        [f32(rows, width // 2)] * 2 + [bf16(rows, rows), f32(rows, LANES)],
        scratch_shapes=[pltpu.VMEM((3 * rows, rows), BF16), pltpu.VMEM((3 * rows, width), BF16)],
    )
    leaf_z, relay_low, relay_high = [], [], []
    for part in parts:
        shared = (kept,) if part == 0 else ()
        z_part, far_low, far_high = call(
            functools.partial(run_far, first=first),
            (
                blocks[3],
                turned,
                d_low[part],
                d_high[part],
                part_y[part],
                scale,
                *shared,
            ),
            [vmem()] * (6 + len(shared)),
            (
                bf16(rows, width // 2),
                bf16(half, width // 2),
                bf16(half + first * len(shared), width // 2),
            ),
            scratch_shapes=[pltpu.VMEM((rows, width // 2), BF16)],
        )
        leaf_z.append(z_part)
        relay_low.append(exchange(far_low, GRP, 1))
        relay_high.append(exchange(far_high, GRP, 2))

    near_x_low, near_y_high, near_x_high, near_y_low, own = call(
        run_near,
        (*blocks[:3], *leaf_z),
        [vmem()] * 5,
        [bf16(half, width)] * 2 + [f32(half, width)] * 2 + [f32(rows, width)],
        scratch_shapes=[pltpu.VMEM((rows, width), BF16)],
    )
    leaf_block = call(
        functools.partial(run_leaf, rows=fac_rows, cols=cols),
        (kept, d_high[0], relay_high[0], jnp.swapaxes(sep_rhs, 1, 2), sep_dinv),
        [vmem()] * 5,
        bf16(first + (levels + tiles) * sep_block, LANES),
        after=(own,),
    )
    partner = exchange(leaf_block, LEAF, 1)
    sum_x_low = exchange(near_x_low, GRP, 1)
    sum_y_high = exchange(near_y_high, GRP, 2)
    pair_block = call(
        functools.partial(run_pair, first=first, sep_block=sep_block),
        (leaf_block, partner),
        [vmem(), vmem()],
        bf16((levels + tiles) * first, LANES),
    )
    count = lax.axis_size(LEAF) // 2
    pairs = [pair_block] + [exchange(pair_block, LEAF, 2 * mask) for mask in range(1, count)]
    nsep = count * first
    first_here, sep_turned = call(
        functools.partial(
            run_tree, count=count, first=first, levels=levels, sep_block=sep_block, cols=cols
        ),
        pairs,
        [vmem()] * count,
        (bf16(first, LANES), jax.ShapeDtypeStruct((levels, sep_block, slice_width), F32)),
        scratch_shapes=[
            pltpu.VMEM((levels, nsep, LANES), BF16),
            pltpu.VMEM((nsep, tiles * LANES), BF16),
            pltpu.VMEM((nsep, LANES), F32),
        ],
    )
    first_all = [first_here] + [exchange(first_here, GRP, mask) for mask in range(1, group)]
    breadths = (width // 4 * 3, width // 4)
    into = [bf16(half, breadth) for breadth in breadths]
    x_sums = call(run_add, (near_x_high, *relay_high), [vmem()] * 3, into)
    y_sums = call(run_add, (near_y_low, *relay_low), [vmem()] * 3, into)
    sum_x_high = [exchange(x_sums[part], GRP, 1) for part in parts]
    sum_y_low = [exchange(y_sums[part], GRP, 2) for part in parts]
    base = call(
        run_base,
        (own, link_turned, *first_all, sum_x_low, sum_y_high),
        [vmem()] * (4 + group),
        [f32(rows, breadth) for breadth in breadths],
        scratch_shapes=[pltpu.VMEM((first, width), BF16)],
    )
    chunks = 4
    leaf_x, start = (), 0
    for part, breadth in zip(parts, breadths):
        leaf_x = (
            call(
                functools.partial(run_last, start=start, chunks=chunks),
                (base[part], sum_y_low[part], sum_x_high[part]),
                [vmem()] * 3,
                f32(rows, width),
                after=leaf_x,
                out_specs=pl.BlockSpec(memory_space=pltpu.HBM),
                scratch_shapes=[pltpu.VMEM((rows, breadth), F32), pltpu.SemaphoreType.DMA((chunks,))],
                input_output_aliases={0: 0} if leaf_x else {},
            ),
        )
        start += breadth
    return leaf_x[0], jnp.swapaxes(sep_turned, 1, 2)


def fits(leaf_rhs, leaf_inv, sep_rhs, sep_factor, leaf_link):
    levels, slice_width, sep_block = sep_rhs.shape
    width = leaf_rhs.shape[1]
    count = lax.axis_size(GRP)
    leaves = lax.axis_size(LEAF)
    return (
        count == 2**2
        and leaf_inv.shape[1] == count * leaf_rhs.shape[0]
        and leaf_rhs.shape[0] % 256 == 0
        and leaf_rhs.shape[0] // LANES == 8
        and leaf_link.shape[1] == 2 * sep_block
        and sep_block % 16 == 0
        and slice_width % 128 == 0
        and sep_block % sep_factor.shape[0] == 0
        and sep_factor.shape[1] + levels <= sep_block // sep_factor.shape[0] * LANES
        and width == count * slice_width
        and slice_width == LANES
        and width % (leaves * sep_block) == 0
    )


def local(*args):
    leaf_rhs, leaf_inv, _, _, leaf_link, sep_rhs, sep_factor, _ = args
    if fits(leaf_rhs, leaf_inv, sep_rhs, sep_factor, leaf_link):
        return local_pairs(*args)
    return local_general(*args)


def solution(mesh):
    placed = (
        P((LEAF, GRP), None),
        P((LEAF, GRP), None),
        P(LEAF, None),
        P((LEAF, GRP)),
        P((LEAF, GRP), None),
        P(None, GRP, LEAF),
        P((LEAF, GRP), None),
        P(None, LEAF),
    )
    return jax.shard_map(
        local,
        mesh=mesh,
        in_specs=placed,
        out_specs=(P((LEAF, GRP), None), P(None, GRP, LEAF)),
        check_vma=False,
    )
```
